32 devices in a mesh: rep: 4 (over y, x), fsdp: 2 (over core), tm: 4 (over z).
Axes of the slice: x: 2, y: 2, z: 4, core: 2. Of those that a mesh axis runs over, the one named last changes fastest.
Arguments:
- tokens: bfloat16 [8, 2048, 1024], P(('rep', 'fsdp'), 'tm'), may hold values from -6 to 6
- in_weight: float32 [1024, 4384], P('fsdp'), may hold values from -0.1875 to 0.1875
- out_weight: float32 [2048, 1024], P('fsdp'), may hold values from -0.125 to 0.125
- norm_gain: float32 [1024], P('fsdp'), may hold values from 0.5 to 1.5
- conv_weight: float32 [4, 2304], P(None, 'fsdp'), may hold values from -3 to 3
- conv_bias: float32 [2304], P('fsdp'), may hold values from -0.5 to 0.5
- dt_bias: float32 [32], P('fsdp'), may hold values from -1 to 1
- a_log: float32 [32], P('fsdp')
- d_skip: float32 [32], P('fsdp'), may hold values from 0.5 to 1.5
- gate_gain: float32 [2048], P('fsdp'), may hold values from 0.5 to 1.5
- lengths: int32 [8], P(('rep', 'fsdp')), may hold values from 512 to 2048, as said below
- starts: int32 [8], P(('rep', 'fsdp')), may hold values from 0 to 1536, as said below
- cotangent: bfloat16 [8, 2048, 1024], P(('rep', 'fsdp'), 'tm'), may hold values from -6 to 6
Outputs:
- output: bfloat16 [8, 2048, 1024], P(('rep', 'fsdp'), 'tm')
- input_grad: float32 [8, 2048, 1024], P(('rep', 'fsdp'), 'tm')
- grad_in_weight: float32 [1024, 4384], P('fsdp')
- grad_out_weight: float32 [2048, 1024], P('fsdp')
- grad_norm_gain: float32 [1024], P('fsdp')
- grad_conv_weight: float32 [4, 2304], P(None, 'fsdp')
- grad_conv_bias: float32 [2304], P('fsdp')
- grad_dt_bias: float32 [32], P('fsdp')
- grad_a_log: float32 [32], P('fsdp')
- grad_d_skip: float32 [32], P('fsdp')
- grad_gate_gain: float32 [2048], P('fsdp')
The draws below stay inside these ranges and needn't reach their ends.
Inputs may be any that keep to these rules, and one draw needn't show every extreme that they name: Each row holds one sequence, starts + lengths <= 2048; some row has length 2048 and some other row length 512. starts + lengths <= 2048.
All inputs are finite; a program needn't handle non-finite values.
Results may differ from the reference program's by a relative error of at most 0.015.
The reference program's roundings to bfloat16 on the way count: a program that leaves them out, or rounds other values in their place, can miss the bound.
Values may be sent and summed in bfloat16 or wider, within the bound.
No kernel may reach another device: no remote copies, remote signals or barrier semaphores. Data moves between devices by JAX's collectives and lax.ppermute only.
A program may use at most 192 MiB of HBM per device.

```python
import jax
import jax.numpy as jnp
from jax import lax

D = 1024
H = 32
P_SIZE = 64
N = 128
K = 4
Q = 256
DIN = 2048
CONV = 2304
PROJ = 4384
ROW = 2048
SEQS = 8


def draw_pair(key):
    base_key = jax.random.fold_in(key, 17)
    first_key, second_key, third_key = jax.random.split(base_key, 3)
    drawn = jax.random.randint(first_key, (SEQS,), ROW // 4, ROW + 1)
    order = jax.random.permutation(second_key, SEQS)
    drawn = drawn.at[order[0]].set(ROW).at[order[1]].set(ROW // 4)
    room = ROW - drawn + 1
    offsets = jax.random.randint(third_key, (SEQS,), 0, room)
    offsets = offsets.at[order[0]].set(0).at[order[1]].set(ROW - ROW // 4)
    return (drawn.astype(jnp.int32), offsets.astype(jnp.int32))


def draw_lengths(key, part):
    return draw_pair(key)[0]


def draw_starts(key, part):
    return draw_pair(key)[1]


def draw_a_log(key, part):
    rate_key = jax.random.fold_in(key, 5)
    uniform_draw = jax.random.uniform(rate_key, (H,), jnp.float32)
    slowest = 0.2 / ROW
    fastest = 0.04
    return (jnp.log(slowest) + uniform_draw * (jnp.log(fastest) - jnp.log(slowest))).astype(jnp.float32)


def level_of(key, dims, shards, least, top_value):
    loudness, own = 1.0, jax.random.fold_in(key, 6)
    for dim, shards_of in shards:
        steps = jnp.exp(jax.random.uniform(jax.random.fold_in(own, dim), (shards_of,), jnp.float32, least / len(shards), top_value / len(shards)))
        loudness = loudness * jnp.repeat(steps, dims[dim] // shards_of).reshape([-1 if axis == dim else 1 for axis in range(len(dims))])
    return loudness


def scatter_about(key, extent, scale, reach, cuts=(), kind=jnp.bfloat16):
    factor_of = level_of(key, extent, cuts, -0.22, 0.18) if cuts else 1.0
    values = jax.random.normal(key, extent, jnp.float32) * scale * factor_of
    return jnp.minimum(jnp.maximum(values, -reach), reach).astype(kind)


def setup_inputs(seed: int = 0) -> dict:
    key_list = jax.random.split(jax.random.key(seed), 14)
    return {
        "tokens": scatter_about(key_list[0], (SEQS, ROW, D), 1.0, 6.0, ((0, 8), (1, 4))),
        "in_weight": scatter_about(key_list[1], (D, PROJ), D ** -0.5, 0.1875, ((0, 2),), jnp.float32),
        "out_weight": scatter_about(key_list[2], (DIN, D), DIN ** -0.5, 0.125, ((0, 2),), jnp.float32),
        "norm_gain": jnp.clip(1.0 + 0.1 * jax.random.normal(key_list[3], (D,), jnp.float32), 0.5, 1.5),
        "conv_weight": scatter_about(key_list[4], (K, CONV), K ** -0.5, 3.0, ((1, 2),), jnp.float32),
        "conv_bias": jnp.clip(jax.random.uniform(key_list[5], (CONV,), jnp.float32, -0.5, 0.5) * level_of(key_list[5], (CONV,), ((0, 2),), -0.4, 0.0), -0.5, 0.5),
        "dt_bias": jnp.clip(jax.random.uniform(key_list[6], (H,), jnp.float32, -1.0, 1.0) * level_of(key_list[6], (H,), ((0, 2),), -0.4, 0.0), -1.0, 1.0),
        "a_log": draw_a_log(jax.random.fold_in(key_list[13], 71), 0),
        "d_skip": jnp.clip(0.5 + 1.0 * jax.random.uniform(key_list[8], (H,), jnp.float32) ** level_of(key_list[8], (H,), ((0, 2),), -0.2, 0.2), 0.5, 1.5),
        "gate_gain": jnp.clip(1.0 + 0.1 * jax.random.normal(key_list[9], (DIN,), jnp.float32), 0.5, 1.5),
        "lengths": draw_lengths(jax.random.fold_in(key_list[13], 71), 0),
        "starts": draw_starts(jax.random.fold_in(key_list[13], 71), 0),
        "cotangent": scatter_about(key_list[12], (SEQS, ROW, D), 1.0, 6.0, ((0, 8), (1, 4))),
    }


EPS = 1e-05
HIGHEST = lax.Precision.HIGHEST

@jax.custom_vjp
def low(v):
    return lax.optimization_barrier(v.astype(jnp.bfloat16)).astype(jnp.float32)

@jax.custom_vjp
def low_back(v):
    return v

def low_keep(v):
    return (low(v), None)

def low_pass(kept, grad):
    return (grad,)

def back_keep(v):
    return (v, None)

def back_low(kept, grad):
    return (low(grad),)
low.defvjp(low_keep, low_pass)
low_back.defvjp(back_keep, back_low)

def rms_scale(values, gain_row):
    return values * lax.rsqrt(lax.optimization_barrier(jnp.mean(values * values, axis=-1, keepdims=True)) + EPS) * gain_row

def block_terms(carried, inputs_x, steps_dt, rates, in_map, out_map):
    running = jnp.cumsum(steps_dt * rates[None, :], axis=0)
    length_q = inputs_x.shape[0]
    below_diag = (jnp.arange(length_q)[:, None] >= jnp.arange(length_q)[None, :])[:, :, None]
    spread = running[:, None, :] - running[None, :, :]
    decays = jnp.where(below_diag, jnp.exp(jnp.where(below_diag, spread, 0.0)), 0.0)
    scores = jnp.dot(out_map, in_map.T, precision=HIGHEST)
    weights = scores[:, :, None] * decays * steps_dt[None, :, :]
    within = jnp.einsum('ijh,jhp->ihp', weights, inputs_x, precision=HIGHEST)
    carry_term = jnp.exp(running)[:, :, None] * jnp.einsum('in,hpn->ihp', out_map, carried, precision=HIGHEST)
    closing = jnp.exp(running[-1:, :] - running) * steps_dt
    fresh_terms = jnp.einsum('jh,jhp,jn->hpn', closing, inputs_x, in_map, precision=HIGHEST)
    new_state = jnp.exp(running[-1])[:, None, None] * carried + fresh_terms
    return (new_state, within + carry_term)

def block_scan(inputs_x, steps_dt, rates, in_map, out_map, carried, block_len):
    num_blocks = inputs_x.shape[0] // block_len
    head_count = inputs_x.shape[1]

    def advance(state_now, pieces):
        return block_terms(state_now, pieces[0], pieces[1], rates, pieces[2], pieces[3])
    final_state, outputs = lax.scan(jax.checkpoint(advance), carried, (inputs_x.reshape(num_blocks, block_len, head_count, -1), steps_dt.reshape(num_blocks, block_len, head_count), in_map.reshape(num_blocks, block_len, -1), out_map.reshape(num_blocks, block_len, -1)))
    return (outputs.reshape(inputs_x.shape), final_state)

def forward(tokens_f, in_weight, out_weight, norm_gain, conv_weight, conv_bias, dt_bias, a_log, d_skip, gate_gain, lengths, starts):
    in_low = low(in_weight)
    out_low = low(out_weight)
    norm_vec = low(norm_gain)
    conv_taps = low(conv_weight)
    conv_shift = low(conv_bias)
    dt_shift = low(dt_bias)
    decay_log = low(a_log)
    skip_vec = low(d_skip)
    gate_vec = low(gate_gain)
    positions = jnp.arange(ROW).astype(jnp.int32)

    def one_row(items):
        row_tokens, row_length, row_start = items
        valid_rows = ((positions >= row_start) & (positions < row_start + row_length)).astype(jnp.float32)[:, None]
        normed = low(rms_scale(row_tokens, norm_vec))
        projected = low_back(low(jnp.dot(normed, in_low, precision=HIGHEST, preferred_element_type=jnp.float32)))
        gate_z = projected[:, :DIN]
        local_rows = projected[:, DIN:DIN + CONV] * valid_rows
        padded = jnp.concatenate([jnp.zeros((K - 1, CONV), jnp.float32), local_rows], axis=0)
        mixed = conv_shift[None, :] + sum((conv_taps[offset][None, :] * padded[offset:offset + ROW] for offset in range(K)))
        active = jax.nn.silu(mixed)
        inputs_x = active[:, :DIN].reshape(ROW, H, P_SIZE)
        in_map = active[:, DIN:DIN + N]
        out_map = active[:, DIN + N:]
        steps_dt = jax.nn.softplus(projected[:, DIN + CONV:] + dt_shift[None, :]) * valid_rows
        rates = -jnp.exp(decay_log)
        zeros_state = jnp.zeros((H, P_SIZE, N), jnp.float32)
        mix_y, final_state = block_scan(inputs_x, steps_dt, rates, in_map, out_map, zeros_state, Q)
        full_y = (mix_y + skip_vec[None, :, None] * inputs_x).reshape(ROW, DIN)
        gated = low(rms_scale(full_y * jax.nn.silu(gate_z), gate_vec) * valid_rows)
        return row_tokens + jnp.dot(gated, out_low, precision=HIGHEST, preferred_element_type=jnp.float32)
    return lax.map(one_row, (tokens_f, lengths, starts))

def reference(tokens, in_weight, out_weight, norm_gain, conv_weight, conv_bias, dt_bias, a_log, d_skip, gate_gain, lengths, starts, cotangent):

    def closed(*params):
        return forward(*params, lengths, starts)
    result, back_fn = jax.vjp(closed, tokens.astype(jnp.float32), in_weight, out_weight, norm_gain, conv_weight, conv_bias, dt_bias, a_log, d_skip, gate_gain)
    grads = back_fn(cotangent.astype(jnp.float32))
    return (result.astype(jnp.bfloat16), grads[0], grads[1], grads[2], grads[3], grads[4], grads[5], grads[6], grads[7], grads[8], grads[9])
```

```python
import jax
import jax.numpy as jnp
from jax import lax
from jax.experimental import pallas as pl
from jax.experimental.pallas import tpu as pltpu
from jax.sharding import PartitionSpec as P

H = 32
P_SIZE = 64
N = 128
K = 4
DIN = 2048
CONV = 2304
EPS = 1e-05
QB = 128
HALO = 16
GROUP = 256
LANE = 128

bf16 = jnp.bfloat16
f32 = jnp.float32
HIGHEST = lax.Precision.HIGHEST

VMEM_LIMIT = 60 * 1024 * 1024


def nn(a, b):
    return lax.dot_general(a, b, (((1,), (0,)), ((), ())), preferred_element_type=f32)


def nt(a, b):
    return lax.dot_general(a, b, (((1,), (1,)), ((), ())), preferred_element_type=f32)


def exact_nn(a, b):
    return lax.dot_general(
        a, b, (((1,), (0,)), ((), ())), precision=HIGHEST, preferred_element_type=f32
    )


def iota(shape, dim):
    return lax.broadcasted_iota(jnp.int32, shape, dim)


def sigmoid(v):
    return 1.0 / (1.0 + jnp.exp(-v))


def split_two(v):
    hi = v.astype(bf16)
    lo = (v - hi.astype(f32)).astype(bf16)
    return hi, lo


def const_spec(shape):
    return pl.BlockSpec(shape, lambda *_: tuple(0 for _ in shape))


def params(steps=1):
    return pltpu.CompilerParams(
        dimension_semantics=("arbitrary",) * steps, vmem_limit_bytes=VMEM_LIMIT
    )


def call(kernel, grid, in_specs, out_specs, out_shape, scratch, flops, nbytes, name):
    return pl.pallas_call(
        kernel,
        grid_spec=pltpu.PrefetchScalarGridSpec(
            num_scalar_prefetch=1,
            grid=grid,
            in_specs=in_specs,
            out_specs=out_specs,
            scratch_shapes=scratch,
        ),
        out_shape=out_shape,
        compiler_params=params(len(grid)),
        cost_estimate=pl.CostEstimate(flops=flops, bytes_accessed=nbytes, transcendentals=0),
        name=name,
    )


def spread(cols, pair):
    left = cols[:, 2 * pair : 2 * pair + 1]
    right = cols[:, 2 * pair + 1 : 2 * pair + 2]
    lanes = iota((cols.shape[0], LANE), 1)
    return jnp.where(lanes < P_SIZE, left, right)


def spread_group(cols):
    return jnp.concatenate([spread(cols, 0), spread(cols, 1)], axis=1)


def block_diag(pair_low):
    lanes = iota(pair_low.shape, 1)
    zero = jnp.zeros_like(pair_low)
    return jnp.concatenate(
        [jnp.where(lanes < P_SIZE, pair_low, zero), jnp.where(lanes < P_SIZE, zero, pair_low)],
        axis=0,
    )


def head_columns(cols, group):
    return pltpu.roll(cols, lax.rem(LANE - 4 * group, LANE), 1)


def head_picker(lanes_in, first_head):
    rows = iota((lanes_in, LANE), 0) // P_SIZE + first_head
    return (rows == iota((lanes_in, LANE), 1)).astype(bf16)


def front_kernel(
    scal, tok, halo, gain, w_own, w_oth, r_own, r_oth, taps, heads,
    normed, u_out, act_out, dact_out, dt_out, sg_out, cum_out, cumt_out, st_out,
    ubuf, bt, ecl,
):
    step = pl.program_id(0)
    tok_count = tok.shape[0]
    half = w_own.shape[0]
    own = pl.ds(pl.multiple_of(scal[0] * half, LANE), half)
    oth = pl.ds(pl.multiple_of((1 - scal[0]) * half, LANE), half)
    lo = scal[1]
    hi = scal[2]

    @pl.when(step == 0)
    def _():
        def rows_of(src, base, dst, count):
            x = src[pl.ds(base, count), :].astype(f32)
            ms = jnp.mean(x * x, axis=-1, keepdims=True)
            normed[pl.ds(dst, count), :] = (x * lax.rsqrt(ms + EPS) * gain[...]).astype(bf16)

        rows_of(halo, 0, 0, HALO)

        def body(i, carry):
            base = pl.multiple_of(i * 64, 64)
            rows_of(tok, base, pl.multiple_of(base + HALO, 16), 64)
            return carry

        lax.fori_loop(0, tok_count // 64, body, 0)
        r = nn(normed[HALO:, own], r_own[...]) + nn(normed[HALO:, oth], r_oth[...])
        pre = r.astype(bf16).astype(f32) + heads[0:1, :]
        pos = iota((tok_count, LANE), 0)
        keep = (pos >= lo) & (pos < hi) & (iota((tok_count, LANE), 1) < H)
        soft = jnp.maximum(pre, 0.0) + jnp.log1p(jnp.exp(-jnp.abs(pre)))
        dt = jnp.where(keep, soft, 0.0)
        dt_out[...] = dt
        sg_out[...] = jnp.where(keep, sigmoid(pre), 0.0)
        da = dt * heads[1:2, :]
        tri = (iota((QB, QB), 0) >= iota((QB, QB), 1)).astype(f32)
        carry = jnp.zeros((1, LANE), f32)
        for q in range(tok_count // QB):
            cum = exact_nn(tri, da[q * QB : (q + 1) * QB]) + carry
            cum_out[q * QB : (q + 1) * QB, :] = cum
            cumt_out[:, q * QB : (q + 1) * QB] = cum.T
            carry = cum[QB - 1 : QB]
        ecl[...] = jnp.exp(carry - cum_out[...])

    u = nn(normed[:, own], w_own[...]) + nn(normed[:, oth], w_oth[...])
    pos = iota(u.shape, 0) - HALO
    u = jnp.where((pos >= lo) & (pos < hi), u, 0.0).astype(bf16)
    u_out[...] = u
    ubuf[...] = u.astype(f32)
    c = taps[4:5, :] + sum(
        taps[k : k + 1, :] * ubuf[HALO - 3 + k : HALO - 3 + k + tok_count, :] for k in range(K)
    )
    s = sigmoid(c)
    act = (c * s).astype(bf16)
    act_out[...] = act
    dact_out[...] = (s * (1.0 + c * (1.0 - s))).astype(bf16)

    @pl.when(step == 0)
    def _():
        bt[...] = act[:, :N].astype(f32).T.astype(bf16)

    @pl.when(step > 0)
    def _():
        group = step - 1
        dtg = spread_group(head_columns(dt_out[...], group))
        ecg = spread_group(head_columns(ecl[...], group))
        xt = (act.astype(f32) * dtg).astype(bf16)
        xw = (xt.astype(f32) * ecg).astype(bf16)
        st_out[...] = nn(bt[...], xw)


def front(scal, tok, halo, gain, wu_own, wu_oth, taps, heads):
    tok_count, d = tok.shape
    half = wu_own.shape[0]
    ext = tok_count + HALO
    groups = CONV // GROUP
    first = groups - 1

    def col(j, *_):
        return (0, (j + first) % groups)

    def weight(rows):
        return pl.BlockSpec((rows, GROUP), col)

    narrow = pl.BlockSpec((half, LANE), lambda j, *_: (0, CONV // LANE))
    return call(
        front_kernel,
        (groups,),
        [
            const_spec((tok_count, d)),
            const_spec((HALO, d)),
            const_spec((1, d)),
            weight(half),
            weight(half),
            narrow,
            narrow,
            weight(8),
            const_spec((8, LANE)),
        ],
        [
            const_spec((ext, d)),
            pl.BlockSpec((ext, GROUP), col),
            pl.BlockSpec((tok_count, GROUP), col),
            pl.BlockSpec((tok_count, GROUP), col),
            const_spec((tok_count, LANE)),
            const_spec((tok_count, LANE)),
            const_spec((tok_count, LANE)),
            const_spec((LANE, tok_count)),
            pl.BlockSpec((N, GROUP), lambda j, *_: (0, jnp.maximum(j - 1, 0))),
        ],
        [
            jax.ShapeDtypeStruct((ext, d), bf16),
            jax.ShapeDtypeStruct((ext, CONV), bf16),
            jax.ShapeDtypeStruct((tok_count, CONV), bf16),
            jax.ShapeDtypeStruct((tok_count, CONV), bf16),
            jax.ShapeDtypeStruct((tok_count, LANE), f32),
            jax.ShapeDtypeStruct((tok_count, LANE), f32),
            jax.ShapeDtypeStruct((tok_count, LANE), f32),
            jax.ShapeDtypeStruct((LANE, tok_count), f32),
            jax.ShapeDtypeStruct((N, DIN), f32),
        ],
        [
            pltpu.VMEM((ext, GROUP), f32),
            pltpu.VMEM((N, tok_count), bf16),
            pltpu.VMEM((tok_count, LANE), f32),
        ],
        2 * ext * d * (CONV + LANE),
        2 * (ext * d + d * CONV + 3 * ext * CONV),
        "front",
    )(scal, tok, halo, gain, wu_own, wu_oth, wu_own, wu_oth, taps, heads)


def intra_kernel(scal, x, bc, dt, cum, cumt, y_out, s0_out, scores, bt):
    group = pl.program_id(0)
    blocks = x.shape[0] // QB

    @pl.when(group == 0)
    def _():
        lower = iota((QB, QB), 0) >= iota((QB, QB), 1)
        bt[...] = bc[:, :N].astype(f32).T.astype(bf16)
        for q in range(blocks):
            rows = slice(q * QB, (q + 1) * QB)
            scores[q] = jnp.where(lower, nt(bc[rows, N:], bc[rows, :N]), 0.0)

    dtr = head_columns(dt[...], group)
    cumr = head_columns(cum[...], group)
    carry = jnp.zeros((N, GROUP), f32)
    for q in range(blocks):
        rows = slice(q * QB, (q + 1) * QB)
        cq = cumr[rows]
        end = cq[QB - 1 : QB]
        start = cumr[q * QB - 1 : q * QB] if q else jnp.zeros((1, LANE), f32)
        xt = (x[rows, :].astype(f32) * spread_group(dtr[rows])).astype(bf16)
        low_carry = carry.astype(bf16)
        s0_out[q] = low_carry
        ys = []
        for pair in range(2):
            mats = []
            for e in range(2):
                h = 2 * pair + e
                row = cumt[0, h : h + 1, rows]
                decay = jnp.exp(jnp.minimum(cq[:, h : h + 1] - row, 0.0))
                mats.append((decay * scores[q]).astype(bf16))
            ys.append(
                nn(
                    jnp.concatenate(mats, axis=1),
                    block_diag(xt[:, pair * LANE : (pair + 1) * LANE]),
                )
            )
        y = jnp.concatenate(ys, axis=1)
        if q:
            y = y + jnp.exp(spread_group(cq - start)) * nn(bc[rows, N:], low_carry)
        y_out[rows, :] = y
        if q < blocks - 1:
            xw = (xt.astype(f32) * jnp.exp(spread_group(end - cq))).astype(bf16)
            fresh = nn(bt[:, rows], xw)
            carry = fresh if q == 0 else fresh + carry * jnp.exp(spread_group(end - start))


def intra(scal, act, dt, cum, cumt):
    tok_count = act.shape[0]
    blocks = tok_count // QB
    groups = DIN // GROUP
    return call(
        intra_kernel,
        (groups,),
        [
            pl.BlockSpec((tok_count, GROUP), lambda j, *_: (0, j)),
            pl.BlockSpec((tok_count, GROUP), lambda j, *_: (0, groups)),
            const_spec((tok_count, LANE)),
            const_spec((tok_count, LANE)),
            pl.BlockSpec((1, 4, tok_count), lambda j, *_: (j, 0, 0)),
        ],
        [
            pl.BlockSpec((tok_count, GROUP), lambda j, *_: (0, j)),
            pl.BlockSpec((blocks, N, GROUP), lambda j, *_: (0, 0, j)),
        ],
        [
            jax.ShapeDtypeStruct((tok_count, DIN), f32),
            jax.ShapeDtypeStruct((blocks, N, DIN), bf16),
        ],
        [pltpu.VMEM((blocks, QB, QB), f32), pltpu.VMEM((N, tok_count), bf16)],
        2 * tok_count * DIN * 3 * N,
        8 * tok_count * DIN,
        "intra",
    )(scal, act, act, dt, cum, cumt)


def gate_kernel(
    scal, yloc, act, z, eg, cum, s_in, vecs,
    gated, ey_out, ez_out, r_loc, r_dev, dc_out, g_out, gs_out,
    pick, vbuf, ytbuf, ydbuf,
):
    step = pl.program_id(0)
    rows = yloc.shape[0]
    groups = DIN // GROUP

    @pl.when(step == 0)
    def _():
        pick[...] = head_picker(DIN, 0)
        g_out[...] = jnp.zeros_like(g_out)
        gs_out[...] = jnp.zeros_like(gs_out)

    pos = iota((rows, 1), 0) + step * rows
    valid = ((pos >= scal[1]) & (pos < scal[2])).astype(f32)
    cq = cum[...]
    ecq = jnp.exp(cq)
    cmat = act[:, DIN + N :]
    ssq = jnp.zeros((rows, GROUP), f32)
    for g in range(groups):
        cols = slice(g * GROUP, (g + 1) * GROUP)
        eg_cum = jnp.concatenate([spread(ecq, 2 * g), spread(ecq, 2 * g + 1)], axis=1)
        yd = eg_cum * nn(cmat, s_in[:, cols])
        ydbuf[:, cols] = yd
        yt = yloc[:, cols] + yd + vecs[1:2, cols] * act[:, cols].astype(f32)
        ytbuf[:, cols] = yt
        zz = z[:, cols].astype(f32)
        v = yt * (zz * sigmoid(zz))
        vbuf[:, cols] = v
        ssq = ssq + v * v
    rs = lax.rsqrt(jnp.sum(ssq, axis=-1, keepdims=True) / DIN + EPS)
    mixed = jnp.zeros((rows, GROUP), f32)
    for g in range(groups):
        cols = slice(g * GROUP, (g + 1) * GROUP)
        n = vbuf[:, cols] * rs
        vbuf[:, cols] = n
        gain = vecs[0:1, cols]
        gated[:, cols] = (n * gain * valid).astype(bf16)
        e = eg[:, cols].astype(f32) * valid
        gs_out[0:1, cols] += jnp.sum(e * n, axis=0, keepdims=True)
        mixed = mixed + e * gain * n
    m2 = jnp.sum(mixed, axis=-1, keepdims=True) / DIN
    rl = jnp.zeros((rows, LANE), f32)
    rd = jnp.zeros((rows, LANE), f32)
    dc = jnp.zeros((rows, N), f32)
    ct = cmat.astype(f32).T.astype(bf16)
    for g in range(groups):
        cols = slice(g * GROUP, (g + 1) * GROUP)
        n = vbuf[:, cols]
        e = eg[:, cols].astype(f32) * valid
        ev = rs * (e * vecs[0:1, cols] - n * m2)
        zz = z[:, cols].astype(f32)
        sz = sigmoid(zz)
        ey = ev * (zz * sz)
        ez_out[:, cols] = (ev * ytbuf[:, cols] * (sz * (1.0 + zz * (1.0 - sz)))).astype(bf16)
        gs_out[1:2, cols] += jnp.sum(ey * act[:, cols].astype(f32), axis=0, keepdims=True)
        low = ey.astype(bf16)
        ey_out[:, cols] = low
        eyf = low.astype(f32)
        ph, pl_ = split_two(eyf * yloc[:, cols])
        rl = rl + nn(ph, pick[cols, :]) + nn(pl_, pick[cols, :])
        rd = rd + nn((eyf * ydbuf[:, cols]).astype(bf16), pick[cols, :])
        eg_cum = jnp.concatenate([spread(ecq, 2 * g), spread(ecq, 2 * g + 1)], axis=1)
        eye = (eyf * eg_cum).astype(bf16)
        g_out[:, cols] += nn(ct, eye)
        dc = dc + nt(eye, s_in[:, cols])
    r_loc[...] = rl
    r_dev[...] = rd
    dc_out[...] = dc


def gate(scal, yloc, act, z, eg, cum, s_in, vecs):
    tok_count = act.shape[0]
    rows = QB

    def rowspec(width):
        return pl.BlockSpec((rows, width), lambda j, *_: (j, 0))

    def out(width, kind):
        return jax.ShapeDtypeStruct((tok_count, width), kind)

    return call(
        gate_kernel,
        (tok_count // rows,),
        [
            rowspec(DIN),
            rowspec(CONV),
            rowspec(DIN),
            rowspec(DIN),
            rowspec(LANE),
            const_spec((N, DIN)),
            const_spec((8, DIN)),
        ],
        [
            rowspec(DIN),
            rowspec(DIN),
            rowspec(DIN),
            rowspec(LANE),
            rowspec(LANE),
            rowspec(LANE),
            const_spec((N, DIN)),
            const_spec((8, DIN)),
        ],
        [
            out(DIN, bf16),
            out(DIN, bf16),
            out(DIN, bf16),
            out(LANE, f32),
            out(LANE, f32),
            out(LANE, f32),
            jax.ShapeDtypeStruct((N, DIN), f32),
            jax.ShapeDtypeStruct((8, DIN), f32),
        ],
        [
            pltpu.VMEM((DIN, LANE), bf16),
            pltpu.VMEM((rows, DIN), f32),
            pltpu.VMEM((rows, DIN), f32),
            pltpu.VMEM((rows, DIN), f32),
        ],
        2 * tok_count * DIN * 6 * N,
        20 * tok_count * DIN,
        "gate",
    )(scal, yloc, act, z, eg, cum, s_in, vecs)


def back_kernel(
    scal, x, bc, dt, cum, cumt, ey, s0,
    dxt_out, db_out, dc_out, r2_out, cq_out,
    scores, dscores, ct,
):
    group = pl.program_id(0)
    last = pl.num_programs(0) - 1
    blocks = x.shape[0] // QB
    upper = iota((QB, QB), 0) <= iota((QB, QB), 1)

    @pl.when(group == 0)
    def _():
        ct[...] = bc[:, N:].astype(f32).T.astype(bf16)
        for q in range(blocks):
            rows = slice(q * QB, (q + 1) * QB)
            scores[q] = jnp.where(upper, nt(bc[rows, :N], bc[rows, N:]), 0.0)
        dscores[...] = jnp.zeros_like(dscores)
        db_out[...] = jnp.zeros_like(db_out)
        dc_out[...] = jnp.zeros_like(dc_out)
        r2_out[...] = jnp.zeros_like(r2_out)
        cq_out[...] = jnp.zeros_like(cq_out)

    dtr = head_columns(dt[...], group)
    cumr = head_columns(cum[...], group)
    picks = [head_picker(LANE, 4 * group + 2 * pair) for pair in range(2)]
    picks2 = [jnp.concatenate([p, p], axis=0) for p in picks]
    pick_all = head_picker(GROUP, 4 * group).astype(f32)
    carry = None
    for q in reversed(range(blocks)):
        rows = slice(q * QB, (q + 1) * QB)
        cq = cumr[rows]
        end = cq[QB - 1 : QB]
        start = cumr[q * QB - 1 : q * QB] if q else jnp.zeros((1, LANE), f32)
        xt = (x[rows, :].astype(f32) * spread_group(dtr[rows])).astype(bf16)
        eyq = ey[rows, :]
        dxs = []
        ds = jnp.zeros((QB, QB), f32)
        for pair in range(2):
            lanes = slice(pair * LANE, (pair + 1) * LANE)
            eybd = block_diag(eyq[:, lanes])
            dm = nt(xt[:, lanes], eybd)
            mats = []
            for e in range(2):
                h = 2 * pair + e
                row = cumt[0, h : h + 1, rows]
                decay = jnp.exp(jnp.minimum(row - cq[:, h : h + 1], 0.0))
                mats.append((decay * scores[q]).astype(bf16))
                ds = ds + decay * dm[:, e * QB : (e + 1) * QB]
            dxs.append(nn(jnp.concatenate(mats, axis=1), eybd))
        dscores[q] += ds
        dx = jnp.concatenate(dxs, axis=1)
        xtf = xt.astype(f32)
        eye = None
        if q:
            eye = (eyq.astype(f32) * jnp.exp(spread_group(cq - start))).astype(bf16)
            dc_out[rows, :] += nt(eye, s0[q])
        if carry is not None:
            low = carry.astype(bf16)
            ecl = jnp.exp(spread_group(end - cq))
            dst = ecl * nn(bc[rows, :N], low)
            db_out[rows, :] += nt((xtf * ecl).astype(bf16), low)
            total = jnp.exp(spread_group(end - start))
            vec = jnp.sum(xtf * dst, axis=0, keepdims=True)
            if q:
                vec = vec + total * jnp.sum(carry * s0[q].astype(f32), axis=0, keepdims=True)
            cq_out[q : q + 1, :] += exact_nn(jnp.broadcast_to(vec, (8, GROUP)), pick_all)[0:1]
            dx = dx + dst
        if q:
            fresh = nn(ct[:, rows], eye)
            carry = fresh if carry is None else fresh + total * carry
        dxt_out[rows, :] = dx.astype(bf16)
        prod = xtf * dx
        acc = jnp.zeros((QB, LANE), f32)
        for pair in range(2):
            ph, pl_ = split_two(prod[:, pair * LANE : (pair + 1) * LANE])
            acc = acc + nn(jnp.concatenate([ph, pl_], axis=1), picks2[pair])
        r2_out[rows, :] += acc

    @pl.when(group == last)
    def _():
        for q in range(blocks):
            rows = slice(q * QB, (q + 1) * QB)
            ds = jnp.where(upper, dscores[q], 0.0)
            db_out[rows, :] += nn(ds.astype(bf16), bc[rows, N:])
            dc_out[rows, :] += nn(ds.T.astype(bf16), bc[rows, :N])


def back(scal, act, dt, cum, cumt, ey, s0):
    tok_count = act.shape[0]
    blocks = tok_count // QB
    groups = DIN // GROUP
    wide = pl.BlockSpec((tok_count, GROUP), lambda j, *_: (0, j))
    small = const_spec((tok_count, LANE))
    return call(
        back_kernel,
        (groups,),
        [
            wide,
            pl.BlockSpec((tok_count, GROUP), lambda j, *_: (0, groups)),
            small,
            small,
            pl.BlockSpec((1, 4, tok_count), lambda j, *_: (j, 0, 0)),
            wide,
            pl.BlockSpec((blocks, N, GROUP), lambda j, *_: (0, 0, j)),
        ],
        [wide, small, small, small, const_spec((8, LANE))],
        [
            jax.ShapeDtypeStruct((tok_count, DIN), bf16),
            jax.ShapeDtypeStruct((tok_count, LANE), f32),
            jax.ShapeDtypeStruct((tok_count, LANE), f32),
            jax.ShapeDtypeStruct((tok_count, LANE), f32),
            jax.ShapeDtypeStruct((8, LANE), f32),
        ],
        [
            pltpu.VMEM((blocks, QB, QB), f32),
            pltpu.VMEM((blocks, QB, QB), f32),
            pltpu.VMEM((N, tok_count), bf16),
        ],
        2 * tok_count * DIN * 8 * N,
        8 * tok_count * DIN,
        "back",
    )(scal, act, act, dt, cum, cumt, ey, s0)


def tail_kernel(
    scal, act, bc, dact, u, ey, dxt, taps, dt, sg, cum, g_in, s_in, skip, heads,
    db_loc, dc_loc, dc_dev, r_loc, r_dev, r2, cq,
    eu_out, er_out, gconv, ghead,
    ebuf, ubuf, p_acc, d_acc, db_acc, gs_acc,
):
    step = pl.program_id(0)
    last = pl.num_programs(0) - 1
    tok_count = act.shape[0]
    ext = tok_count + HALO
    lo = scal[1]
    hi = scal[2]

    @pl.when(step == 0)
    def _():
        p_acc[...] = jnp.zeros_like(p_acc)
        d_acc[...] = jnp.zeros_like(d_acc)
        db_acc[...] = jnp.zeros_like(db_acc)
        gs_acc[...] = jnp.zeros_like(gs_acc)
        ebuf[...] = jnp.zeros_like(ebuf)

    bmat = bc[:, :N]

    @pl.when(step < last)
    def _():
        cumr = head_columns(cum[...], step)
        dtr = spread_group(head_columns(dt[...], step))
        xf = act[...].astype(f32)
        xtf = (xf * dtr).astype(bf16).astype(f32)
        low = g_in[...]
        end = cumr[tok_count - 1 : tok_count]
        ecl = jnp.exp(spread_group(end - cumr))
        dxd = ecl * nn(bmat, low)
        dx = dxt[...].astype(f32) + dxd
        pick = head_picker(GROUP, 4 * step)
        p_acc[...] += nn((xtf * dxd).astype(bf16), pick)
        d_acc[...] += nn((xf * dx).astype(bf16), pick)
        db_acc[...] += nt((xtf * ecl).astype(bf16), low)
        vec = jnp.sum(low.astype(f32) * s_in[...].astype(f32), axis=0, keepdims=True)
        vec = vec * jnp.exp(spread_group(end))
        gs_acc[...] += exact_nn(jnp.broadcast_to(vec, (8, GROUP)), pick.astype(f32))
        ebuf[HALO : HALO + tok_count, :] = (
            dtr * dx + skip[0:1, :] * ey[...].astype(f32)
        ) * dact[...].astype(f32)

    @pl.when(step == last)
    def _():
        ebuf[HALO : HALO + tok_count, :N] = (db_loc[...] + db_acc[...]) * dact[:, :N].astype(f32)
        ebuf[HALO : HALO + tok_count, N:] = (dc_loc[...] + dc_dev[...]) * dact[:, N:].astype(f32)
        rate = heads[1:2, :]
        upper = (iota((QB, QB), 0) <= iota((QB, QB), 1)).astype(f32)
        strict = (iota((QB, QB), 0) > iota((QB, QB), 1)).astype(f32)
        blocks = tok_count // QB
        devs = jnp.zeros((1, LANE), f32)
        suffix = [None] * blocks
        for q in reversed(range(blocks)):
            rows = slice(q * QB, (q + 1) * QB)
            within = exact_nn(upper, r_loc[rows, :] - r2[rows, :]) + cq[q : q + 1, :]
            dev = exact_nn(upper, r_dev[rows, :]) + devs
            devs = dev[0:1]
            suffix[q] = within + dev
        before = gs_acc[0:1, :]
        glog = jnp.zeros((1, LANE), f32)
        gdt = jnp.zeros((1, LANE), f32)
        er_out[0:HALO, :] = jnp.zeros((HALO, LANE), bf16)
        for q in range(blocks):
            rows = slice(q * QB, (q + 1) * QB)
            pq = p_acc[rows, :]
            eda = suffix[q] + exact_nn(strict, pq) + before
            before = before + jnp.sum(pq, axis=0, keepdims=True)
            er = (d_acc[rows, :] + rate * eda) * sg[rows, :]
            gdt = gdt + jnp.sum(er, axis=0, keepdims=True)
            glog = glog + rate * jnp.sum(dt[rows, :] * eda, axis=0, keepdims=True)
            er_out[HALO + q * QB : HALO + (q + 1) * QB, :] = er.astype(bf16)
        ghead[...] = jnp.concatenate([gdt, glog, jnp.zeros((6, LANE), f32)], axis=0)

    ubuf[...] = u[...].astype(f32)
    ec = ebuf[HALO : HALO + tok_count, :]
    gs = [
        jnp.sum(ec * ubuf[HALO - 3 + k : HALO - 3 + k + tok_count, :], axis=0, keepdims=True)
        for k in range(K)
    ]
    gs.append(jnp.sum(ec, axis=0, keepdims=True))
    gs.append(jnp.zeros((3, ec.shape[1]), f32))
    gconv[...] = jnp.concatenate(gs, axis=0)
    eu = sum(taps[k : k + 1, :] * ebuf[3 - k : 3 - k + ext, :] for k in range(K))
    pos = iota(eu.shape, 0) - HALO
    eu_out[...] = jnp.where((pos >= lo) & (pos < hi), eu, 0.0).astype(bf16)


def tail(scal, act, dact, u, ey, dxt, taps, dt, sg, cum, g_in, s_in, skip, heads, smalls):
    tok_count = act.shape[0]
    ext = tok_count + HALO
    groups = DIN // GROUP

    def col(j, *_):
        return (0, j)

    def colx(j, *_):
        return (0, jnp.minimum(j, groups - 1))

    wide = pl.BlockSpec((tok_count, GROUP), col)
    widex = pl.BlockSpec((tok_count, GROUP), colx)
    small = const_spec((tok_count, LANE))
    return call(
        tail_kernel,
        (groups + 1,),
        [
            wide,
            pl.BlockSpec((tok_count, GROUP), lambda j, *_: (0, groups)),
            wide,
            pl.BlockSpec((ext, GROUP), col),
            widex,
            widex,
            pl.BlockSpec((8, GROUP), col),
            small,
            small,
            small,
            pl.BlockSpec((N, GROUP), colx),
            pl.BlockSpec((N, GROUP), colx),
            pl.BlockSpec((8, GROUP), colx),
            const_spec((8, LANE)),
            small,
            small,
            small,
            small,
            small,
            small,
            const_spec((8, LANE)),
        ],
        [
            pl.BlockSpec((ext, GROUP), col),
            const_spec((ext, LANE)),
            pl.BlockSpec((8, GROUP), col),
            const_spec((8, LANE)),
        ],
        [
            jax.ShapeDtypeStruct((ext, CONV), bf16),
            jax.ShapeDtypeStruct((ext, LANE), bf16),
            jax.ShapeDtypeStruct((8, CONV), f32),
            jax.ShapeDtypeStruct((8, LANE), f32),
        ],
        [
            pltpu.VMEM((ext + HALO, GROUP), f32),
            pltpu.VMEM((ext, GROUP), f32),
            pltpu.VMEM((tok_count, LANE), f32),
            pltpu.VMEM((tok_count, LANE), f32),
            pltpu.VMEM((tok_count, LANE), f32),
            pltpu.VMEM((8, LANE), f32),
        ],
        2 * tok_count * DIN * 4 * N,
        12 * tok_count * DIN,
        "tail",
    )(
        scal, act, act, dact, u, ey, dxt, taps, dt, sg, cum, g_in, s_in, skip, heads, *smalls
    )


def splitk_kernel(scal, a, w_own, w_oth, *rest):
    half = w_own.shape[0]
    own = pl.ds(pl.multiple_of(scal[0] * half, LANE), half)
    oth = pl.ds(pl.multiple_of((1 - scal[0]) * half, LANE), half)
    total = nn(a[:, own], w_own[...]) + nn(a[:, oth], w_oth[...])
    if len(rest) == 2:
        total = total + rest[0][...].astype(f32)
    out = rest[-1]
    out[...] = total.astype(out.dtype)


def splitk(scal, a, w_own, w_oth, add, name):
    rows, depth = a.shape
    width = w_own.shape[1]
    col = lambda j, *_: (0, j)
    specs = [
        const_spec((rows, depth)),
        pl.BlockSpec((depth // 2, GROUP), col),
        pl.BlockSpec((depth // 2, GROUP), col),
    ]
    args = [a, w_own, w_oth]
    if add is not None:
        specs.append(pl.BlockSpec((rows, GROUP), col))
        args.append(add)
    return call(
        splitk_kernel,
        (width // GROUP,),
        specs,
        pl.BlockSpec((rows, GROUP), col),
        jax.ShapeDtypeStruct((rows, width), bf16),
        [],
        2 * rows * depth * width,
        2 * (rows * depth + depth * width + rows * width),
        name,
    )(scal, *args)


def halves_kernel(scal, *refs):
    out = refs[-1]
    count = (len(refs) - 1) // 3
    steps = pl.num_programs(0) // 2
    step = pl.program_id(0)

    @pl.when(step < steps)
    def _():
        total = sum(nt(refs[3 * i][...], refs[3 * i + 1][...]) for i in range(count))
        out[...] = total.astype(out.dtype)

    @pl.when(step >= steps)
    def _():
        total = sum(nt(refs[3 * i][...], refs[3 * i + 2][...]) for i in range(count))
        out[...] = total.astype(out.dtype)


def halves(scal, terms, kind, name):
    rows = terms[0][0].shape[0]
    span = terms[0][1].shape[0]
    steps = span // GROUP
    specs = []
    args = []
    flops = 0
    for a, w_own, w_oth in terms:
        depth = a.shape[1]
        specs += [
            const_spec((rows, depth)),
            pl.BlockSpec((GROUP, depth), lambda j, *_: (jnp.minimum(j, steps - 1), 0)),
            pl.BlockSpec((GROUP, depth), lambda j, *_: (jnp.maximum(j - steps, 0), 0)),
        ]
        args += [a, w_own, w_oth]
        flops += 4 * rows * depth * span
    return call(
        halves_kernel,
        (2 * steps,),
        specs,
        pl.BlockSpec((rows, GROUP), lambda j, s: (0, lax.rem(j + steps * s[0], 2 * steps))),
        jax.ShapeDtypeStruct((rows, 2 * span), kind),
        [],
        flops,
        flops // rows,
        name,
    )(scal, *args)


def swap(x):
    return lax.ppermute(x, "fsdp", [(0, 1), (1, 0)])


def shifted(x, by):
    length = lax.axis_size("tm")
    return lax.ppermute(x, "tm", [(i, (i + by) % length) for i in range(length)])


def ordered(core, mine, other, axis):
    return jnp.where(
        core == 0,
        jnp.concatenate([mine, other], axis=axis),
        jnp.concatenate([other, mine], axis=axis),
    )


def bits_of(axis):
    return [(axis, 1 << b) for b in range((lax.axis_size(axis) - 1).bit_length())]


def across(x, axis, bit):
    return lax.ppermute(x, axis, [(i, i ^ bit) for i in range(lax.axis_size(axis))])


def reduced(buf, order):
    for axis, bit in order:
        n = buf.shape[0] // 2
        side = (lax.axis_index(axis) // bit) % 2
        send = lax.dynamic_slice_in_dim(buf, (1 - side) * n, n, 0)
        keep = lax.dynamic_slice_in_dim(buf, side * n, n, 0)
        got = across(send.astype(bf16), axis, bit)
        buf = (keep.astype(f32) + got.astype(f32)).astype(bf16)
    for axis, bit in reversed(order):
        n = buf.shape[0]
        side = (lax.axis_index(axis) // bit) % 2
        got = across(buf, axis, bit)
        both = jnp.zeros((2 * n,) + buf.shape[1:], bf16)
        both = lax.dynamic_update_slice_in_dim(both, buf, side * n, 0)
        buf = lax.dynamic_update_slice_in_dim(both, got, (1 - side) * n, 0)
    return buf


def summed(grad):
    rep = bits_of("rep")
    tm = bits_of("tm")
    cut = len(rep) // 2
    n = grad.shape[0] // 2
    first = reduced(grad[:n], rep + tm)
    second = reduced(grad[n:], rep[cut:] + rep[:cut] + tm)
    return jnp.concatenate([first, second], axis=0).astype(f32)


def body(
    tokens, in_weight, out_weight, norm_gain, conv_weight, conv_bias, dt_bias, a_log,
    d_skip, gate_gain, lengths, starts, cotangent,
):
    core = lax.axis_index("fsdp")
    tm = lax.axis_index("tm")
    tm_size = lax.axis_size("tm")
    tok = tokens[0]
    upstream = cotangent[0]
    tok_count, d = tok.shape
    half_d = in_weight.shape[0]
    half_in = out_weight.shape[0]
    half_conv = conv_bias.shape[0]
    half_heads = dt_bias.shape[0]

    lo = starts[0] - tm * tok_count
    scal = jnp.stack([core, lo, lo + lengths[0]]).astype(jnp.int32)

    def wide(v):
        return jnp.pad(v, (0, half_conv - v.shape[0]))[None]

    pack = jnp.concatenate(
        [
            conv_weight,
            conv_bias[None],
            wide(gate_gain),
            wide(norm_gain),
            wide(jnp.concatenate([dt_bias, a_log, d_skip])),
        ],
        axis=0,
    ).astype(bf16)
    pack_oth = swap(pack)
    halo = shifted(tok[tok_count - HALO :], 1)
    wu_own = jnp.pad(in_weight[:, DIN:], ((0, 0), (0, LANE - H))).astype(bf16)
    wu_oth = swap(wu_own)
    wz_own = in_weight[:, :DIN].astype(bf16)
    wz_oth = swap(wz_own)
    wo_own = out_weight.astype(bf16)
    wo_oth = swap(wo_own)

    def both(row, length):
        return ordered(core, pack[row, :length], pack_oth[row, :length], 0).astype(f32)

    def both_heads(i):
        part = slice(i * half_heads, (i + 1) * half_heads)
        return ordered(core, pack[7, part], pack_oth[7, part], 0).astype(f32)

    taps = jnp.pad(
        ordered(core, pack[:5], pack_oth[:5], 1).astype(f32), ((0, 3), (0, 0))
    )
    gate_vec = both(5, half_in)
    gain = both(6, half_d)[None]
    skip_vec = jnp.repeat(both_heads(2), P_SIZE)
    vecs = jnp.pad(jnp.stack([gate_vec, skip_vec]), ((0, 6), (0, 0)))
    skip8 = jnp.pad(skip_vec[None], ((0, 7), (0, 0)))
    heads = jnp.pad(
        jnp.stack([both_heads(0), -jnp.exp(both_heads(1))]), ((0, 6), (0, LANE - H))
    )

    normed, u, act, dact, dt, sg, cum, cumt, st = front(
        scal, tok, halo, gain, wu_own, wu_oth, taps, heads
    )
    cumt = cumt[:H].reshape(H // 4, 4, tok_count)
    total = jnp.exp(jnp.repeat(cum[tok_count - 1, :H], P_SIZE))[None]

    def chain(local, by, first):
        pieces = []
        for part in range(2):
            cols = slice(part * (DIN // 2), (part + 1) * (DIN // 2))
            send = local[:, cols].astype(bf16)
            got = None
            for hop in range(tm_size - 1):
                got = shifted(send, by)
                got = jnp.where(tm == first, jnp.zeros_like(got), got)
                if hop < tm_size - 2:
                    send = (local[:, cols] + total[:, cols] * got.astype(f32)).astype(bf16)
            pieces.append(got)
        return jnp.concatenate(pieces, axis=1)

    s_in = chain(st, 1, 0)
    z = splitk(scal, normed[HALO:], wz_own, wz_oth, None, "gate_proj")
    eg = halves(scal, [(upstream, wo_own, wo_oth)], bf16, "grad_gated")
    yloc, s0 = intra(scal, act, dt, cum, cumt)
    gated, ey, ez, r_loc, r_dev, dc_dev, g_loc, gs = gate(
        scal, yloc, act, z, eg, cum, s_in, vecs
    )

    def mine(x, half):
        return lax.dynamic_slice_in_dim(x, core * half, half, 1)

    def theirs(x, half):
        return lax.dynamic_slice_in_dim(x, (1 - core) * half, half, 1)

    def outer(a, b):
        return lax.dot_general(a, b, (((0,), (0,)), ((), ())), preferred_element_type=f32)

    up_oth = swap(upstream)
    normed_oth = swap(theirs(normed, half_d))
    normed_own = mine(normed, half_d)
    gated_oth = swap(theirs(gated, half_in))
    ez_oth = swap(ez)
    g_in = chain(g_loc, -1, tm_size - 1)
    grad_out = outer(mine(gated, half_in), upstream) + outer(gated_oth, up_oth)
    grad_z = outer(normed_own[HALO:], ez) + outer(normed_oth[HALO:], ez_oth)
    grad_out_w = summed(grad_out)
    grad_z_w = summed(grad_z)
    output = splitk(scal, gated, wo_own, wo_oth, tok, "out_proj")
    dxt, db_loc, dc_loc, r2, cq = back(scal, act, dt, cum, cumt, ey, s0)
    eu, er, gconv, ghead = tail(
        scal, act, dact, u, ey, dxt, taps, dt, sg, cum, g_in, s_in, skip8, heads,
        (db_loc, dc_loc, dc_dev, r_loc, r_dev, r2, cq),
    )
    eur = jnp.concatenate([eu, er], axis=1)
    eur_oth = swap(eur)
    grad_u = outer(normed_own, eur) + outer(normed_oth, eur_oth)
    grad_u_w = summed(grad_u)

    ez_ext = jnp.pad(ez, ((HALO, 0), (0, 0)))
    e_normed = halves(
        scal, [(ez_ext, wz_own, wz_oth), (eur, wu_own, wu_oth)], f32, "grad_normed"
    )
    ext_tok = jnp.concatenate([halo, tok], axis=0).astype(f32)
    rs = lax.rsqrt(jnp.mean(ext_tok * ext_tok, axis=-1, keepdims=True) + EPS)
    unit = ext_tok * rs
    scaled = e_normed * gain
    grad_in = rs * (scaled - unit * jnp.mean(scaled * unit, axis=-1, keepdims=True))
    grad_gain = jnp.sum(e_normed * unit, axis=0)
    edge = shifted(grad_in[:HALO], -1)
    edge = jnp.where(tm == tm_size - 1, jnp.zeros_like(edge), edge)
    input_grad = upstream.astype(f32) + grad_in[HALO:]
    input_grad = input_grad.at[tok_count - HALO :].add(edge)

    grad_skip = jnp.sum(gs[1].reshape(H, P_SIZE), axis=1)

    def side(v, half):
        return jnp.stack([v[:half], v[half : 2 * half]])

    def slot(v, half):
        return jnp.pad(side(v, half), ((0, 0), (0, half_conv - half)))[:, None]

    head_grads = jnp.stack([ghead[0, :H], ghead[1, :H], grad_skip])
    head_sides = jnp.stack(
        [head_grads[:, :half_heads].reshape(-1), head_grads[:, half_heads:].reshape(-1)]
    )
    packed = jnp.concatenate(
        [
            gconv[:5].reshape(5, 2, half_conv).transpose(1, 0, 2),
            slot(gs[0], half_in),
            slot(grad_gain, half_d),
            jnp.pad(head_sides, ((0, 0), (0, half_conv - 3 * half_heads)))[:, None],
        ],
        axis=1,
    )
    own = lax.dynamic_index_in_dim(packed, core, 0, keepdims=False)
    small = own + swap(lax.dynamic_index_in_dim(packed, 1 - core, 0, keepdims=False))
    for axis, bit in bits_of("rep") + bits_of("tm"):
        small = small + across(small, axis, bit)

    grad_in_w = jnp.concatenate([grad_z_w, grad_u_w[:, : CONV + H]], axis=1)
    hs = half_heads
    return (
        output[None],
        input_grad[None],
        grad_in_w,
        grad_out_w,
        small[6, :half_d],
        small[:4],
        small[4],
        small[7, :hs],
        small[7, hs : 2 * hs],
        small[7, 2 * hs : 3 * hs],
        small[5, :half_in],
    )


def solution(mesh):
    return jax.shard_map(
        body,
        mesh=mesh,
        in_specs=(
            P(("rep", "fsdp"), "tm", None),
            P("fsdp", None),
            P("fsdp", None),
            P("fsdp"),
            P(None, "fsdp"),
            P("fsdp"),
            P("fsdp"),
            P("fsdp"),
            P("fsdp"),
            P("fsdp"),
            P(("rep", "fsdp")),
            P(("rep", "fsdp")),
            P(("rep", "fsdp"), "tm", None),
        ),
        out_specs=(
            P(("rep", "fsdp"), "tm", None),
            P(("rep", "fsdp"), "tm", None),
            P("fsdp", None),
            P("fsdp", None),
            P("fsdp"),
            P(None, "fsdp"),
            P("fsdp"),
            P("fsdp"),
            P("fsdp"),
            P("fsdp"),
            P("fsdp"),
        ),
        check_vma=False,
    )
```

```python
import jax
import jax.numpy as jnp
from jax import lax
from jax.experimental import pallas as pl
from jax.experimental.pallas import tpu as pltpu
from jax.sharding import PartitionSpec as P

H = 32
P_SIZE = 64
N = 128
K = 4
DIN = 2048
CONV = 2304
EPS = 1e-05
QB = 128
HALO = 16
GROUP = 256
LANE = 128

bf16 = jnp.bfloat16
f32 = jnp.float32
HIGHEST = lax.Precision.HIGHEST

VMEM_LIMIT = 60 * 1024 * 1024


def nn(a, b):
    return lax.dot_general(a, b, (((1,), (0,)), ((), ())), preferred_element_type=f32)


def nt(a, b):
    return lax.dot_general(a, b, (((1,), (1,)), ((), ())), preferred_element_type=f32)


def exact_nn(a, b):
    return lax.dot_general(
        a, b, (((1,), (0,)), ((), ())), precision=HIGHEST, preferred_element_type=f32
    )


def iota(shape, dim):
    return lax.broadcasted_iota(jnp.int32, shape, dim)


def tn(a, b):
    return lax.dot_general(a, b, (((0,), (0,)), ((), ())), preferred_element_type=f32)


def sigmoid(v):
    return 0.5 + 0.5 * jnp.tanh(0.5 * v)


def split_two(v):
    hi = v.astype(bf16)
    lo = (v - hi.astype(f32)).astype(bf16)
    return hi, lo


def const_spec(shape):
    return pl.BlockSpec(shape, lambda *_: tuple(0 for _ in shape))


def params(steps=1):
    return pltpu.CompilerParams(
        dimension_semantics=("arbitrary",) * steps, vmem_limit_bytes=VMEM_LIMIT
    )


def call(kernel, grid, in_specs, out_specs, out_shape, scratch, flops, nbytes, name):
    return pl.pallas_call(
        kernel,
        grid_spec=pltpu.PrefetchScalarGridSpec(
            num_scalar_prefetch=1,
            grid=grid,
            in_specs=in_specs,
            out_specs=out_specs,
            scratch_shapes=scratch,
        ),
        out_shape=out_shape,
        compiler_params=params(len(grid)),
        cost_estimate=pl.CostEstimate(flops=flops, bytes_accessed=nbytes, transcendentals=0),
        name=name,
    )


def spread(cols, pair):
    left = cols[:, 2 * pair : 2 * pair + 1]
    right = cols[:, 2 * pair + 1 : 2 * pair + 2]
    lanes = iota((cols.shape[0], LANE), 1)
    return jnp.where(lanes < P_SIZE, left, right)


def spread_group(cols):
    return jnp.concatenate([spread(cols, 0), spread(cols, 1)], axis=1)


def block_diag(pair_low):
    lanes = iota(pair_low.shape, 1)
    zero = jnp.zeros_like(pair_low)
    return jnp.concatenate(
        [jnp.where(lanes < P_SIZE, pair_low, zero), jnp.where(lanes < P_SIZE, zero, pair_low)],
        axis=0,
    )


def head_columns(cols, group):
    return pltpu.roll(cols, lax.rem(LANE - 4 * group, LANE), 1)


def head_picker(lanes_in, first_head):
    rows = iota((lanes_in, LANE), 0) // P_SIZE + first_head
    return (rows == iota((lanes_in, LANE), 1)).astype(bf16)


def pack_kernel(scal, own, oth, taps, vecs, heads, gain):
    core = scal[0]
    span = own.shape[1]
    half_in = vecs.shape[1] // 2
    half_d = gain.shape[1] // 2
    taps[...] = jnp.zeros_like(taps)
    vecs[...] = jnp.zeros_like(vecs)
    sides = []
    for src, place in ((own, core), (oth, 1 - core)):
        block = src[...].astype(f32)

        def at(width):
            return pl.ds(pl.multiple_of(place * width, LANE), width)

        taps[0:5, at(span)] = block[0:5]
        vecs[0:1, at(half_in)] = block[5:6, :half_in]
        gain[0:1, at(half_d)] = block[6:7, :half_d]
        sides.append(jnp.broadcast_to(block[7:8, :LANE], (8, LANE)))
    width = H // 2
    lanes = iota((8, LANE), 1)
    rows = []
    for i in range(3):
        first = jnp.where(core == 0, sides[0], sides[1])
        second = jnp.where(core == 0, sides[1], sides[0])
        low = pltpu.roll(first, (LANE - i * width) % LANE, 1)
        high = pltpu.roll(second, (LANE - i * width + width) % LANE, 1)
        rows.append(jnp.where(lanes < width, low, jnp.where(lanes < H, high, 0.0)))
    rate = jnp.where(lanes < H, -jnp.exp(rows[1]), 0.0)
    pick = iota((8, LANE), 0)
    heads[...] = jnp.where(pick == 0, rows[0], jnp.where(pick == 1, rate, 0.0))
    skip = rows[2].astype(bf16)
    expand = (iota((LANE, DIN), 1) // P_SIZE == iota((LANE, DIN), 0)).astype(bf16)
    vecs[1:2, :] = nn(skip, expand)[0:1]


def pack_vectors(scal, own, oth, d):
    return call(
        pack_kernel,
        (1,),
        [const_spec(own.shape), const_spec(oth.shape)],
        [const_spec((8, CONV)), const_spec((8, DIN)), const_spec((8, LANE)), const_spec((1, d))],
        [
            jax.ShapeDtypeStruct((8, CONV), f32),
            jax.ShapeDtypeStruct((8, DIN), f32),
            jax.ShapeDtypeStruct((8, LANE), f32),
            jax.ShapeDtypeStruct((1, d), f32),
        ],
        [],
        10**6,
        10**5,
        "vectors",
    )(scal, own, oth)


def front_kernel(
    scal, tok, halo, gain, w_own, w_oth, r_own, r_oth, taps, heads,
    n_own, n_oth, u_out, act_out, dact_out, dt_out, sg_out, cum_out, cumt_out, st_out,
    ubuf, bt, ecl,
):
    step = pl.program_id(0)
    tok_count = tok.shape[0]
    half = w_own.shape[1]
    own = pl.ds(pl.multiple_of(scal[0] * half, LANE), half)
    oth = pl.ds(pl.multiple_of((1 - scal[0]) * half, LANE), half)
    lo = scal[1]
    hi = scal[2]

    @pl.when(step == 0)
    def _():
        def rows_of(src, base, dst, count):
            x = src[pl.ds(base, count), :].astype(f32)
            rs = lax.rsqrt(jnp.mean(x * x, axis=-1, keepdims=True) + EPS)
            for out, cols in ((n_own, own), (n_oth, oth)):
                part = src[pl.ds(base, count), cols].astype(f32)
                out[pl.ds(dst, count), :] = (part * rs * gain[:, cols]).astype(bf16)

        rows_of(halo, 0, 0, HALO)

        def body(i, carry):
            base = pl.multiple_of(i * 64, 64)
            rows_of(tok, base, pl.multiple_of(base + HALO, 16), 64)
            return carry

        lax.fori_loop(0, tok_count // 64, body, 0)
        r = nt(n_own[HALO:, :], r_own[...]) + nt(n_oth[HALO:, :], r_oth[...])
        pre = r.astype(bf16).astype(f32) + heads[0:1, :]
        pos = iota((tok_count, LANE), 0)
        keep = (pos >= lo) & (pos < hi) & (iota((tok_count, LANE), 1) < H)
        soft = jnp.maximum(pre, 0.0) + jnp.log1p(jnp.exp(-jnp.abs(pre)))
        dt = jnp.where(keep, soft, 0.0)
        dt_out[...] = dt
        sg_out[...] = jnp.where(keep, 1.0 / (1.0 + jnp.exp(-pre)), 0.0)
        da = dt * heads[1:2, :]
        tri = (iota((QB, QB), 0) >= iota((QB, QB), 1)).astype(f32)
        carry = jnp.zeros((1, LANE), f32)
        for q in range(tok_count // QB):
            cum = exact_nn(tri, da[q * QB : (q + 1) * QB]) + carry
            cum_out[q * QB : (q + 1) * QB, :] = cum
            cumt_out[:, q * QB : (q + 1) * QB] = cum.T
            carry = cum[QB - 1 : QB]
        ecl[...] = jnp.exp(carry - cum_out[...])

    u = nt(n_own[...], w_own[...]) + nt(n_oth[...], w_oth[...])
    pos = iota(u.shape, 0) - HALO
    u = jnp.where((pos >= lo) & (pos < hi), u, 0.0).astype(bf16)
    u_out[...] = u
    ubuf[...] = u.astype(f32)
    c = taps[4:5, :] + sum(
        taps[k : k + 1, :] * ubuf[HALO - 3 + k : HALO - 3 + k + tok_count, :] for k in range(K)
    )
    s = sigmoid(c)
    act = (c * s).astype(bf16)
    act_out[...] = act
    dact_out[...] = (s * (1.0 + c * (1.0 - s))).astype(bf16)

    @pl.when(step == 0)
    def _():
        bt[...] = act[:, :N].astype(f32).T.astype(bf16)

    @pl.when(step > 0)
    def _():
        group = step - 1
        dtg = spread_group(head_columns(dt_out[...], group))
        ecg = spread_group(head_columns(ecl[...], group))
        xt = (act.astype(f32) * dtg).astype(bf16)
        xw = (xt.astype(f32) * ecg).astype(bf16)
        st_out[...] = nn(bt[...], xw)


def front(scal, tok, halo, gain, wu_own, wu_oth, taps, heads):
    tok_count, d = tok.shape
    half = wu_own.shape[1]
    ext = tok_count + HALO
    groups = CONV // GROUP
    first = groups - 1

    def col(j, *_):
        return (0, (j + first) % groups)

    weight = pl.BlockSpec((GROUP, half), lambda j, *_: ((j + first) % groups, 0))
    narrow = pl.BlockSpec((LANE, half), lambda j, *_: (CONV // LANE, 0))
    return call(
        front_kernel,
        (groups,),
        [
            const_spec((tok_count, d)),
            const_spec((HALO, d)),
            const_spec((1, d)),
            weight,
            weight,
            narrow,
            narrow,
            pl.BlockSpec((8, GROUP), col),
            const_spec((8, LANE)),
        ],
        [
            const_spec((ext, half)),
            const_spec((ext, half)),
            pl.BlockSpec((ext, GROUP), col),
            pl.BlockSpec((tok_count, GROUP), col),
            pl.BlockSpec((tok_count, GROUP), col),
            const_spec((tok_count, LANE)),
            const_spec((tok_count, LANE)),
            const_spec((tok_count, LANE)),
            const_spec((LANE, tok_count)),
            pl.BlockSpec((N, GROUP), lambda j, *_: (0, jnp.maximum(j - 1, 0))),
        ],
        [
            jax.ShapeDtypeStruct((ext, half), bf16),
            jax.ShapeDtypeStruct((ext, half), bf16),
            jax.ShapeDtypeStruct((ext, CONV), bf16),
            jax.ShapeDtypeStruct((tok_count, CONV), bf16),
            jax.ShapeDtypeStruct((tok_count, CONV), bf16),
            jax.ShapeDtypeStruct((tok_count, LANE), f32),
            jax.ShapeDtypeStruct((tok_count, LANE), f32),
            jax.ShapeDtypeStruct((tok_count, LANE), f32),
            jax.ShapeDtypeStruct((LANE, tok_count), f32),
            jax.ShapeDtypeStruct((N, DIN), f32),
        ],
        [
            pltpu.VMEM((ext, GROUP), f32),
            pltpu.VMEM((N, tok_count), bf16),
            pltpu.VMEM((tok_count, LANE), f32),
        ],
        2 * ext * d * (CONV + LANE),
        2 * (ext * d + d * CONV + 3 * ext * CONV),
        "front",
    )(scal, tok, halo, gain, wu_own, wu_oth, wu_own, wu_oth, taps, heads)


def intra_kernel(scal, x, bc, dt, cum, cumt, y_out, s0_out, scores, bt):
    group = pl.program_id(0)
    blocks = x.shape[0] // QB

    @pl.when(group == 0)
    def _():
        lower = iota((QB, QB), 0) >= iota((QB, QB), 1)
        bt[...] = bc[:, :N].astype(f32).T.astype(bf16)
        for q in range(blocks):
            rows = slice(q * QB, (q + 1) * QB)
            scores[q] = jnp.where(lower, nt(bc[rows, N:], bc[rows, :N]), 0.0)

    dtr = head_columns(dt[...], group)
    cumr = head_columns(cum[...], group)
    carry = jnp.zeros((N, GROUP), f32)
    for q in range(blocks):
        rows = slice(q * QB, (q + 1) * QB)
        cq = cumr[rows]
        end = cq[QB - 1 : QB]
        start = cumr[q * QB - 1 : q * QB] if q else jnp.zeros((1, LANE), f32)
        xt = (x[rows, :].astype(f32) * spread_group(dtr[rows])).astype(bf16)
        low_carry = carry.astype(bf16)
        s0_out[q] = low_carry
        ys = []
        for pair in range(2):
            mats = []
            for e in range(2):
                h = 2 * pair + e
                row = cumt[0, h : h + 1, rows]
                decay = jnp.exp(jnp.minimum(cq[:, h : h + 1] - row, 0.0))
                mats.append((decay * scores[q]).astype(bf16))
            ys.append(
                nn(
                    jnp.concatenate(mats, axis=1),
                    block_diag(xt[:, pair * LANE : (pair + 1) * LANE]),
                )
            )
        y = jnp.concatenate(ys, axis=1)
        if q:
            y = y + jnp.exp(spread_group(cq - start)) * nn(bc[rows, N:], low_carry)
        y_out[rows, :] = y
        if q < blocks - 1:
            xw = (xt.astype(f32) * jnp.exp(spread_group(end - cq))).astype(bf16)
            fresh = nn(bt[:, rows], xw)
            carry = fresh if q == 0 else fresh + carry * jnp.exp(spread_group(end - start))


def intra(scal, act, dt, cum, cumt):
    tok_count = act.shape[0]
    blocks = tok_count // QB
    groups = DIN // GROUP
    return call(
        intra_kernel,
        (groups,),
        [
            pl.BlockSpec((tok_count, GROUP), lambda j, *_: (0, j)),
            pl.BlockSpec((tok_count, GROUP), lambda j, *_: (0, groups)),
            const_spec((tok_count, LANE)),
            const_spec((tok_count, LANE)),
            pl.BlockSpec((1, 4, tok_count), lambda j, *_: (j, 0, 0)),
        ],
        [
            pl.BlockSpec((tok_count, GROUP), lambda j, *_: (0, j)),
            pl.BlockSpec((blocks, N, GROUP), lambda j, *_: (0, 0, j)),
        ],
        [
            jax.ShapeDtypeStruct((tok_count, DIN), f32),
            jax.ShapeDtypeStruct((blocks, N, DIN), bf16),
        ],
        [pltpu.VMEM((blocks, QB, QB), f32), pltpu.VMEM((N, tok_count), bf16)],
        2 * tok_count * DIN * 3 * N,
        8 * tok_count * DIN,
        "intra",
    )(scal, act, act, dt, cum, cumt)


def gate_kernel(
    scal, yloc, act, z, eg, cum, s_in, vecs,
    gated, ey_out, ez_out, r_loc, r_dev, dc_out, g_out, gs_out,
    pick, vbuf, ytbuf, ydbuf,
):
    step = pl.program_id(0)
    rows = yloc.shape[0]
    groups = DIN // GROUP
    per = groups // 2

    @pl.when(step == 0)
    def _():
        pick[...] = head_picker(DIN, 0)
        g_out[...] = jnp.zeros_like(g_out)
        gs_out[...] = jnp.zeros_like(gs_out)

    pos = iota((rows, 1), 0) + step * rows
    valid = ((pos >= scal[1]) & (pos < scal[2])).astype(f32)
    cq = cum[...]
    ecq = jnp.exp(cq)
    cmat = act[:, DIN + N :]
    ssq = jnp.zeros((rows, GROUP), f32)
    for g in range(groups):
        cols = slice(g * GROUP, (g + 1) * GROUP)
        eg_cum = jnp.concatenate([spread(ecq, 2 * g), spread(ecq, 2 * g + 1)], axis=1)
        yd = eg_cum * nn(cmat, s_in[:, cols])
        ydbuf[:, cols] = yd
        yt = yloc[:, cols] + yd + vecs[1:2, cols] * act[:, cols].astype(f32)
        ytbuf[:, cols] = yt
        zz = z[:, cols].astype(f32)
        v = yt * (zz * sigmoid(zz))
        vbuf[:, cols] = v
        ssq = ssq + v * v
    rs = lax.rsqrt(jnp.sum(ssq, axis=-1, keepdims=True) / DIN + EPS)
    mixed = jnp.zeros((rows, GROUP), f32)
    for g in range(groups):
        cols = slice(g * GROUP, (g + 1) * GROUP)
        n = vbuf[:, cols] * rs
        vbuf[:, cols] = n
        gain = vecs[0:1, cols]
        side = (g // per) ^ scal[0]
        local = slice((g % per) * GROUP, (g % per + 1) * GROUP)
        gated[side, :, local] = (n * gain * valid).astype(bf16)
        e = eg[side, :, local].astype(f32) * valid
        gs_out[0:1, cols] += jnp.sum(e * n, axis=0, keepdims=True)
        mixed = mixed + e * gain * n
    m2 = jnp.sum(mixed, axis=-1, keepdims=True) / DIN
    rl = jnp.zeros((rows, LANE), f32)
    rd = jnp.zeros((rows, LANE), f32)
    dc = jnp.zeros((rows, N), f32)
    ct = cmat.astype(f32).T.astype(bf16)
    for g in range(groups):
        cols = slice(g * GROUP, (g + 1) * GROUP)
        n = vbuf[:, cols]
        side = (g // per) ^ scal[0]
        local = slice((g % per) * GROUP, (g % per + 1) * GROUP)
        e = eg[side, :, local].astype(f32) * valid
        ev = rs * (e * vecs[0:1, cols] - n * m2)
        zz = z[:, cols].astype(f32)
        sz = sigmoid(zz)
        ey = ev * (zz * sz)
        ez_out[:, cols] = (ev * ytbuf[:, cols] * (sz * (1.0 + zz * (1.0 - sz)))).astype(bf16)
        gs_out[1:2, cols] += jnp.sum(ey * act[:, cols].astype(f32), axis=0, keepdims=True)
        low = ey.astype(bf16)
        ey_out[:, cols] = low
        eyf = low.astype(f32)
        ph, pl_ = split_two(eyf * yloc[:, cols])
        rl = rl + nn(ph, pick[cols, :]) + nn(pl_, pick[cols, :])
        rd = rd + nn((eyf * ydbuf[:, cols]).astype(bf16), pick[cols, :])
        eg_cum = jnp.concatenate([spread(ecq, 2 * g), spread(ecq, 2 * g + 1)], axis=1)
        eye = (eyf * eg_cum).astype(bf16)
        g_out[:, cols] += nn(ct, eye)
        dc = dc + nt(eye, s_in[:, cols])
    r_loc[...] = rl
    r_dev[...] = rd
    dc_out[...] = dc


def gate(scal, yloc, act, z, eg, cum, s_in, vecs):
    tok_count = act.shape[0]
    rows = QB

    def rowspec(width):
        return pl.BlockSpec((rows, width), lambda j, *_: (j, 0))

    def out(width, kind):
        return jax.ShapeDtypeStruct((tok_count, width), kind)

    sides = pl.BlockSpec((2, rows, DIN // 2), lambda j, *_: (0, j, 0))

    return call(
        gate_kernel,
        (tok_count // rows,),
        [
            rowspec(DIN),
            rowspec(CONV),
            rowspec(DIN),
            sides,
            rowspec(LANE),
            const_spec((N, DIN)),
            const_spec((8, DIN)),
        ],
        [
            sides,
            rowspec(DIN),
            rowspec(DIN),
            rowspec(LANE),
            rowspec(LANE),
            rowspec(LANE),
            const_spec((N, DIN)),
            const_spec((8, DIN)),
        ],
        [
            jax.ShapeDtypeStruct((2, tok_count, DIN // 2), bf16),
            out(DIN, bf16),
            out(DIN, bf16),
            out(LANE, f32),
            out(LANE, f32),
            out(LANE, f32),
            jax.ShapeDtypeStruct((N, DIN), f32),
            jax.ShapeDtypeStruct((8, DIN), f32),
        ],
        [
            pltpu.VMEM((DIN, LANE), bf16),
            pltpu.VMEM((rows, DIN), f32),
            pltpu.VMEM((rows, DIN), f32),
            pltpu.VMEM((rows, DIN), f32),
        ],
        2 * tok_count * DIN * 6 * N,
        20 * tok_count * DIN,
        "gate",
    )(scal, yloc, act, z, eg, cum, s_in, vecs)


def back_kernel(
    scal, x, bc, dt, cum, cumt, ey, s0,
    dxt_out, db_out, dc_out, r2_out, cq_out,
    scores, dscores, ct,
):
    group = pl.program_id(0)
    last = pl.num_programs(0) - 1
    blocks = x.shape[0] // QB
    upper = iota((QB, QB), 0) <= iota((QB, QB), 1)

    @pl.when(group == 0)
    def _():
        ct[...] = bc[:, N:].astype(f32).T.astype(bf16)
        for q in range(blocks):
            rows = slice(q * QB, (q + 1) * QB)
            scores[q] = jnp.where(upper, nt(bc[rows, :N], bc[rows, N:]), 0.0)
        dscores[...] = jnp.zeros_like(dscores)
        db_out[...] = jnp.zeros_like(db_out)
        dc_out[...] = jnp.zeros_like(dc_out)
        r2_out[...] = jnp.zeros_like(r2_out)
        cq_out[...] = jnp.zeros_like(cq_out)

    dtr = head_columns(dt[...], group)
    cumr = head_columns(cum[...], group)
    picks = [head_picker(LANE, 4 * group + 2 * pair) for pair in range(2)]
    picks2 = [jnp.concatenate([p, p], axis=0) for p in picks]
    pick_all = head_picker(GROUP, 4 * group).astype(f32)
    carry = None
    for q in reversed(range(blocks)):
        rows = slice(q * QB, (q + 1) * QB)
        cq = cumr[rows]
        end = cq[QB - 1 : QB]
        start = cumr[q * QB - 1 : q * QB] if q else jnp.zeros((1, LANE), f32)
        xt = (x[rows, :].astype(f32) * spread_group(dtr[rows])).astype(bf16)
        eyq = ey[rows, :]
        dxs = []
        ds = jnp.zeros((QB, QB), f32)
        for pair in range(2):
            lanes = slice(pair * LANE, (pair + 1) * LANE)
            eybd = block_diag(eyq[:, lanes])
            dm = nt(xt[:, lanes], eybd)
            mats = []
            for e in range(2):
                h = 2 * pair + e
                row = cumt[0, h : h + 1, rows]
                decay = jnp.exp(jnp.minimum(row - cq[:, h : h + 1], 0.0))
                mats.append((decay * scores[q]).astype(bf16))
                ds = ds + decay * dm[:, e * QB : (e + 1) * QB]
            dxs.append(nn(jnp.concatenate(mats, axis=1), eybd))
        dscores[q] += ds
        dx = jnp.concatenate(dxs, axis=1)
        xtf = xt.astype(f32)
        eye = None
        if q:
            eye = (eyq.astype(f32) * jnp.exp(spread_group(cq - start))).astype(bf16)
            dc_out[rows, :] += nt(eye, s0[q])
        if carry is not None:
            low = carry.astype(bf16)
            ecl = jnp.exp(spread_group(end - cq))
            dst = ecl * nn(bc[rows, :N], low)
            db_out[rows, :] += nt((xtf * ecl).astype(bf16), low)
            total = jnp.exp(spread_group(end - start))
            vec = jnp.sum(xtf * dst, axis=0, keepdims=True)
            if q:
                vec = vec + total * jnp.sum(carry * s0[q].astype(f32), axis=0, keepdims=True)
            cq_out[q : q + 1, :] += exact_nn(jnp.broadcast_to(vec, (8, GROUP)), pick_all)[0:1]
            dx = dx + dst
        if q:
            fresh = nn(ct[:, rows], eye)
            carry = fresh if carry is None else fresh + total * carry
        dxt_out[rows, :] = dx.astype(bf16)
        prod = xtf * dx
        acc = jnp.zeros((QB, LANE), f32)
        for pair in range(2):
            ph, pl_ = split_two(prod[:, pair * LANE : (pair + 1) * LANE])
            acc = acc + nn(jnp.concatenate([ph, pl_], axis=1), picks2[pair])
        r2_out[rows, :] += acc

    @pl.when(group == last)
    def _():
        for q in range(blocks):
            rows = slice(q * QB, (q + 1) * QB)
            ds = jnp.where(upper, dscores[q], 0.0)
            db_out[rows, :] += nn(ds.astype(bf16), bc[rows, N:])
            dc_out[rows, :] += nn(ds.T.astype(bf16), bc[rows, :N])


def back(scal, act, dt, cum, cumt, ey, s0):
    tok_count = act.shape[0]
    blocks = tok_count // QB
    groups = DIN // GROUP
    wide = pl.BlockSpec((tok_count, GROUP), lambda j, *_: (0, j))
    small = const_spec((tok_count, LANE))
    return call(
        back_kernel,
        (groups,),
        [
            wide,
            pl.BlockSpec((tok_count, GROUP), lambda j, *_: (0, groups)),
            small,
            small,
            pl.BlockSpec((1, 4, tok_count), lambda j, *_: (j, 0, 0)),
            wide,
            pl.BlockSpec((blocks, N, GROUP), lambda j, *_: (0, 0, j)),
        ],
        [wide, small, small, small, const_spec((8, LANE))],
        [
            jax.ShapeDtypeStruct((tok_count, DIN), bf16),
            jax.ShapeDtypeStruct((tok_count, LANE), f32),
            jax.ShapeDtypeStruct((tok_count, LANE), f32),
            jax.ShapeDtypeStruct((tok_count, LANE), f32),
            jax.ShapeDtypeStruct((8, LANE), f32),
        ],
        [
            pltpu.VMEM((blocks, QB, QB), f32),
            pltpu.VMEM((blocks, QB, QB), f32),
            pltpu.VMEM((N, tok_count), bf16),
        ],
        2 * tok_count * DIN * 8 * N,
        8 * tok_count * DIN,
        "back",
    )(scal, act, act, dt, cum, cumt, ey, s0)


def tail_kernel(
    scal, act, bc, dact, u, ey, dxt, taps, dt, sg, cum, g_in, s_in, skip, heads,
    db_loc, dc_loc, dc_dev, r_loc, r_dev, r2, cq,
    eu_out, gconv, ghead,
    ebuf, ubuf, p_acc, d_acc, db_acc, gs_acc,
):
    step = pl.program_id(0)
    last = pl.num_programs(0) - 2
    tok_count = act.shape[0]
    ext = tok_count + HALO
    lo = scal[1]
    hi = scal[2]

    @pl.when(step == 0)
    def _():
        p_acc[...] = jnp.zeros_like(p_acc)
        d_acc[...] = jnp.zeros_like(d_acc)
        db_acc[...] = jnp.zeros_like(db_acc)
        gs_acc[...] = jnp.zeros_like(gs_acc)
        ebuf[...] = jnp.zeros_like(ebuf)

    bmat = bc[:, :N]

    @pl.when(step < last)
    def _():
        cumr = head_columns(cum[...], step)
        dtr = spread_group(head_columns(dt[...], step))
        xf = act[...].astype(f32)
        xtf = (xf * dtr).astype(bf16).astype(f32)
        low = g_in[...]
        end = cumr[tok_count - 1 : tok_count]
        ecl = jnp.exp(spread_group(end - cumr))
        dxd = ecl * nn(bmat, low)
        dx = dxt[...].astype(f32) + dxd
        pick = head_picker(GROUP, 4 * step)
        p_acc[...] += nn((xtf * dxd).astype(bf16), pick)
        d_acc[...] += nn((xf * dx).astype(bf16), pick)
        db_acc[...] += nt((xtf * ecl).astype(bf16), low)
        vec = jnp.sum(low.astype(f32) * s_in[...].astype(f32), axis=0, keepdims=True)
        vec = vec * jnp.exp(spread_group(end))
        gs_acc[...] += exact_nn(jnp.broadcast_to(vec, (8, GROUP)), pick.astype(f32))
        ebuf[HALO : HALO + tok_count, :] = (
            dtr * dx + skip[1:2, :] * ey[...].astype(f32)
        ) * dact[...].astype(f32)

    @pl.when(step == last)
    def _():
        ebuf[HALO : HALO + tok_count, :N] = (db_loc[...] + db_acc[...]) * dact[:, :N].astype(f32)
        ebuf[HALO : HALO + tok_count, N:] = (dc_loc[...] + dc_dev[...]) * dact[:, N:].astype(f32)

    @pl.when(step > last)
    def _():
        rate = heads[1:2, :]
        upper = (iota((QB, QB), 0) <= iota((QB, QB), 1)).astype(f32)
        strict = (iota((QB, QB), 0) > iota((QB, QB), 1)).astype(f32)
        blocks = tok_count // QB
        devs = jnp.zeros((1, LANE), f32)
        suffix = [None] * blocks
        for q in reversed(range(blocks)):
            rows = slice(q * QB, (q + 1) * QB)
            within = exact_nn(upper, r_loc[rows, :] - r2[rows, :]) + cq[q : q + 1, :]
            dev = exact_nn(upper, r_dev[rows, :]) + devs
            devs = dev[0:1]
            suffix[q] = within + dev
        before = gs_acc[0:1, :]
        glog = jnp.zeros((1, LANE), f32)
        gdt = jnp.zeros((1, LANE), f32)
        eu_out[...] = jnp.zeros_like(eu_out)
        for q in range(blocks):
            rows = slice(q * QB, (q + 1) * QB)
            pq = p_acc[rows, :]
            eda = suffix[q] + exact_nn(strict, pq) + before
            before = before + jnp.sum(pq, axis=0, keepdims=True)
            er = (d_acc[rows, :] + rate * eda) * sg[rows, :]
            gdt = gdt + jnp.sum(er, axis=0, keepdims=True)
            glog = glog + rate * jnp.sum(dt[rows, :] * eda, axis=0, keepdims=True)
            eu_out[HALO + q * QB : HALO + (q + 1) * QB, :LANE] = er.astype(bf16)
        ghead[...] = jnp.concatenate([gdt, glog, jnp.zeros((6, LANE), f32)], axis=0)

    @pl.when(step <= last)
    def _():
        ubuf[...] = u[...].astype(f32)
        ec = ebuf[HALO : HALO + tok_count, :]
        gs = [
            jnp.sum(ec * ubuf[HALO - 3 + k : HALO - 3 + k + tok_count, :], axis=0, keepdims=True)
            for k in range(K)
        ]
        gs.append(jnp.sum(ec, axis=0, keepdims=True))
        gs.append(jnp.zeros((3, ec.shape[1]), f32))
        gconv[...] = jnp.concatenate(gs, axis=0)
        eu = sum(taps[k : k + 1, :] * ebuf[3 - k : 3 - k + ext, :] for k in range(K))
        pos = iota(eu.shape, 0) - HALO
        eu_out[...] = jnp.where((pos >= lo) & (pos < hi), eu, 0.0).astype(bf16)


def tail(scal, act, dact, u, ey, dxt, taps, dt, sg, cum, g_in, s_in, skip, heads, smalls):
    tok_count = act.shape[0]
    ext = tok_count + HALO
    groups = DIN // GROUP

    def col(j, *_):
        return (0, jnp.minimum(j, groups))

    def colx(j, *_):
        return (0, jnp.minimum(j, groups - 1))

    wide = pl.BlockSpec((tok_count, GROUP), col)
    widex = pl.BlockSpec((tok_count, GROUP), colx)
    small = const_spec((tok_count, LANE))
    return call(
        tail_kernel,
        (groups + 2,),
        [
            wide,
            pl.BlockSpec((tok_count, GROUP), lambda j, *_: (0, groups)),
            wide,
            pl.BlockSpec((ext, GROUP), col),
            widex,
            widex,
            pl.BlockSpec((8, GROUP), col),
            small,
            small,
            small,
            pl.BlockSpec((N, GROUP), colx),
            pl.BlockSpec((N, GROUP), colx),
            pl.BlockSpec((8, GROUP), lambda j, *_: (0, jnp.minimum(j, groups - 1))),
            const_spec((8, LANE)),
            small,
            small,
            small,
            small,
            small,
            small,
            const_spec((8, LANE)),
        ],
        [
            pl.BlockSpec((ext, GROUP), lambda j, *_: (0, j)),
            pl.BlockSpec((8, GROUP), col),
            const_spec((8, LANE)),
        ],
        [
            jax.ShapeDtypeStruct((ext, CONV + GROUP), bf16),
            jax.ShapeDtypeStruct((8, CONV), f32),
            jax.ShapeDtypeStruct((8, LANE), f32),
        ],
        [
            pltpu.VMEM((ext + HALO, GROUP), f32),
            pltpu.VMEM((ext, GROUP), f32),
            pltpu.VMEM((tok_count, LANE), f32),
            pltpu.VMEM((tok_count, LANE), f32),
            pltpu.VMEM((tok_count, LANE), f32),
            pltpu.VMEM((8, LANE), f32),
        ],
        2 * tok_count * DIN * 4 * N,
        12 * tok_count * DIN,
        "tail",
    )(
        scal, act, act, dact, u, ey, dxt, taps, dt, sg, cum, g_in, s_in, skip, heads, *smalls
    )


def gate_proj_kernel(scal, a_own, a_oth, w_own, w_oth, out):
    out[...] = (
        nt(a_own[HALO:, :], w_own[...]) + nt(a_oth[HALO:, :], w_oth[...])
    ).astype(bf16)


def gate_proj(scal, n_own, n_oth, wz_own, wz_oth):
    ext, half = n_own.shape
    rows = ext - HALO
    wide = 2 * GROUP
    weight = pl.BlockSpec((wide, half), lambda j, *_: (j, 0))
    return call(
        gate_proj_kernel,
        (DIN // wide,),
        [const_spec((ext, half)), const_spec((ext, half)), weight, weight],
        pl.BlockSpec((rows, wide), lambda j, *_: (0, j)),
        jax.ShapeDtypeStruct((rows, DIN), bf16),
        [],
        4 * rows * half * DIN,
        4 * DIN * half,
        "gate_proj",
    )(scal, n_own, n_oth, wz_own, wz_oth)


def grad_gated_kernel(scal, e, w_own, w_oth, out):
    out[0] = nt(e[...], w_own[...]).astype(bf16)
    out[1] = nt(e[...], w_oth[...]).astype(bf16)


def grad_gated(scal, e, wo_own, wo_oth):
    rows, d = e.shape
    half = wo_own.shape[0]
    weight = pl.BlockSpec((GROUP, d), lambda j, *_: (j, 0))
    return call(
        grad_gated_kernel,
        (half // GROUP,),
        [const_spec((rows, d)), weight, weight],
        pl.BlockSpec((2, rows, GROUP), lambda j, *_: (0, 0, j)),
        jax.ShapeDtypeStruct((2, rows, half), bf16),
        [],
        4 * rows * half * d,
        4 * d * half,
        "grad_gated",
    )(scal, e, wo_own, wo_oth)


def out_proj_kernel(scal, a, w_own, w_oth, tok, out):
    total = tok[...].astype(f32) + nn(a[0], w_own[...]) + nn(a[1], w_oth[...])
    out[...] = total.astype(bf16)


def out_proj(scal, gated, wo_own, wo_oth, tok):
    rows, d = tok.shape
    half = wo_own.shape[0]
    wide = 2 * GROUP
    weight = pl.BlockSpec((half, wide), lambda j, *_: (0, j))
    cols = pl.BlockSpec((rows, wide), lambda j, *_: (0, j))
    return call(
        out_proj_kernel,
        (d // wide,),
        [const_spec(gated.shape), weight, weight, cols],
        cols,
        jax.ShapeDtypeStruct((rows, d), bf16),
        [],
        4 * rows * half * d,
        4 * d * half,
        "out_proj",
    )(scal, gated, wo_own, wo_oth, tok)


def input_back_kernel(
    scal, ez, eu, wz_own, wz_oth, wu_own, wu_oth, tok, halo, up, gain,
    grad_out, edge_out, gain_out,
    acc,
):
    step = pl.program_id(0)
    per = pl.num_programs(0) // 2
    half = acc.shape[1] // 2
    side = jnp.where(step < per, scal[0], 1 - scal[0])
    place = pl.ds(pl.multiple_of(side * half + lax.rem(step, per) * GROUP, GROUP), GROUP)

    def fill(wz, wu):
        part = nn(eu[...], wu[...])
        acc[0:HALO, place] = part[0:HALO]
        acc[HALO:, place] = part[HALO:] + nn(ez[...], wz[...])

    @pl.when(step < per)
    def _():
        fill(wz_own, wu_own)

    @pl.when(step >= per)
    def _():
        fill(wz_oth, wu_oth)

    def norm_back(x, rows):
        rs = lax.rsqrt(jnp.mean(x * x, axis=-1, keepdims=True) + EPS)
        unit = x * rs
        en = acc[rows, :]
        scaled = en * gain[...]
        gain_out[0:1, :] += jnp.sum(en * unit, axis=0, keepdims=True)
        return rs * (scaled - unit * jnp.mean(scaled * unit, axis=-1, keepdims=True))

    @pl.when(step == 2 * per - 1)
    def _():
        gain_out[...] = jnp.zeros_like(gain_out)
        edge_out[...] = norm_back(halo[...].astype(f32), pl.ds(0, HALO))

        def body(i, carry):
            rows = pl.ds(pl.multiple_of(i * 64, 64), 64)
            ext_rows = pl.ds(pl.multiple_of(i * 64 + HALO, 16), 64)
            grad_out[rows, :] = up[rows, :].astype(f32) + norm_back(
                tok[rows, :].astype(f32), ext_rows
            )
            return carry

        lax.fori_loop(0, tok.shape[0] // 64, body, 0)


def input_back(scal, ez, eu, wz_own, wz_oth, wu_own, wu_oth, tok, halo, up, gain):
    rows, d = tok.shape
    ext = rows + HALO
    half = wz_own.shape[1]
    per = half // GROUP

    def own(depth):
        return pl.BlockSpec((depth, GROUP), lambda j, *_: (0, jnp.minimum(j, per - 1)))

    def oth(depth):
        return pl.BlockSpec((depth, GROUP), lambda j, *_: (0, jnp.maximum(j - per, 0)))

    zd = wz_own.shape[0]
    ud = wu_own.shape[0]
    return call(
        input_back_kernel,
        (2 * per,),
        [
            const_spec(ez.shape),
            const_spec(eu.shape),
            own(zd),
            oth(zd),
            own(ud),
            oth(ud),
            const_spec((rows, d)),
            const_spec((HALO, d)),
            const_spec((rows, d)),
            const_spec((1, d)),
        ],
        [const_spec((rows, d)), const_spec((HALO, d)), const_spec((8, d))],
        [
            jax.ShapeDtypeStruct((rows, d), f32),
            jax.ShapeDtypeStruct((HALO, d), f32),
            jax.ShapeDtypeStruct((8, d), f32),
        ],
        [pltpu.VMEM((ext, d), f32)],
        2 * ext * d * (zd + ud),
        2 * d * (zd + ud) + 8 * rows * d,
        "input_back",
    )(scal, ez, eu, wz_own, wz_oth, wu_own, wu_oth, tok, halo, up, gain)


BLOCKS = 16


def outer_kernel(spans, keys, offset, has_rates, scal, l1, l2, r1, r2, *rest):
    if has_rates:
        e1, e2 = rest[:2]
        rest = rest[2:]
    step = pl.program_id(0)
    rows = l1.shape[1]
    total = rest[0].shape[1]
    count = rows // total
    tail = r1.shape[0] - l1.shape[0] if offset else 0
    acc = tn(l1[...], r1[tail:, :]) + tn(l2[...], r2[tail:, :])
    low = acc.astype(bf16)
    for i, (span, key) in enumerate(zip(spans, keys)):
        keep, send = rest[2 * i], rest[2 * i + 1]
        for t in range(count):
            place = (step * count + t) ^ scal[key]
            part = low[t * total : (t + 1) * total, span]

            @pl.when(place < BLOCKS // 2)
            def _():
                keep[place] = part

            @pl.when(place >= BLOCKS // 2)
            def _():
                send[place - BLOCKS // 2] = part

    if has_rates:
        @pl.when(step == 0)
        def _():
            rest[-1][...] = (tn(e1[...], r1[...]) + tn(e2[...], r2[...]))[:H]


def outer(scal, l1, l2, r1, r2, width, rows, step_rows, spans, keys, rates, name):
    toks = l1.shape[0]
    ext = r1.shape[0]
    cols = r1.shape[1]
    specs = [
        pl.BlockSpec((toks, step_rows), lambda j, *_: (0, j)),
        pl.BlockSpec((toks, step_rows), lambda j, *_: (0, j)),
        const_spec((ext, cols)),
        const_spec((ext, cols)),
    ]
    args = [l1, l2, r1, r2]
    if rates:
        spec = pl.BlockSpec((toks, LANE), lambda j, *_: (0, CONV // LANE))
        specs += [spec, spec]
        args += [l1, l2]
    outs = []
    for span in spans:
        shape = (BLOCKS // 2, rows, span.stop - span.start)
        outs += [shape, shape]
    shapes = [jax.ShapeDtypeStruct(o, bf16) for o in outs]
    if rates:
        outs.append((H, cols))
        shapes.append(jax.ShapeDtypeStruct((H, cols), f32))

    def kernel(*refs):
        outer_kernel(spans, keys, ext != toks, rates, *refs)

    return call(
        kernel,
        (width // step_rows,),
        specs,
        [const_spec(o) for o in outs],
        shapes,
        [],
        4 * toks * width * cols,
        4 * toks * width,
        name,
    )(scal, *args)


def finish_kernel(key, scal, near, far, *rest):
    out = rest[-1]
    place = pl.program_id(0) ^ scal[key]

    @pl.when(place < BLOCKS // 2)
    def _():
        out[...] = near[0].astype(f32)

    @pl.when(place >= BLOCKS // 2)
    def _():
        out[...] = far[0].astype(f32)


def finish(scal, near, far, key, height, name):
    half, rows, cols = near.shape

    def near_map(j, s):
        return (jnp.minimum(j ^ s[key], half - 1), 0, 0)

    def far_map(j, s):
        return (jnp.maximum((j ^ s[key]) - half, 0), 0, 0)

    def kernel(*refs):
        finish_kernel(key, *refs)

    return call(
        kernel,
        (BLOCKS,),
        [pl.BlockSpec((1, rows, cols), near_map), pl.BlockSpec((1, rows, cols), far_map)],
        pl.BlockSpec((rows, cols), lambda j, *_: (j, 0)),
        jax.ShapeDtypeStruct((height, cols), f32),
        [],
        0,
        6 * BLOCKS * rows * cols,
        name,
    )(scal, near, far)


def finish_conv_kernel(spans, keys, scal, rates, *rest):
    streams = rest[: 2 * len(spans)]
    out, buf, sems = rest[2 * len(spans) + 1 :]
    half, rows, _ = streams[0].shape
    last = pltpu.make_async_copy(
        rates, out.at[pl.ds(DIN + CONV, H), :], sems.at[BLOCKS]
    )
    last.start()
    copies = [last]
    for t in range(BLOCKS):
        for i, (span, key) in enumerate(zip(spans, keys)):
            near, far = streams[2 * i], streams[2 * i + 1]
            place = t ^ scal[key]
            dst = slice(t * rows, (t + 1) * rows)

            @pl.when(place < half)
            def _():
                buf[dst, span] = near[place].astype(f32)

            @pl.when(place >= half)
            def _():
                buf[dst, span] = far[place - half].astype(f32)

        copy = pltpu.make_async_copy(
            buf.at[pl.ds(t * rows, rows), :],
            out.at[pl.ds(DIN + t * rows, rows), :],
            sems.at[t],
        )
        copy.start()
        copies.append(copy)
    for copy in copies:
        copy.wait()


def finish_conv(scal, streams, spans, keys, rates, target):
    def kernel(*refs):
        finish_conv_kernel(spans, keys, *refs)

    count = len(streams)
    return pl.pallas_call(
        kernel,
        grid_spec=pltpu.PrefetchScalarGridSpec(
            num_scalar_prefetch=1,
            grid=(1,),
            in_specs=[const_spec(rates.shape)]
            + [const_spec(s.shape) for s in streams]
            + [pl.BlockSpec(memory_space=pl.ANY)],
            out_specs=pl.BlockSpec(memory_space=pl.ANY),
            scratch_shapes=[
                pltpu.VMEM((CONV, target.shape[1]), f32),
                pltpu.SemaphoreType.DMA((BLOCKS + 1,)),
            ],
        ),
        out_shape=jax.ShapeDtypeStruct(target.shape, f32),
        input_output_aliases={2 + count: 0},
        compiler_params=params(1),
        cost_estimate=pl.CostEstimate(
            flops=0, bytes_accessed=6 * CONV * target.shape[1], transcendentals=0
        ),
        name="finish_conv",
    )(scal, rates, *streams, target)


def swap(x):
    return lax.ppermute(x, "fsdp", [(0, 1), (1, 0)])


def shifted(x, by):
    length = lax.axis_size("tm")
    return lax.ppermute(x, "tm", [(i, (i + by) % length) for i in range(length)])


def bits_of(axis):
    return [(axis, 1 << b) for b in range((lax.axis_size(axis) - 1).bit_length())]


def across(x, axis, bit):
    return lax.ppermute(x, axis, [(i, i ^ bit) for i in range(lax.axis_size(axis))])


def orders():
    rep = bits_of("rep")
    tm = bits_of("tm")[::-1]
    cut = len(rep) // 2
    depth = BLOCKS.bit_length() - 1
    found = []
    for lead in (rep, rep[cut:] + rep[:cut]):
        every = lead + tm
        found.append((every[:depth], every[depth:]))
    return found


def code_of(order):
    place = 0
    for axis, bit in order[0]:
        place = 2 * place + (lax.axis_index(axis) // bit) % 2
    return place


def reduce_blocks(keep, send, order):
    first, extra = order
    for axis, bit in first[:-2]:
        got = across(send, axis, bit)
        n = keep.shape[0] // 2
        total = keep.astype(f32) + got.astype(f32)
        last = (axis, bit) == first[-3]
        low = total.astype(bf16)
        keep, send = (low, None) if last else (low[:n], low[n:])
    axis, high = first[-2]
    step = first[-1][1]
    total = keep[0:1].astype(f32)
    for k in range(1, 4):
        mask = (high if k & 2 else 0) ^ (step if k & 1 else 0)
        total = total + across(keep[k : k + 1], axis, mask).astype(f32)
    piece = total.astype(bf16)
    for axis_, bit in extra:
        piece = (piece.astype(f32) + across(piece, axis_, bit).astype(f32)).astype(bf16)
    return piece


def spread_blocks(piece, order):
    first = order[0]
    axis, high = first[-2]
    step = first[-1][1]
    parts = [piece]
    for k in range(1, 4):
        mask = (high if k & 2 else 0) ^ (step if k & 1 else 0)
        parts.append(across(piece, axis, mask))
    near = jnp.concatenate(parts, axis=0)
    middle = first[1:-2]
    for axis_, bit in reversed(middle):
        near = jnp.concatenate([near, across(near, axis_, bit)], axis=0)
    return near, across(near, *first[0])


def body(
    tokens, in_weight, out_weight, norm_gain, conv_weight, conv_bias, dt_bias, a_log,
    d_skip, gate_gain, lengths, starts, cotangent,
):
    core = lax.axis_index("fsdp")
    tm = lax.axis_index("tm")
    tm_size = lax.axis_size("tm")
    tok = tokens[0]
    upstream = cotangent[0]
    tok_count, d = tok.shape
    half_d = in_weight.shape[0]
    half_in = out_weight.shape[0]
    half_conv = conv_bias.shape[0]
    half_heads = dt_bias.shape[0]
    order_a, order_b = orders()

    lo = starts[0] - tm * tok_count
    scal = jnp.stack(
        [core, lo, lo + lengths[0], code_of(order_a), code_of(order_b)]
    ).astype(jnp.int32)

    def fill(v):
        return [v, jnp.zeros((half_conv - v.shape[0],), f32)]

    pack = jnp.concatenate(
        [conv_weight.reshape(-1), conv_bias]
        + fill(gate_gain)
        + fill(norm_gain)
        + [dt_bias, a_log, d_skip, jnp.zeros((half_conv - 3 * half_heads,), f32)]
    )
    pack = pack.reshape(8, half_conv).astype(bf16)
    pack_oth = swap(pack)
    halo = shifted(tok[tok_count - HALO :], 1)
    w_t = in_weight.T
    wu_own = jnp.pad(w_t[DIN:], ((0, GROUP - H), (0, 0))).astype(bf16)
    wu_oth = swap(wu_own)
    wz_own = w_t[:DIN].astype(bf16)
    wz_oth = swap(wz_own)
    wo_own = out_weight.astype(bf16)
    wo_oth = swap(wo_own)
    up_oth = swap(upstream)

    taps, vecs, heads, gain = pack_vectors(scal, pack, pack_oth, d)
    n_own, n_oth, u, act, dact, dt, sg, cum, cumt, st = front(
        scal, tok, halo, gain, wu_own, wu_oth, taps, heads
    )
    n_got = swap(n_oth)
    cumt = cumt[:H].reshape(H // 4, 4, tok_count)
    total = jnp.exp(jnp.repeat(cum[tok_count - 1, :H], P_SIZE))[None]

    def chain(local, by, first):
        pieces = []
        for part in range(2):
            cols = slice(part * (DIN // 2), (part + 1) * (DIN // 2))
            send = local[:, cols].astype(bf16)
            got = None
            for hop in range(tm_size - 1):
                got = shifted(send, by)
                got = jnp.where(tm == first, jnp.zeros_like(got), got)
                if hop < tm_size - 2:
                    send = (local[:, cols] + total[:, cols] * got.astype(f32)).astype(bf16)
            pieces.append(got)
        return jnp.concatenate(pieces, axis=1)

    s_in = chain(st, 1, 0)
    z = gate_proj(scal, n_own, n_oth, wz_own, wz_oth)
    eg = grad_gated(scal, upstream, wo_own, wo_oth)
    yloc, s0 = intra(scal, act, dt, cum, cumt)
    gated, ey, ez, r_loc, r_dev, dc_dev, g_loc, gs = gate(
        scal, yloc, act, z, eg, cum, s_in, vecs
    )

    gated_got = swap(gated[1])
    ez_got = swap(ez)
    g_in = chain(g_loc, -1, tm_size - 1)
    full = [slice(0, d)]
    a_keep, a_send = outer(
        scal, gated[0], gated_got, upstream, up_oth,
        half_in, half_in // BLOCKS, GROUP, full, [3], False, "grad_out",
    )
    half_span = [slice(0, half_d)]
    b_keep, b_send = outer(
        scal, ez, ez_got, n_own, n_got,
        DIN, DIN // BLOCKS, 2 * GROUP, half_span, [4], False, "grad_z",
    )
    a_piece = reduce_blocks(a_keep, a_send, order_a)
    b_piece = reduce_blocks(b_keep, b_send, order_b)
    a_near, a_far = spread_blocks(a_piece, order_a)
    b_near, b_far = spread_blocks(b_piece, order_b)
    output = out_proj(scal, gated, wo_own, wo_oth, tok)
    dxt, db_loc, dc_loc, r2, cq = back(scal, act, dt, cum, cumt, ey, s0)
    eu, gconv, ghead = tail(
        scal, act, dact, u, ey, dxt, taps, dt, sg, cum, g_in, s_in, vecs, heads,
        (db_loc, dc_loc, dc_dev, r_loc, r_dev, r2, cq),
    )
    eu_got = swap(eu)
    spans = [slice(0, half_d // 2), slice(half_d // 2, half_d)]
    c1_keep, c1_send, c2_keep, c2_send, g_rates = outer(
        scal, eu, eu_got, n_own, n_got,
        CONV, CONV // BLOCKS, CONV // 2, spans, [3, 4], True, "grad_u",
    )
    c1_piece = reduce_blocks(c1_keep, c1_send, order_a)
    c2_piece = reduce_blocks(c2_keep, c2_send, order_b)
    c1_near, c1_far = spread_blocks(c1_piece, order_a)
    c2_near, c2_far = spread_blocks(c2_piece, order_b)

    grad_in, edge, ggain = input_back(
        scal, ez, eu, wz_own, wz_oth, wu_own, wu_oth, tok, halo, upstream, gain
    )
    edge = shifted(edge, -1)
    edge = jnp.where(tm == tm_size - 1, jnp.zeros_like(edge), edge)
    input_grad = grad_in.at[tok_count - HALO :].add(edge)

    grad_skip = jnp.sum(gs[1].reshape(H, P_SIZE), axis=1)

    def side(v, half):
        return jnp.stack([v[:half], v[half : 2 * half]])

    def slot(v, half):
        return jnp.pad(side(v, half), ((0, 0), (0, half_conv - half)))[:, None]

    head_grads = jnp.stack([ghead[0, :H], ghead[1, :H], grad_skip])
    head_sides = jnp.stack(
        [head_grads[:, :half_heads].reshape(-1), head_grads[:, half_heads:].reshape(-1)]
    )
    packed = jnp.concatenate(
        [
            gconv[:5].reshape(5, 2, half_conv).transpose(1, 0, 2),
            slot(gs[0], half_in),
            slot(ggain[0], half_d),
            jnp.pad(head_sides, ((0, 0), (0, half_conv - 3 * half_heads)))[:, None],
        ],
        axis=1,
    )
    own = lax.dynamic_index_in_dim(packed, core, 0, keepdims=False)
    small = own + swap(lax.dynamic_index_in_dim(packed, 1 - core, 0, keepdims=False))
    small = jnp.concatenate([small, g_rates.reshape(8, -1)], axis=1)
    for axis, bit in bits_of("rep") + bits_of("tm"):
        small = small + across(small, axis, bit)
    rates = small[:, half_conv:].reshape(H, half_d)

    grad_out_w = finish(scal, a_near, a_far, 3, half_in, "finish_out")
    grad_in_t = finish(scal, b_near, b_far, 4, DIN + CONV + H, "finish_z")
    grad_in_t = finish_conv(
        scal, [c1_near, c1_far, c2_near, c2_far], spans, [3, 4], rates, grad_in_t
    )
    hs = half_heads
    return (
        output[None],
        input_grad[None],
        grad_in_t.T,
        grad_out_w,
        small[6, :half_d],
        small[:4, :half_conv],
        small[4, :half_conv],
        small[7, :hs],
        small[7, hs : 2 * hs],
        small[7, 2 * hs : 3 * hs],
        small[5, :half_in],
    )


def solution(mesh):
    return jax.shard_map(
        body,
        mesh=mesh,
        in_specs=(
            P(("rep", "fsdp"), "tm", None),
            P("fsdp", None),
            P("fsdp", None),
            P("fsdp"),
            P(None, "fsdp"),
            P("fsdp"),
            P("fsdp"),
            P("fsdp"),
            P("fsdp"),
            P("fsdp"),
            P(("rep", "fsdp")),
            P(("rep", "fsdp")),
            P(("rep", "fsdp"), "tm", None),
        ),
        out_specs=(
            P(("rep", "fsdp"), "tm", None),
            P(("rep", "fsdp"), "tm", None),
            P("fsdp", None),
            P("fsdp", None),
            P("fsdp"),
            P(None, "fsdp"),
            P("fsdp"),
            P("fsdp"),
            P("fsdp"),
            P("fsdp"),
            P("fsdp"),
        ),
        check_vma=False,
    )
```

```python
import jax
import jax.numpy as jnp
from jax import lax
from jax.experimental import pallas as pl
from jax.experimental.pallas import tpu as pltpu
from jax.sharding import PartitionSpec as P

H = 32
P_SIZE = 64
N = 128
K = 4
DIN = 2048
CONV = 2304
EPS = 1e-05
QB = 128
HALO = 16
GROUP = 256
LANE = 128

bf16 = jnp.bfloat16
f32 = jnp.float32
HIGHEST = lax.Precision.HIGHEST

VMEM_LIMIT = 60 * 1024 * 1024
COST = 1000
CHUNKS = 4
BLOCKS = 16


def nn(a, b):
    return lax.dot_general(a, b, (((1,), (0,)), ((), ())), preferred_element_type=f32)


def nt(a, b):
    return lax.dot_general(a, b, (((1,), (1,)), ((), ())), preferred_element_type=f32)


def exact_nn(a, b):
    return lax.dot_general(
        a, b, (((1,), (0,)), ((), ())), precision=HIGHEST, preferred_element_type=f32
    )


def iota(shape, dim):
    return lax.broadcasted_iota(jnp.int32, shape, dim)


def tn(a, b):
    return lax.dot_general(a, b, (((0,), (0,)), ((), ())), preferred_element_type=f32)


def sigmoid(v):
    return 0.5 + 0.5 * jnp.tanh(0.5 * v)


def split_two(v):
    hi = v.astype(bf16)
    lo = (v - hi.astype(f32)).astype(bf16)
    return hi, lo


def const_spec(shape):
    return pl.BlockSpec(shape, lambda *_: tuple(0 for _ in shape))


def params(steps=1):
    return pltpu.CompilerParams(
        dimension_semantics=("arbitrary",) * steps, vmem_limit_bytes=VMEM_LIMIT
    )


def call(kernel, grid, in_specs, out_specs, out_shape, scratch, flops, nbytes, name):
    return pl.pallas_call(
        kernel,
        grid_spec=pltpu.PrefetchScalarGridSpec(
            num_scalar_prefetch=1,
            grid=grid,
            in_specs=in_specs,
            out_specs=out_specs,
            scratch_shapes=scratch,
        ),
        out_shape=out_shape,
        compiler_params=params(len(grid)),
        cost_estimate=pl.CostEstimate(
            flops=flops // COST, bytes_accessed=nbytes // COST, transcendentals=0
        ),
        name=name,
    )


def spread(cols, pair):
    left = cols[:, 2 * pair : 2 * pair + 1]
    right = cols[:, 2 * pair + 1 : 2 * pair + 2]
    lanes = iota((cols.shape[0], LANE), 1)
    return jnp.where(lanes < P_SIZE, left, right)


def spread_group(cols):
    return jnp.concatenate([spread(cols, 0), spread(cols, 1)], axis=1)


def block_diag(pair_low):
    lanes = iota(pair_low.shape, 1)
    zero = jnp.zeros_like(pair_low)
    return jnp.concatenate(
        [jnp.where(lanes < P_SIZE, pair_low, zero), jnp.where(lanes < P_SIZE, zero, pair_low)],
        axis=0,
    )


def head_columns(cols, group):
    return pltpu.roll(cols, lax.rem(LANE - 4 * group, LANE), 1)


def head_picker(lanes_in, first_head):
    rows = iota((lanes_in, LANE), 0) // P_SIZE + first_head
    return (rows == iota((lanes_in, LANE), 1)).astype(bf16)


def pack_kernel(scal, own, oth, taps, vecs, heads, gain):
    core = scal[0]
    span = own.shape[1]
    half_in = vecs.shape[1] // 2
    half_d = gain.shape[1] // 2
    taps[...] = jnp.zeros_like(taps)
    vecs[...] = jnp.zeros_like(vecs)
    sides = []
    for src, place in ((own, core), (oth, 1 - core)):
        block = src[...].astype(f32)

        def at(width):
            return pl.ds(pl.multiple_of(place * width, LANE), width)

        taps[0:5, at(span)] = block[0:5]
        vecs[0:1, at(half_in)] = block[5:6, :half_in]
        gain[0:1, at(half_d)] = block[6:7, :half_d]
        sides.append(jnp.broadcast_to(block[7:8, :LANE], (8, LANE)))
    width = H // 2
    lanes = iota((8, LANE), 1)
    rows = []
    for i in range(3):
        first = jnp.where(core == 0, sides[0], sides[1])
        second = jnp.where(core == 0, sides[1], sides[0])
        low = pltpu.roll(first, (LANE - i * width) % LANE, 1)
        high = pltpu.roll(second, (LANE - i * width + width) % LANE, 1)
        rows.append(jnp.where(lanes < width, low, jnp.where(lanes < H, high, 0.0)))
    rate = jnp.where(lanes < H, -jnp.exp(rows[1]), 0.0)
    pick = iota((8, LANE), 0)
    heads[...] = jnp.where(pick == 0, rows[0], jnp.where(pick == 1, rate, 0.0))
    skip = rows[2].astype(bf16)
    expand = (iota((LANE, DIN), 1) // P_SIZE == iota((LANE, DIN), 0)).astype(bf16)
    vecs[1:2, :] = nn(skip, expand)[0:1]


def pack_vectors(scal, own, oth, d):
    return call(
        pack_kernel,
        (1,),
        [const_spec(own.shape), const_spec(oth.shape)],
        [const_spec((8, CONV)), const_spec((8, DIN)), const_spec((8, LANE)), const_spec((1, d))],
        [
            jax.ShapeDtypeStruct((8, CONV), f32),
            jax.ShapeDtypeStruct((8, DIN), f32),
            jax.ShapeDtypeStruct((8, LANE), f32),
            jax.ShapeDtypeStruct((1, d), f32),
        ],
        [],
        10**6,
        10**5,
        "vectors",
    )(scal, own, oth)


def front_kernel(
    scal, tok, halo, gain, w_own, w_oth, r_own, r_oth, taps, heads,
    n_own, n_oth, u_out, act_out, dact_out, dt_out, sg_out, cum_out, cumt_out, st_out,
    ubuf, bt, ecl,
):
    step = pl.program_id(0)
    tok_count = tok.shape[0]
    half = w_own.shape[1]
    own = pl.ds(pl.multiple_of(scal[0] * half, LANE), half)
    oth = pl.ds(pl.multiple_of((1 - scal[0]) * half, LANE), half)
    lo = scal[1]
    hi = scal[2]

    @pl.when(step == 0)
    def _():
        def rows_of(src, base, dst, count):
            x = src[pl.ds(base, count), :].astype(f32)
            rs = lax.rsqrt(jnp.mean(x * x, axis=-1, keepdims=True) + EPS)
            for out, cols in ((n_own, own), (n_oth, oth)):
                part = src[pl.ds(base, count), cols].astype(f32)
                out[pl.ds(dst, count), :] = (part * rs * gain[:, cols]).astype(bf16)

        rows_of(halo, 0, 0, HALO)

        def body(i, carry):
            base = pl.multiple_of(i * 64, 64)
            rows_of(tok, base, pl.multiple_of(base + HALO, 16), 64)
            return carry

        lax.fori_loop(0, tok_count // 64, body, 0)
        r = nt(n_own[HALO:, :], r_own[...]) + nt(n_oth[HALO:, :], r_oth[...])
        pre = r.astype(bf16).astype(f32) + heads[0:1, :]
        pos = iota((tok_count, LANE), 0)
        keep = (pos >= lo) & (pos < hi) & (iota((tok_count, LANE), 1) < H)
        soft = jnp.maximum(pre, 0.0) + jnp.log1p(jnp.exp(-jnp.abs(pre)))
        dt = jnp.where(keep, soft, 0.0)
        dt_out[...] = dt
        sg_out[...] = jnp.where(keep, 1.0 / (1.0 + jnp.exp(-pre)), 0.0)
        da = dt * heads[1:2, :]
        tri = (iota((QB, QB), 0) >= iota((QB, QB), 1)).astype(f32)
        carry = jnp.zeros((1, LANE), f32)
        for q in range(tok_count // QB):
            cum = exact_nn(tri, da[q * QB : (q + 1) * QB]) + carry
            cum_out[q * QB : (q + 1) * QB, :] = cum
            cumt_out[:, q * QB : (q + 1) * QB] = cum.T
            carry = cum[QB - 1 : QB]
        ecl[...] = jnp.exp(carry - cum_out[...])

    u = nt(n_own[...], w_own[...]) + nt(n_oth[...], w_oth[...])
    pos = iota(u.shape, 0) - HALO
    u = jnp.where((pos >= lo) & (pos < hi), u, 0.0).astype(bf16)
    u_out[...] = u
    ubuf[...] = u.astype(f32)
    c = taps[4:5, :] + sum(
        taps[k : k + 1, :] * ubuf[HALO - 3 + k : HALO - 3 + k + tok_count, :] for k in range(K)
    )
    s = sigmoid(c)
    act = (c * s).astype(bf16)
    act_out[...] = act
    dact_out[...] = (s * (1.0 + c * (1.0 - s))).astype(bf16)

    @pl.when(step == 0)
    def _():
        bt[...] = act[:, :N].astype(f32).T.astype(bf16)

    @pl.when(step > 0)
    def _():
        group = step - 1
        dtg = spread_group(head_columns(dt_out[...], group))
        ecg = spread_group(head_columns(ecl[...], group))
        xt = (act.astype(f32) * dtg).astype(bf16)
        xw = (xt.astype(f32) * ecg).astype(bf16)
        st_out[...] = nn(bt[...], xw)


def front(scal, tok, halo, gain, wu_own, wu_oth, taps, heads):
    tok_count, d = tok.shape
    half = wu_own.shape[1]
    ext = tok_count + HALO
    groups = CONV // GROUP
    first = groups - 1

    def col(j, *_):
        return (0, (j + first) % groups)

    weight = pl.BlockSpec((GROUP, half), lambda j, *_: ((j + first) % groups, 0))
    narrow = pl.BlockSpec((LANE, half), lambda j, *_: (CONV // LANE, 0))
    return call(
        front_kernel,
        (groups,),
        [
            const_spec((tok_count, d)),
            const_spec((HALO, d)),
            const_spec((1, d)),
            weight,
            weight,
            narrow,
            narrow,
            pl.BlockSpec((8, GROUP), col),
            const_spec((8, LANE)),
        ],
        [
            const_spec((ext, half)),
            const_spec((ext, half)),
            pl.BlockSpec((ext, GROUP), col),
            pl.BlockSpec((tok_count, GROUP), col),
            pl.BlockSpec((tok_count, GROUP), col),
            const_spec((tok_count, LANE)),
            const_spec((tok_count, LANE)),
            const_spec((tok_count, LANE)),
            const_spec((LANE, tok_count)),
            pl.BlockSpec((N, GROUP), lambda j, *_: (0, jnp.maximum(j - 1, 0))),
        ],
        [
            jax.ShapeDtypeStruct((ext, half), bf16),
            jax.ShapeDtypeStruct((ext, half), bf16),
            jax.ShapeDtypeStruct((ext, CONV), bf16),
            jax.ShapeDtypeStruct((tok_count, CONV), bf16),
            jax.ShapeDtypeStruct((tok_count, CONV), bf16),
            jax.ShapeDtypeStruct((tok_count, LANE), f32),
            jax.ShapeDtypeStruct((tok_count, LANE), f32),
            jax.ShapeDtypeStruct((tok_count, LANE), f32),
            jax.ShapeDtypeStruct((LANE, tok_count), f32),
            jax.ShapeDtypeStruct((N, DIN), f32),
        ],
        [
            pltpu.VMEM((ext, GROUP), f32),
            pltpu.VMEM((N, tok_count), bf16),
            pltpu.VMEM((tok_count, LANE), f32),
        ],
        2 * ext * d * (CONV + LANE),
        2 * (ext * d + d * CONV + 3 * ext * CONV),
        "front",
    )(scal, tok, halo, gain, wu_own, wu_oth, wu_own, wu_oth, taps, heads)


def intra_kernel(scal, x, bc, dt, cum, cumt, y_out, s0_out, scores, bt):
    group = pl.program_id(0)
    blocks = x.shape[0] // QB

    @pl.when(group == 0)
    def _():
        lower = iota((QB, QB), 0) >= iota((QB, QB), 1)
        bt[...] = bc[:, :N].astype(f32).T.astype(bf16)
        for q in range(blocks):
            rows = slice(q * QB, (q + 1) * QB)
            scores[q] = jnp.where(lower, nt(bc[rows, N:], bc[rows, :N]), 0.0)

    dtr = head_columns(dt[...], group)
    cumr = head_columns(cum[...], group)
    carry = jnp.zeros((N, GROUP), f32)
    for q in range(blocks):
        rows = slice(q * QB, (q + 1) * QB)
        cq = cumr[rows]
        end = cq[QB - 1 : QB]
        start = cumr[q * QB - 1 : q * QB] if q else jnp.zeros((1, LANE), f32)
        xt = (x[rows, :].astype(f32) * spread_group(dtr[rows])).astype(bf16)
        low_carry = carry.astype(bf16)
        s0_out[q] = low_carry
        ys = []
        for pair in range(2):
            mats = []
            for e in range(2):
                h = 2 * pair + e
                row = cumt[0, h : h + 1, rows]
                decay = jnp.exp(jnp.minimum(cq[:, h : h + 1] - row, 0.0))
                mats.append((decay * scores[q]).astype(bf16))
            ys.append(
                nn(
                    jnp.concatenate(mats, axis=1),
                    block_diag(xt[:, pair * LANE : (pair + 1) * LANE]),
                )
            )
        y = jnp.concatenate(ys, axis=1)
        if q:
            y = y + jnp.exp(spread_group(cq - start)) * nn(bc[rows, N:], low_carry)
        y_out[rows, :] = y
        if q < blocks - 1:
            xw = (xt.astype(f32) * jnp.exp(spread_group(end - cq))).astype(bf16)
            fresh = nn(bt[:, rows], xw)
            carry = fresh if q == 0 else fresh + carry * jnp.exp(spread_group(end - start))


def intra(scal, act, dt, cum, cumt):
    tok_count = act.shape[0]
    blocks = tok_count // QB
    groups = DIN // GROUP
    return call(
        intra_kernel,
        (groups,),
        [
            pl.BlockSpec((tok_count, GROUP), lambda j, *_: (0, j)),
            pl.BlockSpec((tok_count, GROUP), lambda j, *_: (0, groups)),
            const_spec((tok_count, LANE)),
            const_spec((tok_count, LANE)),
            pl.BlockSpec((1, 4, tok_count), lambda j, *_: (j, 0, 0)),
        ],
        [
            pl.BlockSpec((tok_count, GROUP), lambda j, *_: (0, j)),
            pl.BlockSpec((blocks, N, GROUP), lambda j, *_: (0, 0, j)),
        ],
        [
            jax.ShapeDtypeStruct((tok_count, DIN), f32),
            jax.ShapeDtypeStruct((blocks, N, DIN), bf16),
        ],
        [pltpu.VMEM((blocks, QB, QB), f32), pltpu.VMEM((N, tok_count), bf16)],
        2 * tok_count * DIN * 3 * N,
        8 * tok_count * DIN,
        "intra",
    )(scal, act, act, dt, cum, cumt)


def gate_kernel(
    scal, yloc, act, z, eg, cum, s_in, vecs,
    own_out, oth_out, ey_out, ez_out, r_loc, r_dev, dc_out, g_out, gs_out,
    pick, vbuf, ytbuf, ydbuf,
):
    step = pl.program_id(0)
    rows = yloc.shape[0]
    groups = DIN // GROUP
    per = groups // 2

    @pl.when(step == 0)
    def _():
        pick[...] = head_picker(DIN, 0)
        g_out[...] = jnp.zeros_like(g_out)
        gs_out[...] = jnp.zeros_like(gs_out)

    pos = iota((rows, 1), 0) + step * rows
    valid = ((pos >= scal[1]) & (pos < scal[2])).astype(f32)
    cq = cum[...]
    ecq = jnp.exp(cq)
    cmat = act[:, DIN + N :]
    ssq = jnp.zeros((rows, GROUP), f32)
    for g in range(groups):
        cols = slice(g * GROUP, (g + 1) * GROUP)
        eg_cum = jnp.concatenate([spread(ecq, 2 * g), spread(ecq, 2 * g + 1)], axis=1)
        yd = eg_cum * nn(cmat, s_in[:, cols])
        ydbuf[:, cols] = yd
        yt = yloc[:, cols] + yd + vecs[1:2, cols] * act[:, cols].astype(f32)
        ytbuf[:, cols] = yt
        zz = z[:, cols].astype(f32)
        v = yt * (zz * sigmoid(zz))
        vbuf[:, cols] = v
        ssq = ssq + v * v
    rs = lax.rsqrt(jnp.sum(ssq, axis=-1, keepdims=True) / DIN + EPS)
    mixed = jnp.zeros((rows, GROUP), f32)
    low_half = scal[0] == 0
    for i in range(per):
        local = slice(i * GROUP, (i + 1) * GROUP)
        outs = []
        for half in range(2):
            g = half * per + i
            cols = slice(g * GROUP, (g + 1) * GROUP)
            n = vbuf[:, cols] * rs
            vbuf[:, cols] = n
            gain = vecs[0:1, cols]
            outs.append((n * gain * valid).astype(bf16))
            e = eg[half ^ scal[0], :, local].astype(f32) * valid
            gs_out[0:1, cols] += jnp.sum(e * n, axis=0, keepdims=True)
            mixed = mixed + e * gain * n
        own_out[:, local] = jnp.where(low_half, outs[0], outs[1])
        oth_out[:, local] = jnp.where(low_half, outs[1], outs[0])
    m2 = jnp.sum(mixed, axis=-1, keepdims=True) / DIN
    rl = jnp.zeros((rows, LANE), f32)
    rd = jnp.zeros((rows, LANE), f32)
    dc = jnp.zeros((rows, N), f32)
    ct = cmat.astype(f32).T.astype(bf16)
    for g in range(groups):
        cols = slice(g * GROUP, (g + 1) * GROUP)
        n = vbuf[:, cols]
        side = (g // per) ^ scal[0]
        local = slice((g % per) * GROUP, (g % per + 1) * GROUP)
        e = eg[side, :, local].astype(f32) * valid
        ev = rs * (e * vecs[0:1, cols] - n * m2)
        zz = z[:, cols].astype(f32)
        sz = sigmoid(zz)
        ey = ev * (zz * sz)
        ez_out[:, cols] = (ev * ytbuf[:, cols] * (sz * (1.0 + zz * (1.0 - sz)))).astype(bf16)
        gs_out[1:2, cols] += jnp.sum(ey * act[:, cols].astype(f32), axis=0, keepdims=True)
        low = ey.astype(bf16)
        ey_out[:, cols] = low
        eyf = low.astype(f32)
        ph, pl_ = split_two(eyf * yloc[:, cols])
        rl = rl + nn(ph, pick[cols, :]) + nn(pl_, pick[cols, :])
        rd = rd + nn((eyf * ydbuf[:, cols]).astype(bf16), pick[cols, :])
        eg_cum = jnp.concatenate([spread(ecq, 2 * g), spread(ecq, 2 * g + 1)], axis=1)
        eye = (eyf * eg_cum).astype(bf16)
        g_out[:, cols] += nn(ct, eye)
        dc = dc + nt(eye, s_in[:, cols])
    r_loc[...] = rl
    r_dev[...] = rd
    dc_out[...] = dc


def gate(scal, yloc, act, z, eg, cum, s_in, vecs):
    tok_count = act.shape[0]
    rows = QB

    def rowspec(width):
        return pl.BlockSpec((rows, width), lambda j, *_: (j, 0))

    def out(width, kind):
        return jax.ShapeDtypeStruct((tok_count, width), kind)

    sides = pl.BlockSpec((2, rows, DIN // 2), lambda j, *_: (0, j, 0))

    return call(
        gate_kernel,
        (tok_count // rows,),
        [
            rowspec(DIN),
            rowspec(CONV),
            rowspec(DIN),
            sides,
            rowspec(LANE),
            const_spec((N, DIN)),
            const_spec((8, DIN)),
        ],
        [
            rowspec(DIN // 2),
            rowspec(DIN // 2),
            rowspec(DIN),
            rowspec(DIN),
            rowspec(LANE),
            rowspec(LANE),
            rowspec(LANE),
            const_spec((N, DIN)),
            const_spec((8, DIN)),
        ],
        [
            out(DIN // 2, bf16),
            out(DIN // 2, bf16),
            out(DIN, bf16),
            out(DIN, bf16),
            out(LANE, f32),
            out(LANE, f32),
            out(LANE, f32),
            jax.ShapeDtypeStruct((N, DIN), f32),
            jax.ShapeDtypeStruct((8, DIN), f32),
        ],
        [
            pltpu.VMEM((DIN, LANE), bf16),
            pltpu.VMEM((rows, DIN), f32),
            pltpu.VMEM((rows, DIN), f32),
            pltpu.VMEM((rows, DIN), f32),
        ],
        2 * tok_count * DIN * 6 * N,
        20 * tok_count * DIN,
        "gate",
    )(scal, yloc, act, z, eg, cum, s_in, vecs)


def back_kernel(
    scal, x, bc, dt, cum, cumt, ey, s0,
    dxt_out, db_out, dc_out, r2_out, cq_out,
    scores, dscores, ct,
):
    group = pl.program_id(0)
    last = pl.num_programs(0) - 1
    blocks = x.shape[0] // QB
    upper = iota((QB, QB), 0) <= iota((QB, QB), 1)

    @pl.when(group == 0)
    def _():
        ct[...] = bc[:, N:].astype(f32).T.astype(bf16)
        for q in range(blocks):
            rows = slice(q * QB, (q + 1) * QB)
            scores[q] = jnp.where(upper, nt(bc[rows, :N], bc[rows, N:]), 0.0)
        dscores[...] = jnp.zeros_like(dscores)
        db_out[...] = jnp.zeros_like(db_out)
        dc_out[...] = jnp.zeros_like(dc_out)
        r2_out[...] = jnp.zeros_like(r2_out)
        cq_out[...] = jnp.zeros_like(cq_out)

    dtr = head_columns(dt[...], group)
    cumr = head_columns(cum[...], group)
    picks = [head_picker(LANE, 4 * group + 2 * pair) for pair in range(2)]
    picks2 = [jnp.concatenate([p, p], axis=0) for p in picks]
    pick_all = head_picker(GROUP, 4 * group).astype(f32)
    carry = None
    for q in reversed(range(blocks)):
        rows = slice(q * QB, (q + 1) * QB)
        cq = cumr[rows]
        end = cq[QB - 1 : QB]
        start = cumr[q * QB - 1 : q * QB] if q else jnp.zeros((1, LANE), f32)
        xt = (x[rows, :].astype(f32) * spread_group(dtr[rows])).astype(bf16)
        eyq = ey[rows, :]
        dxs = []
        ds = jnp.zeros((QB, QB), f32)
        for pair in range(2):
            lanes = slice(pair * LANE, (pair + 1) * LANE)
            eybd = block_diag(eyq[:, lanes])
            dm = nt(xt[:, lanes], eybd)
            mats = []
            for e in range(2):
                h = 2 * pair + e
                row = cumt[0, h : h + 1, rows]
                decay = jnp.exp(jnp.minimum(row - cq[:, h : h + 1], 0.0))
                mats.append((decay * scores[q]).astype(bf16))
                ds = ds + decay * dm[:, e * QB : (e + 1) * QB]
            dxs.append(nn(jnp.concatenate(mats, axis=1), eybd))
        dscores[q] += ds
        dx = jnp.concatenate(dxs, axis=1)
        xtf = xt.astype(f32)
        eye = None
        if q:
            eye = (eyq.astype(f32) * jnp.exp(spread_group(cq - start))).astype(bf16)
            dc_out[rows, :] += nt(eye, s0[q])
        if carry is not None:
            low = carry.astype(bf16)
            ecl = jnp.exp(spread_group(end - cq))
            dst = ecl * nn(bc[rows, :N], low)
            db_out[rows, :] += nt((xtf * ecl).astype(bf16), low)
            total = jnp.exp(spread_group(end - start))
            vec = jnp.sum(xtf * dst, axis=0, keepdims=True)
            if q:
                vec = vec + total * jnp.sum(carry * s0[q].astype(f32), axis=0, keepdims=True)
            cq_out[q : q + 1, :] += exact_nn(jnp.broadcast_to(vec, (8, GROUP)), pick_all)[0:1]
            dx = dx + dst
        if q:
            fresh = nn(ct[:, rows], eye)
            carry = fresh if carry is None else fresh + total * carry
        dxt_out[rows, :] = dx.astype(bf16)
        prod = xtf * dx
        acc = jnp.zeros((QB, LANE), f32)
        for pair in range(2):
            ph, pl_ = split_two(prod[:, pair * LANE : (pair + 1) * LANE])
            acc = acc + nn(jnp.concatenate([ph, pl_], axis=1), picks2[pair])
        r2_out[rows, :] += acc

    @pl.when(group == last)
    def _():
        for q in range(blocks):
            rows = slice(q * QB, (q + 1) * QB)
            ds = jnp.where(upper, dscores[q], 0.0)
            db_out[rows, :] += nn(ds.astype(bf16), bc[rows, N:])
            dc_out[rows, :] += nn(ds.T.astype(bf16), bc[rows, :N])


def back(scal, act, dt, cum, cumt, ey, s0):
    tok_count = act.shape[0]
    blocks = tok_count // QB
    groups = DIN // GROUP
    wide = pl.BlockSpec((tok_count, GROUP), lambda j, *_: (0, j))
    small = const_spec((tok_count, LANE))
    return call(
        back_kernel,
        (groups,),
        [
            wide,
            pl.BlockSpec((tok_count, GROUP), lambda j, *_: (0, groups)),
            small,
            small,
            pl.BlockSpec((1, 4, tok_count), lambda j, *_: (j, 0, 0)),
            wide,
            pl.BlockSpec((blocks, N, GROUP), lambda j, *_: (0, 0, j)),
        ],
        [wide, small, small, small, const_spec((8, LANE))],
        [
            jax.ShapeDtypeStruct((tok_count, DIN), bf16),
            jax.ShapeDtypeStruct((tok_count, LANE), f32),
            jax.ShapeDtypeStruct((tok_count, LANE), f32),
            jax.ShapeDtypeStruct((tok_count, LANE), f32),
            jax.ShapeDtypeStruct((8, LANE), f32),
        ],
        [
            pltpu.VMEM((blocks, QB, QB), f32),
            pltpu.VMEM((blocks, QB, QB), f32),
            pltpu.VMEM((N, tok_count), bf16),
        ],
        2 * tok_count * DIN * 8 * N,
        8 * tok_count * DIN,
        "back",
    )(scal, act, act, dt, cum, cumt, ey, s0)


def tail_kernel(
    scal, act, bc, dact, u, ey, dxt, taps, dt, sg, cum, g_in, s_in, skip, heads,
    db_loc, dc_loc, dc_dev, r_loc, r_dev, r2, cq,
    *rest,
):
    chunks = rest[: CHUNKS + 1]
    gconv, ghead, ebuf, ubuf, p_acc, d_acc, db_acc, gs_acc = rest[CHUNKS + 1 :]
    eu_out = chunks[-1]
    step = pl.program_id(0)
    last = pl.num_programs(0) - 2
    tok_count = act.shape[0]
    ext = tok_count + HALO
    lo = scal[1]
    hi = scal[2]

    @pl.when(step == 0)
    def _():
        p_acc[...] = jnp.zeros_like(p_acc)
        d_acc[...] = jnp.zeros_like(d_acc)
        db_acc[...] = jnp.zeros_like(db_acc)
        gs_acc[...] = jnp.zeros_like(gs_acc)
        ebuf[...] = jnp.zeros_like(ebuf)

    bmat = bc[:, :N]

    @pl.when(step < last)
    def _():
        cumr = head_columns(cum[...], step)
        dtr = spread_group(head_columns(dt[...], step))
        xf = act[...].astype(f32)
        xtf = (xf * dtr).astype(bf16).astype(f32)
        low = g_in[...]
        end = cumr[tok_count - 1 : tok_count]
        ecl = jnp.exp(spread_group(end - cumr))
        dxd = ecl * nn(bmat, low)
        dx = dxt[...].astype(f32) + dxd
        pick = head_picker(GROUP, 4 * step)
        p_acc[...] += nn((xtf * dxd).astype(bf16), pick)
        d_acc[...] += nn((xf * dx).astype(bf16), pick)
        db_acc[...] += nt((xtf * ecl).astype(bf16), low)
        vec = jnp.sum(low.astype(f32) * s_in[...].astype(f32), axis=0, keepdims=True)
        vec = vec * jnp.exp(spread_group(end))
        gs_acc[...] += exact_nn(jnp.broadcast_to(vec, (8, GROUP)), pick.astype(f32))
        ebuf[HALO : HALO + tok_count, :] = (
            dtr * dx + skip[1:2, :] * ey[...].astype(f32)
        ) * dact[...].astype(f32)

    @pl.when(step == last)
    def _():
        ebuf[HALO : HALO + tok_count, :N] = (db_loc[...] + db_acc[...]) * dact[:, :N].astype(f32)
        ebuf[HALO : HALO + tok_count, N:] = (dc_loc[...] + dc_dev[...]) * dact[:, N:].astype(f32)

    @pl.when(step > last)
    def _():
        rate = heads[1:2, :]
        upper = (iota((QB, QB), 0) <= iota((QB, QB), 1)).astype(f32)
        strict = (iota((QB, QB), 0) > iota((QB, QB), 1)).astype(f32)
        blocks = tok_count // QB
        devs = jnp.zeros((1, LANE), f32)
        suffix = [None] * blocks
        for q in reversed(range(blocks)):
            rows = slice(q * QB, (q + 1) * QB)
            within = exact_nn(upper, r_loc[rows, :] - r2[rows, :]) + cq[q : q + 1, :]
            dev = exact_nn(upper, r_dev[rows, :]) + devs
            devs = dev[0:1]
            suffix[q] = within + dev
        before = gs_acc[0:1, :]
        glog = jnp.zeros((1, LANE), f32)
        gdt = jnp.zeros((1, LANE), f32)
        eu_out[...] = jnp.zeros_like(eu_out)
        for q in range(blocks):
            rows = slice(q * QB, (q + 1) * QB)
            pq = p_acc[rows, :]
            eda = suffix[q] + exact_nn(strict, pq) + before
            before = before + jnp.sum(pq, axis=0, keepdims=True)
            er = (d_acc[rows, :] + rate * eda) * sg[rows, :]
            gdt = gdt + jnp.sum(er, axis=0, keepdims=True)
            glog = glog + rate * jnp.sum(dt[rows, :] * eda, axis=0, keepdims=True)
            eu_out[HALO + q * QB : HALO + (q + 1) * QB, :LANE] = er.astype(bf16)
        ghead[...] = jnp.concatenate([gdt, glog, jnp.zeros((6, LANE), f32)], axis=0)

    @pl.when(step <= last)
    def _():
        ubuf[...] = u[...].astype(f32)
        ec = ebuf[HALO : HALO + tok_count, :]
        gs = [
            jnp.sum(ec * ubuf[HALO - 3 + k : HALO - 3 + k + tok_count, :], axis=0, keepdims=True)
            for k in range(K)
        ]
        gs.append(jnp.sum(ec, axis=0, keepdims=True))
        gs.append(jnp.zeros((3, ec.shape[1]), f32))
        gconv[...] = jnp.concatenate(gs, axis=0)
        eu = sum(taps[k : k + 1, :] * ebuf[3 - k : 3 - k + ext, :] for k in range(K))
        pos = iota(eu.shape, 0) - HALO
        eu = jnp.where((pos >= lo) & (pos < hi), eu, 0.0).astype(bf16)
        for c, chunk in enumerate(chunks):
            @pl.when(step // 2 == c)
            def _():
                chunk[...] = eu


def tail(scal, act, dact, u, ey, dxt, taps, dt, sg, cum, g_in, s_in, skip, heads, smalls):
    tok_count = act.shape[0]
    ext = tok_count + HALO
    groups = DIN // GROUP

    def col(j, *_):
        return (0, jnp.minimum(j, groups))

    def colx(j, *_):
        return (0, jnp.minimum(j, groups - 1))

    def chunk(c):
        return pl.BlockSpec((ext, GROUP), lambda j, *_: (0, jnp.clip(j - 2 * c, 0, 1)))

    wide = pl.BlockSpec((tok_count, GROUP), col)
    widex = pl.BlockSpec((tok_count, GROUP), colx)
    small = const_spec((tok_count, LANE))
    return call(
        tail_kernel,
        (groups + 2,),
        [
            wide,
            pl.BlockSpec((tok_count, GROUP), lambda j, *_: (0, groups)),
            wide,
            pl.BlockSpec((ext, GROUP), col),
            widex,
            widex,
            pl.BlockSpec((8, GROUP), col),
            small,
            small,
            small,
            pl.BlockSpec((N, GROUP), colx),
            pl.BlockSpec((N, GROUP), colx),
            pl.BlockSpec((8, GROUP), lambda j, *_: (0, jnp.minimum(j, groups - 1))),
            const_spec((8, LANE)),
            small,
            small,
            small,
            small,
            small,
            small,
            const_spec((8, LANE)),
        ],
        [
            *[chunk(c) for c in range(CHUNKS + 1)],
            pl.BlockSpec((8, GROUP), col),
            const_spec((8, LANE)),
        ],
        [
            *[jax.ShapeDtypeStruct((ext, 2 * GROUP), bf16)] * (CHUNKS + 1),
            jax.ShapeDtypeStruct((8, CONV), f32),
            jax.ShapeDtypeStruct((8, LANE), f32),
        ],
        [
            pltpu.VMEM((ext + HALO, GROUP), f32),
            pltpu.VMEM((ext, GROUP), f32),
            pltpu.VMEM((tok_count, LANE), f32),
            pltpu.VMEM((tok_count, LANE), f32),
            pltpu.VMEM((tok_count, LANE), f32),
            pltpu.VMEM((8, LANE), f32),
        ],
        2 * tok_count * DIN * 4 * N,
        12 * tok_count * DIN,
        "tail",
    )(
        scal, act, act, dact, u, ey, dxt, taps, dt, sg, cum, g_in, s_in, skip, heads, *smalls
    )


def gate_proj_kernel(scal, a_own, a_oth, w_own, w_oth, out):
    out[...] = (
        nt(a_own[HALO:, :], w_own[...]) + nt(a_oth[HALO:, :], w_oth[...])
    ).astype(bf16)


def gate_proj(scal, n_own, n_oth, wz_own, wz_oth):
    ext, half = n_own.shape
    rows = ext - HALO
    wide = 2 * GROUP
    weight = pl.BlockSpec((wide, half), lambda j, *_: (j, 0))
    return call(
        gate_proj_kernel,
        (DIN // wide,),
        [const_spec((ext, half)), const_spec((ext, half)), weight, weight],
        pl.BlockSpec((rows, wide), lambda j, *_: (0, j)),
        jax.ShapeDtypeStruct((rows, DIN), bf16),
        [],
        4 * rows * half * DIN,
        4 * DIN * half,
        "gate_proj",
    )(scal, n_own, n_oth, wz_own, wz_oth)


def grad_gated_kernel(scal, e, w_own, w_oth, out):
    out[0] = nt(e[...], w_own[...]).astype(bf16)
    out[1] = nt(e[...], w_oth[...]).astype(bf16)


def grad_gated(scal, e, wo_own, wo_oth):
    rows, d = e.shape
    half = wo_own.shape[0]
    weight = pl.BlockSpec((GROUP, d), lambda j, *_: (j, 0))
    return call(
        grad_gated_kernel,
        (half // GROUP,),
        [const_spec((rows, d)), weight, weight],
        pl.BlockSpec((2, rows, GROUP), lambda j, *_: (0, 0, j)),
        jax.ShapeDtypeStruct((2, rows, half), bf16),
        [],
        4 * rows * half * d,
        4 * d * half,
        "grad_gated",
    )(scal, e, wo_own, wo_oth)


def out_proj_kernel(scal, a_own, a_oth, w_own, w_oth, tok, out):
    total = tok[...].astype(f32) + nn(a_own[...], w_own[...]) + nn(a_oth[...], w_oth[...])
    out[...] = total.astype(bf16)


def out_proj(scal, g_own, g_oth, wo_own, wo_oth, tok):
    rows, d = tok.shape
    half = wo_own.shape[0]
    wide = 2 * GROUP
    weight = pl.BlockSpec((half, wide), lambda j, *_: (0, j))
    cols = pl.BlockSpec((rows, wide), lambda j, *_: (0, j))
    return call(
        out_proj_kernel,
        (d // wide,),
        [const_spec(g_own.shape), const_spec(g_oth.shape), weight, weight, cols],
        cols,
        jax.ShapeDtypeStruct((rows, d), bf16),
        [],
        4 * rows * half * d,
        4 * d * half,
        "out_proj",
    )(scal, g_own, g_oth, wo_own, wo_oth, tok)


def input_back_kernel(
    scal, ez, wz_own, wz_oth, wu_own, wu_oth, tok, halo, up, gain, *rest
):
    chunks = rest[: CHUNKS + 1]
    grad_out, edge_out, gain_out, acc = rest[CHUNKS + 1 :]
    step = pl.program_id(0)
    per = pl.num_programs(0) // 2
    half = acc.shape[1] // 2
    side = jnp.where(step < per, scal[0], 1 - scal[0])
    place = pl.ds(pl.multiple_of(side * half + lax.rem(step, per) * GROUP, GROUP), GROUP)

    def fill(wz, wu):
        deep = chunks[0].shape[1]
        part = sum(nn(e[...], wu[c * deep : (c + 1) * deep]) for c, e in enumerate(chunks))
        acc[0:HALO, place] = part[0:HALO]
        acc[HALO:, place] = part[HALO:] + nn(ez[...], wz[...])

    @pl.when(step < per)
    def _():
        fill(wz_own, wu_own)

    @pl.when(step >= per)
    def _():
        fill(wz_oth, wu_oth)

    def norm_back(x, rows):
        rs = lax.rsqrt(jnp.mean(x * x, axis=-1, keepdims=True) + EPS)
        unit = x * rs
        en = acc[rows, :]
        scaled = en * gain[...]
        gain_out[0:1, :] += jnp.sum(en * unit, axis=0, keepdims=True)
        return rs * (scaled - unit * jnp.mean(scaled * unit, axis=-1, keepdims=True))

    @pl.when(step == 2 * per - 1)
    def _():
        gain_out[...] = jnp.zeros_like(gain_out)
        edge_out[...] = norm_back(halo[...].astype(f32), pl.ds(0, HALO))

        def body(i, carry):
            rows = pl.ds(pl.multiple_of(i * 64, 64), 64)
            ext_rows = pl.ds(pl.multiple_of(i * 64 + HALO, 16), 64)
            grad_out[rows, :] = up[rows, :].astype(f32) + norm_back(
                tok[rows, :].astype(f32), ext_rows
            )
            return carry

        lax.fori_loop(0, tok.shape[0] // 64, body, 0)


def input_back(scal, ez, eu, wz_own, wz_oth, wu_own, wu_oth, tok, halo, up, gain):
    rows, d = tok.shape
    ext = rows + HALO
    half = wz_own.shape[1]
    per = half // GROUP

    def own(depth):
        return pl.BlockSpec((depth, GROUP), lambda j, *_: (0, jnp.minimum(j, per - 1)))

    def oth(depth):
        return pl.BlockSpec((depth, GROUP), lambda j, *_: (0, jnp.maximum(j - per, 0)))

    zd = wz_own.shape[0]
    ud = wu_own.shape[0]
    return call(
        input_back_kernel,
        (2 * per,),
        [
            const_spec(ez.shape),
            own(zd),
            oth(zd),
            own(ud),
            oth(ud),
            const_spec((rows, d)),
            const_spec((HALO, d)),
            const_spec((rows, d)),
            const_spec((1, d)),
            *[const_spec(e.shape) for e in eu],
        ],
        [const_spec((rows, d)), const_spec((HALO, d)), const_spec((8, d))],
        [
            jax.ShapeDtypeStruct((rows, d), f32),
            jax.ShapeDtypeStruct((HALO, d), f32),
            jax.ShapeDtypeStruct((8, d), f32),
        ],
        [pltpu.VMEM((ext, d), f32)],
        2 * ext * d * (zd + ud),
        2 * d * (zd + ud) + 8 * rows * d,
        "input_back",
    )(scal, ez, wz_own, wz_oth, wu_own, wu_oth, tok, halo, up, gain, *eu)


SIDE = 4


def place_blocks(groups, base, group, parts, rows):
    where = group ^ (base // SIDE)
    within = lax.rem(base, SIDE)
    for k in range(SIDE):
        @pl.when(where == k)
        def _():
            for i, part in enumerate(parts):
                for span, value in zip(rows, part):
                    groups[k][i ^ within, span, :] = value


def outer_ab_kernel(scal, a1, a2, ra1, ra2, b1, b2, rb1, rb2, *groups):
    step = pl.program_id(0)
    base = scal[3]
    width = groups[0].shape[2]
    high = a1.shape[1] // SIDE
    deep = b1.shape[1] // SIDE

    @pl.when(step < SIDE)
    def _():
        low = (tn(a1[...], ra1[...]) + tn(a2[...], ra2[...])).astype(bf16)
        parts = [
            (low[i * high : (i + 1) * high, :width], low[i * high : (i + 1) * high, width:])
            for i in range(SIDE)
        ]
        place_blocks(groups, base, step, parts, [slice(0, high), slice(high, 2 * high)])

    @pl.when(step >= SIDE)
    def _():
        low = (tn(b1[...], rb1[HALO:, :]) + tn(b2[...], rb2[HALO:, :])).astype(bf16)
        parts = [(low[i * deep : (i + 1) * deep],) for i in range(SIDE)]
        place_blocks(groups, base, step - SIDE, parts, [slice(2 * high, 2 * high + deep)])


def outer_ab(scal, a1, a2, ra1, ra2, b1, b2, rb1, rb2):
    toks = a1.shape[0]
    width = rb1.shape[1]
    a_cols = a1.shape[1] // SIDE
    b_cols = b1.shape[1] // SIDE
    shape = (SIDE, 2 * a_cols // SIDE + b_cols // SIDE, width)
    a_spec = pl.BlockSpec((toks, a_cols), lambda j, *_: (0, jnp.minimum(j, SIDE - 1)))
    b_spec = pl.BlockSpec((toks, b_cols), lambda j, *_: (0, jnp.maximum(j - SIDE, 0)))
    return call(
        outer_ab_kernel,
        (2 * SIDE,),
        [
            a_spec,
            a_spec,
            const_spec(ra1.shape),
            const_spec(ra2.shape),
            b_spec,
            b_spec,
            const_spec(rb1.shape),
            const_spec(rb2.shape),
        ],
        [const_spec(shape)] * SIDE,
        [jax.ShapeDtypeStruct(shape, bf16)] * SIDE,
        [],
        8 * toks * a1.shape[1] * ra1.shape[1],
        10**7,
        "outer_ab",
    )(scal, a1, a2, ra1, ra2, b1, b2, rb1, rb2)


def outer_c_kernel(scal, *rest):
    mine = rest[: CHUNKS + 1]
    other = rest[CHUNKS + 1 : 2 * CHUNKS + 2]
    r1, r2 = rest[2 * CHUNKS + 2 : 2 * CHUNKS + 4]
    groups = rest[2 * CHUNKS + 4 : 2 * CHUNKS + 4 + SIDE]
    base = scal[3]
    within = lax.rem(base, SIDE)
    offset = 0
    for c in range(CHUNKS + 1):
        acc = tn(mine[c][...], r1[...]) + tn(other[c][...], r2[...])
        low = acc.astype(bf16)
        height = (low.shape[0] if c < CHUNKS else 2 * N) // BLOCKS
        span = slice(offset, offset + height)
        offset += height
        for k in range(SIDE):
            @pl.when(base // SIDE == k)
            def _():
                for t in range(BLOCKS):
                    groups[(t // SIDE) ^ k][(t % SIDE) ^ within, span, :] = low[
                        t * height : (t + 1) * height
                    ]
    rest[-1][...] = acc[2 * N : 2 * N + H]


def outer_c(scal, mine, other, r1, r2):
    toks, width = r1.shape
    shape = (SIDE, CONV // BLOCKS, width)
    args = [*mine, *other, r1, r2]
    return call(
        outer_c_kernel,
        (1,),
        [const_spec(a.shape) for a in args],
        [const_spec(shape)] * SIDE + [const_spec((H, width))],
        [jax.ShapeDtypeStruct(shape, bf16)] * SIDE + [jax.ShapeDtypeStruct((H, width), f32)],
        [],
        4 * toks * CONV * width,
        10**7,
        "outer_c",
    )(scal, *args)


def own_copies(kernel, args, outs, scratch, aliases, name):
    return pl.pallas_call(
        kernel,
        grid_spec=pltpu.PrefetchScalarGridSpec(
            num_scalar_prefetch=1,
            grid=(1,),
            in_specs=[pl.BlockSpec(memory_space=pl.ANY)] * (len(args) - 1),
            out_specs=[pl.BlockSpec(memory_space=pl.ANY)] * len(outs),
            scratch_shapes=scratch,
        ),
        out_shape=outs,
        input_output_aliases=aliases,
        compiler_params=params(1),
        cost_estimate=pl.CostEstimate(flops=0, bytes_accessed=10**4, transcendentals=0),
        name=name,
    )(*args)


def unload(scal, ab, c, first, targets, shapes, rates, name):
    _, rows_ab, width = ab[0].shape
    rows_c = c[0].shape[1]
    half_in, d = shapes[0]
    high = half_in // BLOCKS
    deep = DIN // BLOCKS
    tall = DIN // (CHUNKS * BLOCKS)
    pieces = [(DIN + i * tall * BLOCKS, tall, i * tall) for i in range(CHUNKS)]
    pieces.append((DIN + CONV - 2 * N, 2 * N // BLOCKS, CHUNKS * tall))
    count = len(ab)
    blocks = sum(p.shape[0] for p in ab)
    extra = [rates] if rates is not None else []
    skip = 2 * count + len(extra) + len(targets)

    def kernel(scal, *refs):
        out_a, out_b, ab_buf, c_buf, wide_a, wide_b, wide_c, in_sems, sems = refs[skip:]
        stores = []

        def send(src, dst, sem):
            store = pltpu.make_async_copy(src, dst, sem)
            store.start()
            stores.append(store)

        def rows_at(ref, start, t, size):
            return ref.at[pl.ds(pl.multiple_of(start + t * size, size), size), :]

        loads = []
        row = 0
        for i in range(count):
            n = ab[i].shape[0]
            for j, (src, buf) in enumerate(((refs[i], ab_buf), (refs[count + i], c_buf))):
                load = pltpu.make_async_copy(src, buf.at[pl.ds(row, n)], in_sems.at[j, i])
                load.start()
                loads.append((load, j, row, n))
            row += n
        if extra:
            send(refs[2 * count], out_b.at[pl.ds(DIN + CONV, H), :], sems.at[blocks, 0])
        for load, kind, row, n in loads:
            load.wait()
            for p in range(row, row + n):
                t = (first + p) ^ scal[3]
                if kind == 0:
                    wide_a[p, :, 0:width] = ab_buf[p, 0:high].astype(f32)
                    wide_a[p, :, width:] = ab_buf[p, high : 2 * high].astype(f32)
                    wide_b[p] = ab_buf[p, 2 * high :].astype(f32)
                    send(wide_a.at[p], rows_at(out_a, 0, t, high), sems.at[p, 0])
                    send(wide_b.at[p], rows_at(out_b, 0, t, deep), sems.at[p, 1])
                    continue
                wide_c[p] = c_buf[p].astype(f32)
                for i, (start, height, inner) in enumerate(pieces):
                    send(
                        wide_c.at[p, pl.ds(inner, height)],
                        rows_at(out_b, start, t, height),
                        sems.at[p, 2 + i],
                    )
        for store in stores:
            store.wait()

    args = [scal, *ab, *c, *extra, *targets]
    return own_copies(
        kernel,
        args,
        [jax.ShapeDtypeStruct(shape, f32) for shape in shapes],
        [
            pltpu.VMEM((blocks, rows_ab, width), bf16),
            pltpu.VMEM((blocks, rows_c, width), bf16),
            pltpu.VMEM((blocks, high, d), f32),
            pltpu.VMEM((blocks, deep, width), f32),
            pltpu.VMEM((blocks, rows_c, width), f32),
            pltpu.SemaphoreType.DMA((2, count)),
            pltpu.SemaphoreType.DMA((blocks + 1, 2 + len(pieces))),
        ],
        {len(args) - 2 + i: i for i in range(len(targets))},
        name,
    )


def swap(x):
    return lax.ppermute(x, "fsdp", [(0, 1), (1, 0)])


def shifted(x, by):
    length = lax.axis_size("tm")
    return lax.ppermute(x, "tm", [(i, (i + by) % length) for i in range(length)])


def across(x, axis, mask):
    return lax.ppermute(x, axis, [(i, i ^ mask) for i in range(lax.axis_size(axis))])


def after(value, *deps):
    return lax.optimization_barrier((value, *deps))[0]


def sum_low(values):
    return sum(v.astype(f32) for v in values).astype(bf16)


def exchange_corner(groups):
    half = SIDE // 2
    return across(groups[3][:half], "rep", 2), across(groups[3][half:], "rep", 1)


def exchange_sides(groups, corner, *cover):
    half = SIDE // 2
    lo, hi = corner
    first = after(groups[1], *cover)
    by_x = jnp.concatenate([sum_low([first[:half], lo]), first[half:]])
    by_y = jnp.concatenate([groups[2][:half], sum_low([groups[2][half:], hi])])
    return across(by_x, "rep", 1), across(by_y, "rep", 2)


def sum_parts(own, got, *cover):
    every = [after(own, *cover), *got]
    return [sum_low([g[m] for g in every]) for m in range(SIDE)]


def reduce_times(parts, *cover):
    got = [across(parts[m], "tm", m) for m in range(1, SIDE)]
    piece = sum_low([after(parts[0], *cover), *got])
    for axis in ("rep", "tm"):
        bit = SIDE
        while bit < lax.axis_size(axis):
            piece = sum_low([piece, across(piece, axis, bit)])
            bit *= 2
    return piece


def gather_times(piece, *cover):
    got = [across(piece, "tm", m) for m in range(1, SIDE)]
    return jnp.stack([after(piece, *cover), *got])


def gather_replicas(near):
    by_x = across(near, "rep", 1)
    by_y = across(near, "rep", 2)
    return by_x, by_y


def gather_corner(by_x, by_y):
    return across(by_x[: SIDE // 2], "rep", 2), across(by_y[SIDE // 2 :], "rep", 1)


def chain(local, total, logs, by, *cover):
    size = lax.axis_size("tm")
    tm = lax.axis_index("tm")

    def widen(row):
        return jnp.exp(jnp.repeat(row[0, :H], P_SIZE))[None]

    def moved(v, hops):
        return shifted(v, by * hops)

    def inside(v, hops):
        outside = tm < hops if by > 0 else tm >= size - hops
        return jnp.where(outside, 0.0, v.astype(f32))

    def inclusive(held):
        return (local + total * held).astype(bf16)

    first = moved(local.astype(bf16), 1)
    reach = moved(logs, 1)
    total = after(total, *cover)
    held = inside(first, 1)
    sent = inclusive(held)
    got = moved(sent, 2)

    def finish(*cover):
        nonlocal held, got, reach
        span = 1
        reach = after(reach, *cover)
        while True:
            held = held + widen(reach) * inside(got, span + 1)
            if 2 * span + 1 >= size - 1:
                return held.astype(bf16)
            reach = reach + moved(logs + reach, span + 1)
            span = 2 * span + 1
            got = moved(inclusive(held), span + 1)

    return sent, finish


def body(
    tokens, in_weight, out_weight, norm_gain, conv_weight, conv_bias, dt_bias, a_log,
    d_skip, gate_gain, lengths, starts, cotangent,
):
    core = lax.axis_index("fsdp")
    tm = lax.axis_index("tm")
    tm_size = lax.axis_size("tm")
    tok = tokens[0]
    upstream = cotangent[0]
    tok_count, d = tok.shape
    half_d = in_weight.shape[0]
    half_in = out_weight.shape[0]
    half_conv = conv_bias.shape[0]
    half_heads = dt_bias.shape[0]

    lo = starts[0] - tm * tok_count
    scal = jnp.stack(
        [
            core,
            lo,
            lo + lengths[0],
            SIDE * (lax.axis_index("rep") % SIDE) + tm % SIDE,
        ]
    ).astype(jnp.int32)

    def fill(v):
        return [v, jnp.zeros((half_conv - v.shape[0],), f32)]

    pack = jnp.concatenate(
        [conv_weight.reshape(-1), conv_bias]
        + fill(gate_gain)
        + fill(norm_gain)
        + [dt_bias, a_log, d_skip, jnp.zeros((half_conv - 3 * half_heads,), f32)]
    )
    pack = pack.reshape(8, half_conv).astype(bf16)
    pack_oth = swap(pack)
    edge_tok = tok[tok_count - HALO :]
    halo = shifted(edge_tok, 1)
    w_t = after(in_weight.T, edge_tok)
    wu_own = jnp.pad(w_t[DIN:], ((0, GROUP - H), (0, 0))).astype(bf16)
    wu_oth = swap(wu_own)
    taps, vecs, heads, gain = pack_vectors(scal, pack, pack_oth, d)
    wz_own = w_t[:DIN].astype(bf16)
    wz_oth = swap(wz_own)
    wo_own = after(out_weight, wu_own).astype(bf16)
    wo_oth = swap(wo_own)
    up_oth = swap(upstream)

    n_own, n_oth, u, act, dact, dt, sg, cum, cumt, st = front(
        scal, tok, halo, gain, after(wu_own, wz_own, wo_own), wu_oth, taps, heads
    )
    n_got = swap(n_oth)
    cumt = cumt[:H].reshape(H // 4, 4, tok_count)
    total = jnp.exp(jnp.repeat(cum[tok_count - 1, :H], P_SIZE))[None]

    logs = cum[tok_count - 1 :]
    z = gate_proj(scal, n_own, n_oth, wz_own, wz_oth)
    eg = grad_gated(scal, upstream, wo_own, wo_oth)
    sent, finish = chain(st, total, logs, 1, z, eg)
    yloc, s0 = intra(scal, after(act, sent), dt, cum, cumt)
    s_in = finish(yloc)
    g_own, g_oth, ey, ez, r_loc, r_dev, dc_dev, g_loc, gs = gate(
        scal, yloc, act, z, eg, cum, s_in, vecs
    )

    gated_got = swap(g_oth)
    ez_got = swap(ez)
    ab = outer_ab(scal, g_own, gated_got, upstream, up_oth, ez, ez_got, n_own, n_got)
    sent, finish = chain(g_loc, total, logs, -1, ab[0])
    dxt, db_loc, dc_loc, r2, cq = back(scal, after(act, sent), dt, cum, cumt, ey, s0)
    g_in = finish(dxt)
    ab_corner = exchange_corner(ab)
    ab_got = exchange_sides(ab, ab_corner, dxt)
    *eu, gconv, ghead = tail(
        scal, after(act, *ab_corner), dact, u, ey, dxt, taps, dt, sg, cum, g_in, s_in, vecs, heads,
        (db_loc, dc_loc, dc_dev, r_loc, r_dev, r2, cq),
    )
    eu_got = [swap(e) for e in eu]
    ab_parts = sum_parts(ab[0], ab_got, gconv)
    *c, g_rates = outer_c(scal, eu, eu_got, after(n_own, *ab_parts), n_got)
    output = out_proj(scal, g_own, g_oth, wo_own, wo_oth, after(tok, c[0]))
    c_corner = exchange_corner(c)
    c_got = exchange_sides(c, c_corner, output)
    ab_piece = reduce_times(ab_parts, output)
    grad_in, edge, ggain = input_back(
        scal, ez, eu, wz_own, wz_oth, wu_own, wu_oth, after(tok, ab_piece, *c_corner), halo, upstream, gain
    )
    grad_skip = jnp.sum(gs[1].reshape(H, P_SIZE), axis=1)

    def side(v, half):
        return jnp.stack([v[:half], v[half : 2 * half]])

    def slot(v, half):
        return jnp.pad(side(v, half), ((0, 0), (0, half_conv - half)))[:, None]

    head_grads = jnp.stack([ghead[0, :H], ghead[1, :H], grad_skip])
    head_sides = jnp.stack(
        [head_grads[:, :half_heads].reshape(-1), head_grads[:, half_heads:].reshape(-1)]
    )
    packed = jnp.concatenate(
        [
            gconv[:5].reshape(5, 2, half_conv).transpose(1, 0, 2),
            slot(gs[0], half_in),
            slot(ggain[0], half_d),
            jnp.pad(head_sides, ((0, 0), (0, half_conv - 3 * half_heads)))[:, None],
        ],
        axis=1,
    )
    ab_near = gather_times(ab_piece, packed)
    c_parts = sum_parts(c[0], c_got, ab_near)
    packed = after(packed, *c_parts)
    own = lax.dynamic_index_in_dim(packed, core, 0, keepdims=False)
    small = own + swap(lax.dynamic_index_in_dim(packed, 1 - core, 0, keepdims=False))
    small = jnp.concatenate([small, g_rates.reshape(8, -1)], axis=1)

    def total_over(v, axis):
        v = v + sum(across(v, axis, mask) for mask in range(1, SIDE))
        bit = SIDE
        while bit < lax.axis_size(axis):
            v = v + across(v, axis, bit)
            bit *= 2
        return v

    small = total_over(small, "rep")
    ab_x, ab_y = gather_replicas(ab_near)
    c_piece = reduce_times(c_parts)
    c_near = gather_times(c_piece)
    small = total_over(after(small, c_piece), "tm")
    edge = shifted(edge, -1)
    edge = jnp.where(tm == tm_size - 1, jnp.zeros_like(edge), edge)
    input_grad = grad_in.at[tok_count - HALO :].add(edge)
    c_x, c_y = gather_replicas(c_near)
    ab_lo, ab_hi = gather_corner(ab_x, ab_y)
    c_lo, c_hi = gather_corner(c_x, c_y)
    rates = small[:, half_conv:].reshape(H, half_d)

    shapes = [(half_in, d), (DIN + CONV + H, half_d)]
    near = unload(
        scal, [ab_near, ab_x, ab_y], [c_near, c_x, c_y], 0, [], shapes, rates, "finish_near"
    )
    grad_out_w, grad_in_t = unload(
        scal, [ab_lo, ab_hi], [c_lo, c_hi], 3 * SIDE, near, shapes, None, "finish_far"
    )
    hs = half_heads
    return (
        output[None],
        input_grad[None],
        grad_in_t.T,
        grad_out_w,
        small[6, :half_d],
        small[:4, :half_conv],
        small[4, :half_conv],
        small[7, :hs],
        small[7, hs : 2 * hs],
        small[7, 2 * hs : 3 * hs],
        small[5, :half_in],
    )


def solution(mesh):
    return jax.shard_map(
        body,
        mesh=mesh,
        in_specs=(
            P(("rep", "fsdp"), "tm", None),
            P("fsdp", None),
            P("fsdp", None),
            P("fsdp"),
            P(None, "fsdp"),
            P("fsdp"),
            P("fsdp"),
            P("fsdp"),
            P("fsdp"),
            P("fsdp"),
            P(("rep", "fsdp")),
            P(("rep", "fsdp")),
            P(("rep", "fsdp"), "tm", None),
        ),
        out_specs=(
            P(("rep", "fsdp"), "tm", None),
            P(("rep", "fsdp"), "tm", None),
            P("fsdp", None),
            P("fsdp", None),
            P("fsdp"),
            P(None, "fsdp"),
            P("fsdp"),
            P("fsdp"),
            P("fsdp"),
            P("fsdp"),
            P("fsdp"),
        ),
        check_vma=False,
    )
```

```python
import jax
import jax.numpy as jnp
from jax import lax
from jax.experimental import pallas as pl
from jax.experimental.pallas import tpu as pltpu
from jax.sharding import PartitionSpec as P

H = 32
P_SIZE = 64
N = 128
K = 4
DIN = 2048
CONV = 2304
EPS = 1e-05
QB = 128
HALO = 16
GROUP = 256
LANE = 128

bf16 = jnp.bfloat16
f32 = jnp.float32
HIGHEST = lax.Precision.HIGHEST

VMEM_LIMIT = 60 * 1024 * 1024
COST = 1000
CHUNKS = 4
BLOCKS = 16


def nn(a, b):
    return lax.dot_general(a, b, (((1,), (0,)), ((), ())), preferred_element_type=f32)


def nt(a, b):
    return lax.dot_general(a, b, (((1,), (1,)), ((), ())), preferred_element_type=f32)


def exact_nn(a, b):
    return lax.dot_general(
        a, b, (((1,), (0,)), ((), ())), precision=HIGHEST, preferred_element_type=f32
    )


def iota(shape, dim):
    return lax.broadcasted_iota(jnp.int32, shape, dim)


def tn(a, b):
    return lax.dot_general(a, b, (((0,), (0,)), ((), ())), preferred_element_type=f32)


def sigmoid(v):
    return 0.5 + 0.5 * jnp.tanh(0.5 * v)


def split_two(v):
    hi = v.astype(bf16)
    lo = (v - hi.astype(f32)).astype(bf16)
    return hi, lo


def const_spec(shape):
    return pl.BlockSpec(shape, lambda *_: tuple(0 for _ in shape))


def params(steps=1):
    return pltpu.CompilerParams(
        dimension_semantics=("arbitrary",) * steps, vmem_limit_bytes=VMEM_LIMIT
    )


def call(kernel, grid, in_specs, out_specs, out_shape, scratch, flops, nbytes, name):
    return pl.pallas_call(
        kernel,
        grid_spec=pltpu.PrefetchScalarGridSpec(
            num_scalar_prefetch=1,
            grid=grid,
            in_specs=in_specs,
            out_specs=out_specs,
            scratch_shapes=scratch,
        ),
        out_shape=out_shape,
        compiler_params=params(len(grid)),
        cost_estimate=pl.CostEstimate(
            flops=flops // COST, bytes_accessed=nbytes // COST, transcendentals=0
        ),
        name=name,
    )


def spread(cols, pair):
    left = cols[:, 2 * pair : 2 * pair + 1]
    right = cols[:, 2 * pair + 1 : 2 * pair + 2]
    lanes = iota((cols.shape[0], LANE), 1)
    return jnp.where(lanes < P_SIZE, left, right)


def spread_group(cols):
    return jnp.concatenate([spread(cols, 0), spread(cols, 1)], axis=1)


def block_diag(pair_low):
    lanes = iota(pair_low.shape, 1)
    zero = jnp.zeros_like(pair_low)
    return jnp.concatenate(
        [jnp.where(lanes < P_SIZE, pair_low, zero), jnp.where(lanes < P_SIZE, zero, pair_low)],
        axis=0,
    )


def head_columns(cols, group):
    return pltpu.roll(cols, lax.rem(LANE - 4 * group, LANE), 1)


def head_picker(lanes_in, first_head):
    rows = iota((lanes_in, LANE), 0) // P_SIZE + first_head
    return (rows == iota((lanes_in, LANE), 1)).astype(bf16)


def pack_kernel(scal, own, oth, taps, vecs, heads, gain):
    core = scal[0]
    span = own.shape[1]
    half_in = vecs.shape[1] // 2
    half_d = gain.shape[1] // 2
    taps[...] = jnp.zeros_like(taps)
    vecs[...] = jnp.zeros_like(vecs)
    sides = []
    for src, place in ((own, core), (oth, 1 - core)):
        block = src[...].astype(bf16).astype(f32)

        def at(width):
            return pl.ds(pl.multiple_of(place * width, LANE), width)

        taps[0:5, at(span)] = block[0:5]
        vecs[0:1, at(half_in)] = block[5:6, :half_in]
        gain[0:1, at(half_d)] = block[6:7, :half_d]
        sides.append(jnp.broadcast_to(block[7:8, :LANE], (8, LANE)))
    width = H // 2
    lanes = iota((8, LANE), 1)
    rows = []
    for i in range(3):
        first = jnp.where(core == 0, sides[0], sides[1])
        second = jnp.where(core == 0, sides[1], sides[0])
        low = pltpu.roll(first, (LANE - i * width) % LANE, 1)
        high = pltpu.roll(second, (LANE - i * width + width) % LANE, 1)
        rows.append(jnp.where(lanes < width, low, jnp.where(lanes < H, high, 0.0)))
    rate = jnp.where(lanes < H, -jnp.exp(rows[1]), 0.0)
    pick = iota((8, LANE), 0)
    heads[...] = jnp.where(pick == 0, rows[0], jnp.where(pick == 1, rate, 0.0))
    skip = rows[2].astype(bf16)
    expand = (iota((LANE, DIN), 1) // P_SIZE == iota((LANE, DIN), 0)).astype(bf16)
    vecs[1:2, :] = nn(skip, expand)[0:1]


def pack_vectors(scal, own, oth, d):
    return call(
        pack_kernel,
        (1,),
        [const_spec(own.shape), const_spec(oth.shape)],
        [const_spec((8, CONV)), const_spec((8, DIN)), const_spec((8, LANE)), const_spec((1, d))],
        [
            jax.ShapeDtypeStruct((8, CONV), f32),
            jax.ShapeDtypeStruct((8, DIN), f32),
            jax.ShapeDtypeStruct((8, LANE), f32),
            jax.ShapeDtypeStruct((1, d), f32),
        ],
        [],
        10**6,
        10**5,
        "vectors",
    )(scal, own, oth)


def front_kernel(
    scal, tok, halo, gain, w_own, w_oth, r_own, r_oth, taps, heads,
    n_own, n_oth, u_out, act_out, dact_out, dt_out, sg_out, cum_out, cumt_out, st_out, st_low,
    ubuf, bt, ecl,
):
    step = pl.program_id(0)
    tok_count = tok.shape[0]
    half = w_own.shape[1]
    own = pl.ds(pl.multiple_of(scal[0] * half, LANE), half)
    oth = pl.ds(pl.multiple_of((1 - scal[0]) * half, LANE), half)
    lo = scal[1]
    hi = scal[2]

    @pl.when(step == 0)
    def _():
        def rows_of(src, base, dst, count):
            x = src[pl.ds(base, count), :].astype(f32)
            rs = lax.rsqrt(jnp.mean(x * x, axis=-1, keepdims=True) + EPS)
            for out, cols in ((n_own, own), (n_oth, oth)):
                part = src[pl.ds(base, count), cols].astype(f32)
                out[pl.ds(dst, count), :] = (part * rs * gain[:, cols]).astype(bf16)

        rows_of(halo, 0, 0, HALO)

        def body(i, carry):
            base = pl.multiple_of(i * 64, 64)
            rows_of(tok, base, pl.multiple_of(base + HALO, 16), 64)
            return carry

        lax.fori_loop(0, tok_count // 64, body, 0)
        r = nt(n_own[HALO:, :], r_own[...]) + nt(n_oth[HALO:, :], r_oth[...])
        pre = r.astype(bf16).astype(f32) + heads[0:1, :]
        pos = iota((tok_count, LANE), 0)
        keep = (pos >= lo) & (pos < hi) & (iota((tok_count, LANE), 1) < H)
        soft = jnp.maximum(pre, 0.0) + jnp.log1p(jnp.exp(-jnp.abs(pre)))
        dt = jnp.where(keep, soft, 0.0)
        dt_out[...] = dt
        sg_out[...] = jnp.where(keep, 1.0 / (1.0 + jnp.exp(-pre)), 0.0)
        da = dt * heads[1:2, :]
        tri = (iota((QB, QB), 0) >= iota((QB, QB), 1)).astype(f32)
        carry = jnp.zeros((1, LANE), f32)
        for q in range(tok_count // QB):
            cum = exact_nn(tri, da[q * QB : (q + 1) * QB]) + carry
            cum_out[q * QB : (q + 1) * QB, :] = cum
            cumt_out[:, q * QB : (q + 1) * QB] = cum.T
            carry = cum[QB - 1 : QB]
        ecl[...] = jnp.exp(carry - cum_out[...])

    u = nt(n_own[...], w_own[...]) + nt(n_oth[...], w_oth[...])
    pos = iota(u.shape, 0) - HALO
    u = jnp.where((pos >= lo) & (pos < hi), u, 0.0).astype(bf16)
    u_out[...] = u
    ubuf[...] = u.astype(f32)
    c = taps[4:5, :] + sum(
        taps[k : k + 1, :] * ubuf[HALO - 3 + k : HALO - 3 + k + tok_count, :] for k in range(K)
    )
    s = sigmoid(c)
    act = (c * s).astype(bf16)
    act_out[...] = act
    dact_out[...] = (s * (1.0 + c * (1.0 - s))).astype(bf16)

    @pl.when(step == 0)
    def _():
        bt[...] = act[:, :N].astype(f32).T.astype(bf16)

    @pl.when(step > 0)
    def _():
        group = step - 1
        dtg = spread_group(head_columns(dt_out[...], group))
        ecg = spread_group(head_columns(ecl[...], group))
        xt = (act.astype(f32) * dtg).astype(bf16)
        xw = (xt.astype(f32) * ecg).astype(bf16)
        state = nn(bt[...], xw)
        st_out[...] = state
        st_low[...] = state.astype(bf16)


def front(scal, tok, halo, gain, wu_own, wu_oth, taps, heads):
    tok_count, d = tok.shape
    half = wu_own.shape[1]
    ext = tok_count + HALO
    groups = CONV // GROUP
    first = groups - 1

    def col(j, *_):
        return (0, (j + first) % groups)

    weight = pl.BlockSpec((GROUP, half), lambda j, *_: ((j + first) % groups, 0))
    narrow = pl.BlockSpec((LANE, half), lambda j, *_: (CONV // LANE, 0))
    return call(
        front_kernel,
        (groups,),
        [
            const_spec((tok_count, d)),
            const_spec((HALO, d)),
            const_spec((1, d)),
            weight,
            weight,
            narrow,
            narrow,
            pl.BlockSpec((8, GROUP), col),
            const_spec((8, LANE)),
        ],
        [
            const_spec((ext, half)),
            const_spec((ext, half)),
            pl.BlockSpec((ext, GROUP), col),
            pl.BlockSpec((tok_count, GROUP), col),
            pl.BlockSpec((tok_count, GROUP), col),
            const_spec((tok_count, LANE)),
            const_spec((tok_count, LANE)),
            const_spec((tok_count, LANE)),
            const_spec((LANE, tok_count)),
            pl.BlockSpec((N, GROUP), lambda j, *_: (0, jnp.maximum(j - 1, 0))),
            pl.BlockSpec((N, GROUP), lambda j, *_: (0, jnp.maximum(j - 1, 0))),
        ],
        [
            jax.ShapeDtypeStruct((ext, half), bf16),
            jax.ShapeDtypeStruct((ext, half), bf16),
            jax.ShapeDtypeStruct((ext, CONV), bf16),
            jax.ShapeDtypeStruct((tok_count, CONV), bf16),
            jax.ShapeDtypeStruct((tok_count, CONV), bf16),
            jax.ShapeDtypeStruct((tok_count, LANE), f32),
            jax.ShapeDtypeStruct((tok_count, LANE), f32),
            jax.ShapeDtypeStruct((tok_count, LANE), f32),
            jax.ShapeDtypeStruct((LANE, tok_count), f32),
            jax.ShapeDtypeStruct((N, DIN), f32),
            jax.ShapeDtypeStruct((N, DIN), bf16),
        ],
        [
            pltpu.VMEM((ext, GROUP), f32),
            pltpu.VMEM((N, tok_count), bf16),
            pltpu.VMEM((tok_count, LANE), f32),
        ],
        2 * ext * d * (CONV + LANE),
        2 * (ext * d + d * CONV + 3 * ext * CONV),
        "front",
    )(scal, tok, halo, gain, wu_own, wu_oth, wu_own, wu_oth, taps, heads)


def intra_kernel(scal, x, bc, dt, cum, cumt, y_out, s0_out, scores, bt):
    group = pl.program_id(0)
    blocks = x.shape[0] // QB

    @pl.when(group == 0)
    def _():
        lower = iota((QB, QB), 0) >= iota((QB, QB), 1)
        bt[...] = bc[:, :N].astype(f32).T.astype(bf16)
        for q in range(blocks):
            rows = slice(q * QB, (q + 1) * QB)
            scores[q] = jnp.where(lower, nt(bc[rows, N:], bc[rows, :N]), 0.0)

    dtr = head_columns(dt[...], group)
    cumr = head_columns(cum[...], group)
    carry = jnp.zeros((N, GROUP), f32)
    for q in range(blocks):
        rows = slice(q * QB, (q + 1) * QB)
        cq = cumr[rows]
        end = cq[QB - 1 : QB]
        start = cumr[q * QB - 1 : q * QB] if q else jnp.zeros((1, LANE), f32)
        xt = (x[rows, :].astype(f32) * spread_group(dtr[rows])).astype(bf16)
        low_carry = carry.astype(bf16)
        s0_out[q] = low_carry
        ys = []
        for pair in range(2):
            mats = []
            for e in range(2):
                h = 2 * pair + e
                row = cumt[0, h : h + 1, rows]
                decay = jnp.exp(jnp.minimum(cq[:, h : h + 1] - row, 0.0))
                mats.append((decay * scores[q]).astype(bf16))
            ys.append(
                nn(
                    jnp.concatenate(mats, axis=1),
                    block_diag(xt[:, pair * LANE : (pair + 1) * LANE]),
                )
            )
        y = jnp.concatenate(ys, axis=1)
        if q:
            y = y + jnp.exp(spread_group(cq - start)) * nn(bc[rows, N:], low_carry)
        y_out[rows, :] = y
        if q < blocks - 1:
            xw = (xt.astype(f32) * jnp.exp(spread_group(end - cq))).astype(bf16)
            fresh = nn(bt[:, rows], xw)
            carry = fresh if q == 0 else fresh + carry * jnp.exp(spread_group(end - start))


def intra(scal, act, dt, cum, cumt):
    tok_count = act.shape[0]
    blocks = tok_count // QB
    groups = DIN // GROUP
    return call(
        intra_kernel,
        (groups,),
        [
            pl.BlockSpec((tok_count, GROUP), lambda j, *_: (0, j)),
            pl.BlockSpec((tok_count, GROUP), lambda j, *_: (0, groups)),
            const_spec((tok_count, LANE)),
            const_spec((tok_count, LANE)),
            pl.BlockSpec((1, 4, tok_count), lambda j, *_: (j, 0, 0)),
        ],
        [
            pl.BlockSpec((tok_count, GROUP), lambda j, *_: (0, j)),
            pl.BlockSpec((blocks, N, GROUP), lambda j, *_: (0, 0, j)),
        ],
        [
            jax.ShapeDtypeStruct((tok_count, DIN), f32),
            jax.ShapeDtypeStruct((blocks, N, DIN), bf16),
        ],
        [pltpu.VMEM((blocks, QB, QB), f32), pltpu.VMEM((N, tok_count), bf16)],
        2 * tok_count * DIN * 3 * N,
        8 * tok_count * DIN,
        "intra",
    )(scal, act, act, dt, cum, cumt)


def gate_kernel(
    scal, yloc, act, z, eg, cum, s_in, vecs,
    own_out, oth_out, ey_out, ez_out, r_loc, r_dev, dc_out, g_out, gs_out, g_low,
    pick, vbuf, ytbuf, ydbuf,
):
    step = pl.program_id(0)
    rows = yloc.shape[0]
    groups = DIN // GROUP
    per = groups // 2

    @pl.when(step == 0)
    def _():
        pick[...] = head_picker(DIN, 0)
        g_out[...] = jnp.zeros_like(g_out)
        gs_out[...] = jnp.zeros_like(gs_out)

    pos = iota((rows, 1), 0) + step * rows
    valid = ((pos >= scal[1]) & (pos < scal[2])).astype(f32)
    cq = cum[...]
    ecq = jnp.exp(cq)
    cmat = act[:, DIN + N :]
    ssq = jnp.zeros((rows, GROUP), f32)
    for g in range(groups):
        cols = slice(g * GROUP, (g + 1) * GROUP)
        eg_cum = jnp.concatenate([spread(ecq, 2 * g), spread(ecq, 2 * g + 1)], axis=1)
        yd = eg_cum * nn(cmat, s_in[:, cols])
        ydbuf[:, cols] = yd
        yt = yloc[:, cols] + yd + vecs[1:2, cols] * act[:, cols].astype(f32)
        ytbuf[:, cols] = yt
        zz = z[:, cols].astype(f32)
        v = yt * (zz * sigmoid(zz))
        vbuf[:, cols] = v
        ssq = ssq + v * v
    rs = lax.rsqrt(jnp.sum(ssq, axis=-1, keepdims=True) / DIN + EPS)
    mixed = jnp.zeros((rows, GROUP), f32)
    low_half = scal[0] == 0
    for i in range(per):
        local = slice(i * GROUP, (i + 1) * GROUP)
        outs = []
        for half in range(2):
            g = half * per + i
            cols = slice(g * GROUP, (g + 1) * GROUP)
            n = vbuf[:, cols] * rs
            vbuf[:, cols] = n
            gain = vecs[0:1, cols]
            outs.append((n * gain * valid).astype(bf16))
            e = eg[half ^ scal[0], :, local].astype(f32) * valid
            gs_out[0:1, cols] += jnp.sum(e * n, axis=0, keepdims=True)
            mixed = mixed + e * gain * n
        own_out[:, local] = jnp.where(low_half, outs[0], outs[1])
        oth_out[:, local] = jnp.where(low_half, outs[1], outs[0])
    m2 = jnp.sum(mixed, axis=-1, keepdims=True) / DIN
    rl = jnp.zeros((rows, LANE), f32)
    rd = jnp.zeros((rows, LANE), f32)
    dc = jnp.zeros((rows, N), f32)
    ct = cmat.astype(f32).T.astype(bf16)
    for g in range(groups):
        cols = slice(g * GROUP, (g + 1) * GROUP)
        n = vbuf[:, cols]
        side = (g // per) ^ scal[0]
        local = slice((g % per) * GROUP, (g % per + 1) * GROUP)
        e = eg[side, :, local].astype(f32) * valid
        ev = rs * (e * vecs[0:1, cols] - n * m2)
        zz = z[:, cols].astype(f32)
        sz = sigmoid(zz)
        ey = ev * (zz * sz)
        ez_out[:, cols] = (ev * ytbuf[:, cols] * (sz * (1.0 + zz * (1.0 - sz)))).astype(bf16)
        gs_out[1:2, cols] += jnp.sum(ey * act[:, cols].astype(f32), axis=0, keepdims=True)
        low = ey.astype(bf16)
        ey_out[:, cols] = low
        eyf = low.astype(f32)
        ph, pl_ = split_two(eyf * yloc[:, cols])
        rl = rl + nn(ph, pick[cols, :]) + nn(pl_, pick[cols, :])
        rd = rd + nn((eyf * ydbuf[:, cols]).astype(bf16), pick[cols, :])
        eg_cum = jnp.concatenate([spread(ecq, 2 * g), spread(ecq, 2 * g + 1)], axis=1)
        eye = (eyf * eg_cum).astype(bf16)
        g_out[:, cols] += nn(ct, eye)
        dc = dc + nt(eye, s_in[:, cols])
    r_loc[...] = rl
    r_dev[...] = rd
    dc_out[...] = dc

    @pl.when(step == pl.num_programs(0) - 1)
    def _():
        g_low[...] = g_out[...].astype(bf16)


def gate(scal, yloc, act, z, eg, cum, s_in, vecs):
    tok_count = act.shape[0]
    rows = QB

    def rowspec(width):
        return pl.BlockSpec((rows, width), lambda j, *_: (j, 0))

    def out(width, kind):
        return jax.ShapeDtypeStruct((tok_count, width), kind)

    sides = pl.BlockSpec((2, rows, DIN // 2), lambda j, *_: (0, j, 0))

    return call(
        gate_kernel,
        (tok_count // rows,),
        [
            rowspec(DIN),
            rowspec(CONV),
            rowspec(DIN),
            sides,
            rowspec(LANE),
            const_spec((N, DIN)),
            const_spec((8, DIN)),
        ],
        [
            rowspec(DIN // 2),
            rowspec(DIN // 2),
            rowspec(DIN),
            rowspec(DIN),
            rowspec(LANE),
            rowspec(LANE),
            rowspec(LANE),
            const_spec((N, DIN)),
            const_spec((8, DIN)),
            const_spec((N, DIN)),
        ],
        [
            out(DIN // 2, bf16),
            out(DIN // 2, bf16),
            out(DIN, bf16),
            out(DIN, bf16),
            out(LANE, f32),
            out(LANE, f32),
            out(LANE, f32),
            jax.ShapeDtypeStruct((N, DIN), f32),
            jax.ShapeDtypeStruct((8, DIN), f32),
            jax.ShapeDtypeStruct((N, DIN), bf16),
        ],
        [
            pltpu.VMEM((DIN, LANE), bf16),
            pltpu.VMEM((rows, DIN), f32),
            pltpu.VMEM((rows, DIN), f32),
            pltpu.VMEM((rows, DIN), f32),
        ],
        2 * tok_count * DIN * 6 * N,
        20 * tok_count * DIN,
        "gate",
    )(scal, yloc, act, z, eg, cum, s_in, vecs)


def back_kernel(
    scal, x, bc, dt, cum, cumt, ey, s0,
    dxt_out, db_out, dc_out, r2_out, cq_out,
    scores, dscores, ct,
):
    group = pl.program_id(0)
    last = pl.num_programs(0) - 1
    blocks = x.shape[0] // QB
    upper = iota((QB, QB), 0) <= iota((QB, QB), 1)

    @pl.when(group == 0)
    def _():
        ct[...] = bc[:, N:].astype(f32).T.astype(bf16)
        for q in range(blocks):
            rows = slice(q * QB, (q + 1) * QB)
            scores[q] = jnp.where(upper, nt(bc[rows, :N], bc[rows, N:]), 0.0)
        dscores[...] = jnp.zeros_like(dscores)
        db_out[...] = jnp.zeros_like(db_out)
        dc_out[...] = jnp.zeros_like(dc_out)
        r2_out[...] = jnp.zeros_like(r2_out)
        cq_out[...] = jnp.zeros_like(cq_out)

    dtr = head_columns(dt[...], group)
    cumr = head_columns(cum[...], group)
    picks = [head_picker(LANE, 4 * group + 2 * pair) for pair in range(2)]
    picks2 = [jnp.concatenate([p, p], axis=0) for p in picks]
    pick_all = head_picker(GROUP, 4 * group).astype(f32)
    carry = None
    for q in reversed(range(blocks)):
        rows = slice(q * QB, (q + 1) * QB)
        cq = cumr[rows]
        end = cq[QB - 1 : QB]
        start = cumr[q * QB - 1 : q * QB] if q else jnp.zeros((1, LANE), f32)
        xt = (x[rows, :].astype(f32) * spread_group(dtr[rows])).astype(bf16)
        eyq = ey[rows, :]
        dxs = []
        ds = jnp.zeros((QB, QB), f32)
        for pair in range(2):
            lanes = slice(pair * LANE, (pair + 1) * LANE)
            eybd = block_diag(eyq[:, lanes])
            dm = nt(xt[:, lanes], eybd)
            mats = []
            for e in range(2):
                h = 2 * pair + e
                row = cumt[0, h : h + 1, rows]
                decay = jnp.exp(jnp.minimum(row - cq[:, h : h + 1], 0.0))
                mats.append((decay * scores[q]).astype(bf16))
                ds = ds + decay * dm[:, e * QB : (e + 1) * QB]
            dxs.append(nn(jnp.concatenate(mats, axis=1), eybd))
        dscores[q] += ds
        dx = jnp.concatenate(dxs, axis=1)
        xtf = xt.astype(f32)
        eye = None
        if q:
            eye = (eyq.astype(f32) * jnp.exp(spread_group(cq - start))).astype(bf16)
            dc_out[rows, :] += nt(eye, s0[q])
        if carry is not None:
            low = carry.astype(bf16)
            ecl = jnp.exp(spread_group(end - cq))
            dst = ecl * nn(bc[rows, :N], low)
            db_out[rows, :] += nt((xtf * ecl).astype(bf16), low)
            total = jnp.exp(spread_group(end - start))
            vec = jnp.sum(xtf * dst, axis=0, keepdims=True)
            if q:
                vec = vec + total * jnp.sum(carry * s0[q].astype(f32), axis=0, keepdims=True)
            cq_out[q : q + 1, :] += exact_nn(jnp.broadcast_to(vec, (8, GROUP)), pick_all)[0:1]
            dx = dx + dst
        if q:
            fresh = nn(ct[:, rows], eye)
            carry = fresh if carry is None else fresh + total * carry
        dxt_out[rows, :] = dx.astype(bf16)
        prod = xtf * dx
        acc = jnp.zeros((QB, LANE), f32)
        for pair in range(2):
            ph, pl_ = split_two(prod[:, pair * LANE : (pair + 1) * LANE])
            acc = acc + nn(jnp.concatenate([ph, pl_], axis=1), picks2[pair])
        r2_out[rows, :] += acc

    @pl.when(group == last)
    def _():
        for q in range(blocks):
            rows = slice(q * QB, (q + 1) * QB)
            ds = jnp.where(upper, dscores[q], 0.0)
            db_out[rows, :] += nn(ds.astype(bf16), bc[rows, N:])
            dc_out[rows, :] += nn(ds.T.astype(bf16), bc[rows, :N])


def back(scal, act, dt, cum, cumt, ey, s0):
    tok_count = act.shape[0]
    blocks = tok_count // QB
    groups = DIN // GROUP
    wide = pl.BlockSpec((tok_count, GROUP), lambda j, *_: (0, j))
    small = const_spec((tok_count, LANE))
    return call(
        back_kernel,
        (groups,),
        [
            wide,
            pl.BlockSpec((tok_count, GROUP), lambda j, *_: (0, groups)),
            small,
            small,
            pl.BlockSpec((1, 4, tok_count), lambda j, *_: (j, 0, 0)),
            wide,
            pl.BlockSpec((blocks, N, GROUP), lambda j, *_: (0, 0, j)),
        ],
        [wide, small, small, small, const_spec((8, LANE))],
        [
            jax.ShapeDtypeStruct((tok_count, DIN), bf16),
            jax.ShapeDtypeStruct((tok_count, LANE), f32),
            jax.ShapeDtypeStruct((tok_count, LANE), f32),
            jax.ShapeDtypeStruct((tok_count, LANE), f32),
            jax.ShapeDtypeStruct((8, LANE), f32),
        ],
        [
            pltpu.VMEM((blocks, QB, QB), f32),
            pltpu.VMEM((blocks, QB, QB), f32),
            pltpu.VMEM((N, tok_count), bf16),
        ],
        2 * tok_count * DIN * 8 * N,
        8 * tok_count * DIN,
        "back",
    )(scal, act, act, dt, cum, cumt, ey, s0)


def tail_kernel(
    scal, act, bc, dact, u, ey, dxt, taps, dt, sg, cum, g_in, s_in, skip, heads,
    db_loc, dc_loc, dc_dev, r_loc, r_dev, r2, cq,
    *rest,
):
    chunks = rest[: CHUNKS + 1]
    gconv, ghead, ebuf, ubuf, p_acc, d_acc, db_acc, gs_acc = rest[CHUNKS + 1 :]
    eu_out = chunks[-1]
    step = pl.program_id(0)
    last = pl.num_programs(0) - 2
    tok_count = act.shape[0]
    ext = tok_count + HALO
    lo = scal[1]
    hi = scal[2]

    @pl.when(step == 0)
    def _():
        p_acc[...] = jnp.zeros_like(p_acc)
        d_acc[...] = jnp.zeros_like(d_acc)
        db_acc[...] = jnp.zeros_like(db_acc)
        gs_acc[...] = jnp.zeros_like(gs_acc)
        ebuf[...] = jnp.zeros_like(ebuf)

    bmat = bc[:, :N]

    @pl.when(step < last)
    def _():
        cumr = head_columns(cum[...], step)
        dtr = spread_group(head_columns(dt[...], step))
        xf = act[...].astype(f32)
        xtf = (xf * dtr).astype(bf16).astype(f32)
        low = g_in[...]
        end = cumr[tok_count - 1 : tok_count]
        ecl = jnp.exp(spread_group(end - cumr))
        dxd = ecl * nn(bmat, low)
        dx = dxt[...].astype(f32) + dxd
        pick = head_picker(GROUP, 4 * step)
        p_acc[...] += nn((xtf * dxd).astype(bf16), pick)
        d_acc[...] += nn((xf * dx).astype(bf16), pick)
        db_acc[...] += nt((xtf * ecl).astype(bf16), low)
        vec = jnp.sum(low.astype(f32) * s_in[...].astype(f32), axis=0, keepdims=True)
        vec = vec * jnp.exp(spread_group(end))
        gs_acc[...] += exact_nn(jnp.broadcast_to(vec, (8, GROUP)), pick.astype(f32))
        ebuf[HALO : HALO + tok_count, :] = (
            dtr * dx + skip[1:2, :] * ey[...].astype(f32)
        ) * dact[...].astype(f32)

    @pl.when(step == last)
    def _():
        ebuf[HALO : HALO + tok_count, :N] = (db_loc[...] + db_acc[...]) * dact[:, :N].astype(f32)
        ebuf[HALO : HALO + tok_count, N:] = (dc_loc[...] + dc_dev[...]) * dact[:, N:].astype(f32)

    @pl.when(step > last)
    def _():
        rate = heads[1:2, :]
        upper = (iota((QB, QB), 0) <= iota((QB, QB), 1)).astype(f32)
        strict = (iota((QB, QB), 0) > iota((QB, QB), 1)).astype(f32)
        blocks = tok_count // QB
        devs = jnp.zeros((1, LANE), f32)
        suffix = [None] * blocks
        for q in reversed(range(blocks)):
            rows = slice(q * QB, (q + 1) * QB)
            within = exact_nn(upper, r_loc[rows, :] - r2[rows, :]) + cq[q : q + 1, :]
            dev = exact_nn(upper, r_dev[rows, :]) + devs
            devs = dev[0:1]
            suffix[q] = within + dev
        before = gs_acc[0:1, :]
        glog = jnp.zeros((1, LANE), f32)
        gdt = jnp.zeros((1, LANE), f32)
        eu_out[...] = jnp.zeros_like(eu_out)
        for q in range(blocks):
            rows = slice(q * QB, (q + 1) * QB)
            pq = p_acc[rows, :]
            eda = suffix[q] + exact_nn(strict, pq) + before
            before = before + jnp.sum(pq, axis=0, keepdims=True)
            er = (d_acc[rows, :] + rate * eda) * sg[rows, :]
            gdt = gdt + jnp.sum(er, axis=0, keepdims=True)
            glog = glog + rate * jnp.sum(dt[rows, :] * eda, axis=0, keepdims=True)
            eu_out[HALO + q * QB : HALO + (q + 1) * QB, :LANE] = er.astype(bf16)
        ghead[...] = jnp.concatenate([gdt, glog, jnp.zeros((6, LANE), f32)], axis=0)

    @pl.when(step <= last)
    def _():
        ubuf[...] = u[...].astype(f32)
        ec = ebuf[HALO : HALO + tok_count, :]
        gs = [
            jnp.sum(ec * ubuf[HALO - 3 + k : HALO - 3 + k + tok_count, :], axis=0, keepdims=True)
            for k in range(K)
        ]
        gs.append(jnp.sum(ec, axis=0, keepdims=True))
        gs.append(jnp.zeros((3, ec.shape[1]), f32))
        gconv[...] = jnp.concatenate(gs, axis=0)
        eu = sum(taps[k : k + 1, :] * ebuf[3 - k : 3 - k + ext, :] for k in range(K))
        pos = iota(eu.shape, 0) - HALO
        eu = jnp.where((pos >= lo) & (pos < hi), eu, 0.0).astype(bf16)
        for c, chunk in enumerate(chunks):
            @pl.when(step // 2 == c)
            def _():
                chunk[...] = eu


def tail(scal, act, dact, u, ey, dxt, taps, dt, sg, cum, g_in, s_in, skip, heads, smalls):
    tok_count = act.shape[0]
    ext = tok_count + HALO
    groups = DIN // GROUP

    def col(j, *_):
        return (0, jnp.minimum(j, groups))

    def colx(j, *_):
        return (0, jnp.minimum(j, groups - 1))

    def chunk(c):
        return pl.BlockSpec((ext, GROUP), lambda j, *_: (0, jnp.clip(j - 2 * c, 0, 1)))

    wide = pl.BlockSpec((tok_count, GROUP), col)
    widex = pl.BlockSpec((tok_count, GROUP), colx)
    small = const_spec((tok_count, LANE))
    return call(
        tail_kernel,
        (groups + 2,),
        [
            wide,
            pl.BlockSpec((tok_count, GROUP), lambda j, *_: (0, groups)),
            wide,
            pl.BlockSpec((ext, GROUP), col),
            widex,
            widex,
            pl.BlockSpec((8, GROUP), col),
            small,
            small,
            small,
            pl.BlockSpec((N, GROUP), colx),
            pl.BlockSpec((N, GROUP), colx),
            pl.BlockSpec((8, GROUP), lambda j, *_: (0, jnp.minimum(j, groups - 1))),
            const_spec((8, LANE)),
            small,
            small,
            small,
            small,
            small,
            small,
            const_spec((8, LANE)),
        ],
        [
            *[chunk(c) for c in range(CHUNKS + 1)],
            pl.BlockSpec((8, GROUP), col),
            const_spec((8, LANE)),
        ],
        [
            *[jax.ShapeDtypeStruct((ext, 2 * GROUP), bf16)] * (CHUNKS + 1),
            jax.ShapeDtypeStruct((8, CONV), f32),
            jax.ShapeDtypeStruct((8, LANE), f32),
        ],
        [
            pltpu.VMEM((ext + HALO, GROUP), f32),
            pltpu.VMEM((ext, GROUP), f32),
            pltpu.VMEM((tok_count, LANE), f32),
            pltpu.VMEM((tok_count, LANE), f32),
            pltpu.VMEM((tok_count, LANE), f32),
            pltpu.VMEM((8, LANE), f32),
        ],
        2 * tok_count * DIN * 4 * N,
        12 * tok_count * DIN,
        "tail",
    )(
        scal, act, act, dact, u, ey, dxt, taps, dt, sg, cum, g_in, s_in, skip, heads, *smalls
    )


def gate_proj_kernel(scal, a_own, a_oth, w_own, w_oth, out):
    out[...] = (
        nt(a_own[HALO:, :], w_own[...]) + nt(a_oth[HALO:, :], w_oth[...])
    ).astype(bf16)


def gate_proj(scal, n_own, n_oth, wz_own, wz_oth):
    ext, half = n_own.shape
    rows = ext - HALO
    wide = 2 * GROUP
    weight = pl.BlockSpec((wide, half), lambda j, *_: (j, 0))
    return call(
        gate_proj_kernel,
        (DIN // wide,),
        [const_spec((ext, half)), const_spec((ext, half)), weight, weight],
        pl.BlockSpec((rows, wide), lambda j, *_: (0, j)),
        jax.ShapeDtypeStruct((rows, DIN), bf16),
        [],
        4 * rows * half * DIN,
        4 * DIN * half,
        "gate_proj",
    )(scal, n_own, n_oth, wz_own, wz_oth)


def grad_gated_kernel(scal, e, w_own, w_oth, out):
    out[0] = nt(e[...], w_own[...]).astype(bf16)
    out[1] = nt(e[...], w_oth[...]).astype(bf16)


def grad_gated(scal, e, wo_own, wo_oth):
    rows, d = e.shape
    half = wo_own.shape[0]
    weight = pl.BlockSpec((GROUP, d), lambda j, *_: (j, 0))
    return call(
        grad_gated_kernel,
        (half // GROUP,),
        [const_spec((rows, d)), weight, weight],
        pl.BlockSpec((2, rows, GROUP), lambda j, *_: (0, 0, j)),
        jax.ShapeDtypeStruct((2, rows, half), bf16),
        [],
        4 * rows * half * d,
        4 * d * half,
        "grad_gated",
    )(scal, e, wo_own, wo_oth)


def out_proj_kernel(scal, a_own, a_oth, w_own, w_oth, tok, out):
    total = tok[...].astype(f32) + nn(a_own[...], w_own[...]) + nn(a_oth[...], w_oth[...])
    out[...] = total.astype(bf16)


def out_proj(scal, g_own, g_oth, wo_own, wo_oth, tok):
    rows, d = tok.shape
    half = wo_own.shape[0]
    wide = 2 * GROUP
    weight = pl.BlockSpec((half, wide), lambda j, *_: (0, j))
    cols = pl.BlockSpec((rows, wide), lambda j, *_: (0, j))
    return call(
        out_proj_kernel,
        (d // wide,),
        [const_spec(g_own.shape), const_spec(g_oth.shape), weight, weight, cols],
        cols,
        jax.ShapeDtypeStruct((rows, d), bf16),
        [],
        4 * rows * half * d,
        4 * d * half,
        "out_proj",
    )(scal, g_own, g_oth, wo_own, wo_oth, tok)


def input_back_kernel(
    scal, ez, wz_own, wz_oth, wu_own, wu_oth, tok, halo, up, gain, *rest
):
    chunks = rest[: CHUNKS + 1]
    grad_out, edge_out, gain_out, acc = rest[CHUNKS + 1 :]
    step = pl.program_id(0)
    per = pl.num_programs(0) // 2
    half = acc.shape[1] // 2
    side = jnp.where(step < per, scal[0], 1 - scal[0])
    place = pl.ds(pl.multiple_of(side * half + lax.rem(step, per) * GROUP, GROUP), GROUP)

    def fill(wz, wu):
        deep = chunks[0].shape[1]
        part = sum(nn(e[...], wu[c * deep : (c + 1) * deep]) for c, e in enumerate(chunks))
        acc[0:HALO, place] = part[0:HALO]
        acc[HALO:, place] = part[HALO:] + nn(ez[...], wz[...])

    @pl.when(step < per)
    def _():
        fill(wz_own, wu_own)

    @pl.when(step >= per)
    def _():
        fill(wz_oth, wu_oth)

    def norm_back(x, rows):
        rs = lax.rsqrt(jnp.mean(x * x, axis=-1, keepdims=True) + EPS)
        unit = x * rs
        en = acc[rows, :]
        scaled = en * gain[...]
        gain_out[0:1, :] += jnp.sum(en * unit, axis=0, keepdims=True)
        return rs * (scaled - unit * jnp.mean(scaled * unit, axis=-1, keepdims=True))

    @pl.when(step == 2 * per - 1)
    def _():
        gain_out[...] = jnp.zeros_like(gain_out)
        edge_out[...] = norm_back(halo[...].astype(f32), pl.ds(0, HALO))

        def body(i, carry):
            rows = pl.ds(pl.multiple_of(i * 64, 64), 64)
            ext_rows = pl.ds(pl.multiple_of(i * 64 + HALO, 16), 64)
            grad_out[rows, :] = up[rows, :].astype(f32) + norm_back(
                tok[rows, :].astype(f32), ext_rows
            )
            return carry

        lax.fori_loop(0, tok.shape[0] // 64, body, 0)


def input_back(scal, ez, eu, wz_own, wz_oth, wu_own, wu_oth, tok, halo, up, gain):
    rows, d = tok.shape
    ext = rows + HALO
    half = wz_own.shape[1]
    per = half // GROUP

    def own(depth):
        return pl.BlockSpec((depth, GROUP), lambda j, *_: (0, jnp.minimum(j, per - 1)))

    def oth(depth):
        return pl.BlockSpec((depth, GROUP), lambda j, *_: (0, jnp.maximum(j - per, 0)))

    zd = wz_own.shape[0]
    ud = wu_own.shape[0]
    return call(
        input_back_kernel,
        (2 * per,),
        [
            const_spec(ez.shape),
            own(zd),
            oth(zd),
            own(ud),
            oth(ud),
            const_spec((rows, d)),
            const_spec((HALO, d)),
            const_spec((rows, d)),
            const_spec((1, d)),
            *[const_spec(e.shape) for e in eu],
        ],
        [const_spec((rows, d)), const_spec((HALO, d)), const_spec((8, d))],
        [
            pltpu.HBM((rows, d), f32),
            jax.ShapeDtypeStruct((HALO, d), f32),
            jax.ShapeDtypeStruct((8, d), f32),
        ],
        [pltpu.VMEM((ext, d), f32)],
        2 * ext * d * (zd + ud),
        2 * d * (zd + ud) + 8 * rows * d,
        "input_back",
    )(scal, ez, wz_own, wz_oth, wu_own, wu_oth, tok, halo, up, gain, *eu)


SIDE = 4


def place_blocks(groups, base, group, parts, rows):
    where = group ^ (base // SIDE)
    within = lax.rem(base, SIDE)
    for k in range(SIDE):
        @pl.when(where == k)
        def _():
            for i, part in enumerate(parts):
                for span, value in zip(rows, part):
                    groups[k][i ^ within, span, :] = value


def outer_ab_kernel(scal, a1, a2, ra1, ra2, b1, b2, rb1, rb2, *groups):
    step = pl.program_id(0)
    base = scal[3]
    width = groups[0].shape[2]
    high = a1.shape[1] // SIDE
    deep = b1.shape[1] // SIDE

    @pl.when(step < SIDE)
    def _():
        low = (tn(a1[...], ra1[...]) + tn(a2[...], ra2[...])).astype(bf16)
        parts = [
            (low[i * high : (i + 1) * high, :width], low[i * high : (i + 1) * high, width:])
            for i in range(SIDE)
        ]
        place_blocks(groups, base, step, parts, [slice(0, high), slice(high, 2 * high)])

    @pl.when(step >= SIDE)
    def _():
        low = (tn(b1[...], rb1[HALO:, :]) + tn(b2[...], rb2[HALO:, :])).astype(bf16)
        parts = [(low[i * deep : (i + 1) * deep],) for i in range(SIDE)]
        place_blocks(groups, base, step - SIDE, parts, [slice(2 * high, 2 * high + deep)])


def outer_ab(scal, a1, a2, ra1, ra2, b1, b2, rb1, rb2):
    toks = a1.shape[0]
    width = rb1.shape[1]
    a_cols = a1.shape[1] // SIDE
    b_cols = b1.shape[1] // SIDE
    shape = (SIDE, 2 * a_cols // SIDE + b_cols // SIDE, width)
    a_spec = pl.BlockSpec((toks, a_cols), lambda j, *_: (0, jnp.minimum(j, SIDE - 1)))
    b_spec = pl.BlockSpec((toks, b_cols), lambda j, *_: (0, jnp.maximum(j - SIDE, 0)))
    return call(
        outer_ab_kernel,
        (2 * SIDE,),
        [
            a_spec,
            a_spec,
            const_spec(ra1.shape),
            const_spec(ra2.shape),
            b_spec,
            b_spec,
            const_spec(rb1.shape),
            const_spec(rb2.shape),
        ],
        [const_spec(shape)] * SIDE,
        [jax.ShapeDtypeStruct(shape, bf16)] * SIDE,
        [],
        8 * toks * a1.shape[1] * ra1.shape[1],
        10**7,
        "outer_ab",
    )(scal, a1, a2, ra1, ra2, b1, b2, rb1, rb2)


def outer_c_kernel(scal, *rest):
    mine = rest[: CHUNKS + 1]
    other = rest[CHUNKS + 1 : 2 * CHUNKS + 2]
    r1, r2 = rest[2 * CHUNKS + 2 : 2 * CHUNKS + 4]
    groups = rest[2 * CHUNKS + 4 : 2 * CHUNKS + 4 + SIDE]
    base = scal[3]
    within = lax.rem(base, SIDE)
    offset = 0
    for c in range(CHUNKS + 1):
        acc = tn(mine[c][...], r1[...]) + tn(other[c][...], r2[...])
        low = acc.astype(bf16)
        height = (low.shape[0] if c < CHUNKS else 2 * N) // BLOCKS
        span = slice(offset, offset + height)
        offset += height
        for k in range(SIDE):
            @pl.when(base // SIDE == k)
            def _():
                for t in range(BLOCKS):
                    groups[(t // SIDE) ^ k][(t % SIDE) ^ within, span, :] = low[
                        t * height : (t + 1) * height
                    ]
    rest[-1][...] = acc[2 * N : 2 * N + H]


def outer_c(scal, mine, other, r1, r2):
    toks, width = r1.shape
    shape = (SIDE, CONV // BLOCKS, width)
    args = [*mine, *other, r1, r2]
    return call(
        outer_c_kernel,
        (1,),
        [const_spec(a.shape) for a in args],
        [const_spec(shape)] * SIDE + [const_spec((H, width))],
        [jax.ShapeDtypeStruct(shape, bf16)] * SIDE + [jax.ShapeDtypeStruct((H, width), f32)],
        [],
        4 * toks * CONV * width,
        10**7,
        "outer_c",
    )(scal, *args)


def own_copies(kernel, args, outs, scratch, aliases, name):
    return pl.pallas_call(
        kernel,
        grid_spec=pltpu.PrefetchScalarGridSpec(
            num_scalar_prefetch=1,
            grid=(1,),
            in_specs=[pl.BlockSpec(memory_space=pl.ANY)] * (len(args) - 1),
            out_specs=[pl.BlockSpec(memory_space=pl.ANY)] * len(outs),
            scratch_shapes=scratch,
        ),
        out_shape=outs,
        input_output_aliases=aliases,
        compiler_params=params(1),
        cost_estimate=pl.CostEstimate(flops=0, bytes_accessed=10**4, transcendentals=0),
        name=name,
    )(*args)


def unload(scal, ab, c, first, targets, shapes, rates, name):
    _, rows_ab, width = ab[0].shape
    rows_c = c[0].shape[1]
    half_in, d = shapes[0]
    high = half_in // BLOCKS
    deep = DIN // BLOCKS
    tall = DIN // (CHUNKS * BLOCKS)
    pieces = [(DIN + i * tall * BLOCKS, tall, i * tall) for i in range(CHUNKS)]
    pieces.append((DIN + CONV - 2 * N, 2 * N // BLOCKS, CHUNKS * tall))
    count = len(ab)
    blocks = sum(p.shape[0] for p in ab)
    extra = [rates] if rates is not None else []
    skip = 2 * count + len(extra) + len(targets)

    def kernel(scal, *refs):
        out_a, out_b, ab_buf, c_buf, wide_a, wide_b, wide_c, in_sems, sems = refs[skip:]
        stores = []

        def send(src, dst, sem):
            store = pltpu.make_async_copy(src, dst, sem)
            store.start()
            stores.append(store)

        def rows_at(ref, start, t, size):
            return ref.at[pl.ds(pl.multiple_of(start + t * size, size), size), :]

        loads = []
        row = 0
        for i in range(count):
            n = ab[i].shape[0]
            for j, (src, buf) in enumerate(((refs[i], ab_buf), (refs[count + i], c_buf))):
                load = pltpu.make_async_copy(src, buf.at[pl.ds(row, n)], in_sems.at[j, i])
                load.start()
                loads.append((load, j, row, n))
            row += n
        if extra:
            send(refs[2 * count], out_b.at[pl.ds(DIN + CONV, H), :], sems.at[blocks, 0])
        for load, kind, row, n in loads:
            load.wait()
            for p in range(row, row + n):
                t = (first + p) ^ scal[3]
                if kind == 0:
                    wide_a[p, :, 0:width] = ab_buf[p, 0:high].astype(f32)
                    wide_a[p, :, width:] = ab_buf[p, high : 2 * high].astype(f32)
                    wide_b[p] = ab_buf[p, 2 * high :].astype(f32)
                    send(wide_a.at[p], rows_at(out_a, 0, t, high), sems.at[p, 0])
                    send(wide_b.at[p], rows_at(out_b, 0, t, deep), sems.at[p, 1])
                    continue
                wide_c[p] = c_buf[p].astype(f32)
                for i, (start, height, inner) in enumerate(pieces):
                    send(
                        wide_c.at[p, pl.ds(inner, height)],
                        rows_at(out_b, start, t, height),
                        sems.at[p, 2 + i],
                    )
        for store in stores:
            store.wait()

    args = [scal, *ab, *c, *extra, *targets]
    return own_copies(
        kernel,
        args,
        [jax.ShapeDtypeStruct(shape, f32) for shape in shapes],
        [
            pltpu.VMEM((blocks, rows_ab, width), bf16),
            pltpu.VMEM((blocks, rows_c, width), bf16),
            pltpu.VMEM((blocks, high, d), f32),
            pltpu.VMEM((blocks, deep, width), f32),
            pltpu.VMEM((blocks, rows_c, width), f32),
            pltpu.SemaphoreType.DMA((2, count)),
            pltpu.SemaphoreType.DMA((blocks + 1, 2 + len(pieces))),
        ],
        {len(args) - 2 + i: i for i in range(len(targets))},
        name,
    )


def swap(x):
    return lax.ppermute(x, "fsdp", [(0, 1), (1, 0)])


def shifted(x, by):
    length = lax.axis_size("tm")
    return lax.ppermute(x, "tm", [(i, (i + by) % length) for i in range(length)])


def across(x, axis, mask):
    return lax.ppermute(x, axis, [(i, i ^ mask) for i in range(lax.axis_size(axis))])


def after(value, *deps):
    return lax.optimization_barrier((value, *deps))[0]


def sum_low(values):
    return sum(v.astype(f32) for v in values).astype(bf16)


def exchange_corner(groups):
    half = SIDE // 2
    return across(groups[3][:half], "rep", 2), across(groups[3][half:], "rep", 1)


def exchange_sides(groups, corner, *cover):
    half = SIDE // 2
    lo, hi = corner
    first = after(groups[1], *cover)
    by_x = jnp.concatenate([sum_low([first[:half], lo]), first[half:]])
    by_y = jnp.concatenate([groups[2][:half], sum_low([groups[2][half:], hi])])
    return across(by_x, "rep", 1), across(by_y, "rep", 2)


def sum_parts(own, got, *cover):
    every = [after(own, *cover), *got]
    return [sum_low([g[m] for g in every]) for m in range(SIDE)]


def reduce_times(parts, *cover):
    got = [across(parts[m], "tm", m) for m in range(1, SIDE)]
    piece = sum_low([after(parts[0], *cover), *got])
    for axis in ("rep", "tm"):
        bit = SIDE
        while bit < lax.axis_size(axis):
            piece = sum_low([piece, across(piece, axis, bit)])
            bit *= 2
    return piece


def gather_times(piece, *cover):
    got = [across(piece, "tm", m) for m in range(1, SIDE)]
    return jnp.stack([after(piece, *cover), *got])


def gather_replicas(near):
    by_x = across(near, "rep", 1)
    by_y = across(near, "rep", 2)
    return by_x, by_y


def gather_corner(by_x, by_y):
    return across(by_x[: SIDE // 2], "rep", 2), across(by_y[SIDE // 2 :], "rep", 1)


def chain(local, low, total, logs, by, *cover):
    size = lax.axis_size("tm")
    tm = lax.axis_index("tm")

    def widen(row):
        return jnp.exp(jnp.repeat(row[0, :H], P_SIZE))[None]

    def moved(v, hops):
        return shifted(v, by * hops)

    def inside(v, hops):
        outside = tm < hops if by > 0 else tm >= size - hops
        return jnp.where(outside, 0.0, v.astype(f32))

    def inclusive(held):
        return (local + total * held).astype(bf16)

    first = moved(low, 1)
    reach = moved(logs, 1)
    total = after(total, *cover)
    held = inside(first, 1)
    sent = inclusive(held)
    got = moved(sent, 2)

    def finish(*cover):
        nonlocal held, got, reach
        span = 1
        reach = after(reach, *cover)
        while True:
            held = held + widen(reach) * inside(got, span + 1)
            if 2 * span + 1 >= size - 1:
                return held.astype(bf16)
            reach = reach + moved(logs + reach, span + 1)
            span = 2 * span + 1
            got = moved(inclusive(held), span + 1)

    return sent, finish


def body(
    tokens, in_weight, out_weight, norm_gain, conv_weight, conv_bias, dt_bias, a_log,
    d_skip, gate_gain, lengths, starts, cotangent,
):
    core = lax.axis_index("fsdp")
    tm = lax.axis_index("tm")
    tm_size = lax.axis_size("tm")
    tok = tokens[0]
    upstream = cotangent[0]
    tok_count, d = tok.shape
    half_d = in_weight.shape[0]
    half_in = out_weight.shape[0]
    half_conv = conv_bias.shape[0]
    half_heads = dt_bias.shape[0]

    lo = starts[0] - tm * tok_count
    scal = jnp.stack(
        [
            core,
            lo,
            lo + lengths[0],
            SIDE * (lax.axis_index("rep") % SIDE) + tm % SIDE,
        ]
    ).astype(jnp.int32)

    def fill(v):
        return [v, jnp.zeros((half_conv - v.shape[0],), f32)]

    pack = jnp.concatenate(
        [conv_weight.reshape(-1), conv_bias]
        + fill(gate_gain)
        + fill(norm_gain)
        + [dt_bias, a_log, d_skip, jnp.zeros((half_conv - 3 * half_heads,), f32)]
    )
    pack = pack.reshape(8, half_conv)
    pack_oth = swap(pack)
    edge_tok = tok[tok_count - HALO :]
    halo = shifted(edge_tok, 1)
    w_t = after(in_weight.T, edge_tok)
    wu_own = jnp.pad(w_t[DIN:], ((0, GROUP - H), (0, 0))).astype(bf16)
    wu_oth = swap(wu_own)
    taps, vecs, heads, gain = pack_vectors(scal, pack, pack_oth, d)
    wz_own = w_t[:DIN].astype(bf16)
    wz_oth = swap(wz_own)
    wo_own = after(out_weight, wu_own).astype(bf16)
    wo_oth = swap(wo_own)
    up_oth = swap(upstream)

    n_own, n_oth, u, act, dact, dt, sg, cum, cumt, st, st_low = front(
        scal, tok, halo, gain, after(wu_own, wz_own, wo_own), wu_oth, taps, heads
    )
    n_got = swap(n_oth)
    cumt = cumt[:H].reshape(H // 4, 4, tok_count)
    total = jnp.exp(jnp.repeat(cum[tok_count - 1, :H], P_SIZE))[None]

    logs = cum[tok_count - 1 :]
    z = gate_proj(scal, n_own, n_oth, wz_own, wz_oth)
    eg = grad_gated(scal, upstream, wo_own, wo_oth)
    sent, finish = chain(st, st_low, total, logs, 1, z, eg)
    yloc, s0 = intra(scal, after(act, sent), dt, cum, cumt)
    s_in = finish(yloc)
    g_own, g_oth, ey, ez, r_loc, r_dev, dc_dev, g_loc, gs, g_low = gate(
        scal, yloc, act, z, eg, cum, s_in, vecs
    )

    gated_got = swap(g_oth)
    ez_got = swap(ez)
    ab = outer_ab(scal, g_own, gated_got, upstream, up_oth, ez, ez_got, n_own, n_got)
    sent, finish = chain(g_loc, g_low, total, logs, -1, ab[0])
    dxt, db_loc, dc_loc, r2, cq = back(scal, after(act, sent), dt, cum, cumt, ey, s0)
    g_in = finish(dxt)
    ab_corner = exchange_corner(ab)
    ab_got = exchange_sides(ab, ab_corner, dxt)
    *eu, gconv, ghead = tail(
        scal, after(act, *ab_corner), dact, u, ey, dxt, taps, dt, sg, cum, g_in, s_in, vecs, heads,
        (db_loc, dc_loc, dc_dev, r_loc, r_dev, r2, cq),
    )
    eu_got = [swap(e) for e in eu]
    ab_parts = sum_parts(ab[0], ab_got, gconv)
    *c, g_rates = outer_c(scal, eu, eu_got, after(n_own, *ab_parts), n_got)
    c_corner = exchange_corner(c)
    grad_in, edge, ggain = input_back(
        scal, ez, eu, wz_own, wz_oth, wu_own, wu_oth, after(tok, c[0]), halo, upstream, gain
    )
    grad_skip = jnp.sum(gs[1].reshape(H, P_SIZE), axis=1)

    def side(v, half):
        return jnp.stack([v[:half], v[half : 2 * half]])

    def slot(v, half):
        return jnp.pad(side(v, half), ((0, 0), (0, half_conv - half)))[:, None]

    head_grads = jnp.stack([ghead[0, :H], ghead[1, :H], grad_skip])
    head_sides = jnp.stack(
        [head_grads[:, :half_heads].reshape(-1), head_grads[:, half_heads:].reshape(-1)]
    )
    packed = jnp.concatenate(
        [
            gconv[:5].reshape(5, 2, half_conv).transpose(1, 0, 2),
            slot(gs[0], half_in),
            slot(ggain[0], half_d),
            jnp.pad(head_sides, ((0, 0), (0, half_conv - 3 * half_heads)))[:, None],
        ],
        axis=1,
    )
    c_got = exchange_sides(c, c_corner, packed)
    ab_piece = reduce_times(ab_parts, packed)
    output = out_proj(scal, g_own, g_oth, wo_own, wo_oth, after(tok, ab_piece))
    c_parts = sum_parts(c[0], c_got, output)
    ab_near = gather_times(ab_piece, *c_parts)
    packed = after(packed, *c_corner)
    own = lax.dynamic_index_in_dim(packed, core, 0, keepdims=False)
    small = own + swap(lax.dynamic_index_in_dim(packed, 1 - core, 0, keepdims=False))
    small = jnp.concatenate([small, g_rates.reshape(8, -1)], axis=1)

    def total_over(v, axis):
        v = v + sum(across(v, axis, mask) for mask in range(1, SIDE))
        bit = SIDE
        while bit < lax.axis_size(axis):
            v = v + across(v, axis, bit)
            bit *= 2
        return v

    small = total_over(small, "rep")
    ab_x, ab_y = gather_replicas(ab_near)
    c_piece = reduce_times(c_parts)
    c_near = gather_times(c_piece)
    small = total_over(after(small, c_piece), "tm")
    edge = shifted(after(edge.astype(bf16), *c_parts), -1).astype(f32)
    edge = jnp.where(tm == tm_size - 1, jnp.zeros_like(edge), edge)
    input_grad = grad_in.at[tok_count - HALO :].add(edge)
    c_x, c_y = gather_replicas(c_near)
    ab_lo, ab_hi = gather_corner(ab_x, ab_y)
    c_lo, c_hi = gather_corner(c_x, c_y)
    rates = small[:, half_conv:].reshape(H, half_d)

    shapes = [(half_in, d), (DIN + CONV + H, half_d)]
    near = unload(
        scal, [ab_near, ab_x, ab_y], [c_near, c_x, c_y], 0, [], shapes, rates, "finish_near"
    )
    grad_out_w, grad_in_t = unload(
        scal, [ab_lo, ab_hi], [c_lo, c_hi], 3 * SIDE, near, shapes, None, "finish_far"
    )
    hs = half_heads
    return (
        output[None],
        input_grad[None],
        grad_in_t.T,
        grad_out_w,
        small[6, :half_d],
        small[:4, :half_conv],
        small[4, :half_conv],
        small[7, :hs],
        small[7, hs : 2 * hs],
        small[7, 2 * hs : 3 * hs],
        small[5, :half_in],
    )


def solution(mesh):
    return jax.shard_map(
        body,
        mesh=mesh,
        in_specs=(
            P(("rep", "fsdp"), "tm", None),
            P("fsdp", None),
            P("fsdp", None),
            P("fsdp"),
            P(None, "fsdp"),
            P("fsdp"),
            P("fsdp"),
            P("fsdp"),
            P("fsdp"),
            P("fsdp"),
            P(("rep", "fsdp")),
            P(("rep", "fsdp")),
            P(("rep", "fsdp"), "tm", None),
        ),
        out_specs=(
            P(("rep", "fsdp"), "tm", None),
            P(("rep", "fsdp"), "tm", None),
            P("fsdp", None),
            P("fsdp", None),
            P("fsdp"),
            P(None, "fsdp"),
            P("fsdp"),
            P("fsdp"),
            P("fsdp"),
            P("fsdp"),
            P("fsdp"),
        ),
        check_vma=False,
    )
```

```python
import jax
import jax.numpy as jnp
from jax import lax
from jax.experimental import pallas as pl
from jax.experimental.pallas import tpu as pltpu
from jax.sharding import PartitionSpec as P

H = 32
P_SIZE = 64
N = 128
K = 4
DIN = 2048
CONV = 2304
EPS = 1e-05
QB = 128
HALO = 16
GROUP = 256
LANE = 128

bf16 = jnp.bfloat16
f32 = jnp.float32
HIGHEST = lax.Precision.HIGHEST

VMEM_LIMIT = 60 * 1024 * 1024
COST = 1000
CHUNKS = 4
BLOCKS = 16


def nn(a, b):
    return lax.dot_general(a, b, (((1,), (0,)), ((), ())), preferred_element_type=f32)


def nt(a, b):
    return lax.dot_general(a, b, (((1,), (1,)), ((), ())), preferred_element_type=f32)


def exact_nn(a, b):
    return lax.dot_general(
        a, b, (((1,), (0,)), ((), ())), precision=HIGHEST, preferred_element_type=f32
    )


def iota(shape, dim):
    return lax.broadcasted_iota(jnp.int32, shape, dim)


def tn(a, b):
    return lax.dot_general(a, b, (((0,), (0,)), ((), ())), preferred_element_type=f32)


def sigmoid(v):
    return 0.5 + 0.5 * jnp.tanh(0.5 * v)


def split_two(v):
    hi = v.astype(bf16)
    lo = (v - hi.astype(f32)).astype(bf16)
    return hi, lo


def const_spec(shape):
    return pl.BlockSpec(shape, lambda *_: tuple(0 for _ in shape))


def params(steps=1):
    return pltpu.CompilerParams(
        dimension_semantics=("arbitrary",) * steps, vmem_limit_bytes=VMEM_LIMIT
    )


def call(kernel, grid, in_specs, out_specs, out_shape, scratch, flops, nbytes, name):
    return pl.pallas_call(
        kernel,
        grid_spec=pltpu.PrefetchScalarGridSpec(
            num_scalar_prefetch=1,
            grid=grid,
            in_specs=in_specs,
            out_specs=out_specs,
            scratch_shapes=scratch,
        ),
        out_shape=out_shape,
        compiler_params=params(len(grid)),
        cost_estimate=pl.CostEstimate(
            flops=flops // COST, bytes_accessed=nbytes // COST, transcendentals=0
        ),
        name=name,
    )


def spread(cols, pair):
    left = cols[:, 2 * pair : 2 * pair + 1]
    right = cols[:, 2 * pair + 1 : 2 * pair + 2]
    lanes = iota((cols.shape[0], LANE), 1)
    return jnp.where(lanes < P_SIZE, left, right)


def spread_group(cols):
    return jnp.concatenate([spread(cols, 0), spread(cols, 1)], axis=1)


def block_diag(pair_low):
    lanes = iota(pair_low.shape, 1)
    zero = jnp.zeros_like(pair_low)
    return jnp.concatenate(
        [jnp.where(lanes < P_SIZE, pair_low, zero), jnp.where(lanes < P_SIZE, zero, pair_low)],
        axis=0,
    )


def head_columns(cols, group):
    return pltpu.roll(cols, lax.rem(LANE - 4 * group, LANE), 1)


def head_picker(lanes_in, first_head):
    rows = iota((lanes_in, LANE), 0) // P_SIZE + first_head
    return (rows == iota((lanes_in, LANE), 1)).astype(bf16)


def pack_kernel(scal, own, oth, taps, vecs, heads, gain):
    core = scal[0]
    span = own.shape[1]
    half_in = vecs.shape[1] // 2
    half_d = gain.shape[1] // 2
    taps[...] = jnp.zeros_like(taps)
    vecs[...] = jnp.zeros_like(vecs)
    sides = []
    for src, place in ((own, core), (oth, 1 - core)):
        block = src[...].astype(bf16).astype(f32)

        def at(width):
            return pl.ds(pl.multiple_of(place * width, LANE), width)

        taps[0:5, at(span)] = block[0:5]
        vecs[0:1, at(half_in)] = block[5:6, :half_in]
        gain[0:1, at(half_d)] = block[6:7, :half_d]
        sides.append(jnp.broadcast_to(block[7:8, :LANE], (8, LANE)))
    width = H // 2
    lanes = iota((8, LANE), 1)
    rows = []
    for i in range(3):
        first = jnp.where(core == 0, sides[0], sides[1])
        second = jnp.where(core == 0, sides[1], sides[0])
        low = pltpu.roll(first, (LANE - i * width) % LANE, 1)
        high = pltpu.roll(second, (LANE - i * width + width) % LANE, 1)
        rows.append(jnp.where(lanes < width, low, jnp.where(lanes < H, high, 0.0)))
    rate = jnp.where(lanes < H, -jnp.exp(rows[1]), 0.0)
    pick = iota((8, LANE), 0)
    heads[...] = jnp.where(pick == 0, rows[0], jnp.where(pick == 1, rate, 0.0))
    skip = rows[2].astype(bf16)
    expand = (iota((LANE, DIN), 1) // P_SIZE == iota((LANE, DIN), 0)).astype(bf16)
    vecs[1:2, :] = nn(skip, expand)[0:1]


def pack_vectors(scal, own, oth, d):
    return call(
        pack_kernel,
        (1,),
        [const_spec(own.shape), const_spec(oth.shape)],
        [const_spec((8, CONV)), const_spec((8, DIN)), const_spec((8, LANE)), const_spec((1, d))],
        [
            jax.ShapeDtypeStruct((8, CONV), f32),
            jax.ShapeDtypeStruct((8, DIN), f32),
            jax.ShapeDtypeStruct((8, LANE), f32),
            jax.ShapeDtypeStruct((1, d), f32),
        ],
        [],
        10**6,
        10**5,
        "vectors",
    )(scal, own, oth)


def front_kernel(
    scal, tok, halo, gain, w_own, w_oth, r_own, r_oth, taps, heads,
    n_own, n_oth, u_out, act_out, dact_out, dt_out, sg_out, cum_out, cumt_out, st_out, st_low,
    ubuf, bt, ecl,
):
    step = pl.program_id(0)
    tok_count = tok.shape[0]
    half = w_own.shape[1]
    own = pl.ds(pl.multiple_of(scal[0] * half, LANE), half)
    oth = pl.ds(pl.multiple_of((1 - scal[0]) * half, LANE), half)
    lo = scal[1]
    hi = scal[2]

    @pl.when(step == 0)
    def _():
        def rows_of(src, base, dst, count):
            x = src[pl.ds(base, count), :].astype(f32)
            rs = lax.rsqrt(jnp.mean(x * x, axis=-1, keepdims=True) + EPS)
            for out, cols in ((n_own, own), (n_oth, oth)):
                part = src[pl.ds(base, count), cols].astype(f32)
                out[pl.ds(dst, count), :] = (part * rs * gain[:, cols]).astype(bf16)

        rows_of(halo, 0, 0, HALO)

        def body(i, carry):
            base = pl.multiple_of(i * 64, 64)
            rows_of(tok, base, pl.multiple_of(base + HALO, 16), 64)
            return carry

        lax.fori_loop(0, tok_count // 64, body, 0)
        r = nt(n_own[HALO:, :], r_own[...]) + nt(n_oth[HALO:, :], r_oth[...])
        pre = r.astype(bf16).astype(f32) + heads[0:1, :]
        pos = iota((tok_count, LANE), 0)
        keep = (pos >= lo) & (pos < hi) & (iota((tok_count, LANE), 1) < H)
        soft = jnp.maximum(pre, 0.0) + jnp.log1p(jnp.exp(-jnp.abs(pre)))
        dt = jnp.where(keep, soft, 0.0)
        dt_out[...] = dt
        sg_out[...] = jnp.where(keep, 1.0 / (1.0 + jnp.exp(-pre)), 0.0)
        da = dt * heads[1:2, :]
        tri = (iota((QB, QB), 0) >= iota((QB, QB), 1)).astype(f32)
        carry = jnp.zeros((1, LANE), f32)
        for q in range(tok_count // QB):
            cum = exact_nn(tri, da[q * QB : (q + 1) * QB]) + carry
            cum_out[q * QB : (q + 1) * QB, :] = cum
            cumt_out[:, q * QB : (q + 1) * QB] = cum.T
            carry = cum[QB - 1 : QB]
        ecl[...] = jnp.exp(carry - cum_out[...])

    u = nt(n_own[...], w_own[...]) + nt(n_oth[...], w_oth[...])
    pos = iota(u.shape, 0) - HALO
    u = jnp.where((pos >= lo) & (pos < hi), u, 0.0).astype(bf16)
    u_out[...] = u
    ubuf[...] = u.astype(f32)
    c = taps[4:5, :] + sum(
        taps[k : k + 1, :] * ubuf[HALO - 3 + k : HALO - 3 + k + tok_count, :] for k in range(K)
    )
    s = sigmoid(c)
    act = (c * s).astype(bf16)
    act_out[...] = act
    dact_out[...] = (s * (1.0 + c * (1.0 - s))).astype(bf16)

    @pl.when(step == 0)
    def _():
        bt[...] = act[:, :N].astype(f32).T.astype(bf16)

    @pl.when(step > 0)
    def _():
        group = step - 1
        dtg = spread_group(head_columns(dt_out[...], group))
        ecg = spread_group(head_columns(ecl[...], group))
        xt = (act.astype(f32) * dtg).astype(bf16)
        xw = (xt.astype(f32) * ecg).astype(bf16)
        state = nn(bt[...], xw)
        st_out[...] = state
        st_low[...] = state.astype(bf16)


def front(scal, tok, halo, gain, wu_own, wu_oth, taps, heads):
    tok_count, d = tok.shape
    half = wu_own.shape[1]
    ext = tok_count + HALO
    groups = CONV // GROUP
    first = groups - 1

    def col(j, *_):
        return (0, (j + first) % groups)

    weight = pl.BlockSpec((GROUP, half), lambda j, *_: ((j + first) % groups, 0))
    narrow = pl.BlockSpec((LANE, half), lambda j, *_: (CONV // LANE, 0))
    return call(
        front_kernel,
        (groups,),
        [
            const_spec((tok_count, d)),
            const_spec((HALO, d)),
            const_spec((1, d)),
            weight,
            weight,
            narrow,
            narrow,
            pl.BlockSpec((8, GROUP), col),
            const_spec((8, LANE)),
        ],
        [
            const_spec((ext, half)),
            const_spec((ext, half)),
            pl.BlockSpec((ext, GROUP), col),
            pl.BlockSpec((tok_count, GROUP), col),
            pl.BlockSpec((tok_count, GROUP), col),
            const_spec((tok_count, LANE)),
            const_spec((tok_count, LANE)),
            const_spec((tok_count, LANE)),
            const_spec((LANE, tok_count)),
            pl.BlockSpec((N, GROUP), lambda j, *_: (0, jnp.maximum(j - 1, 0))),
            pl.BlockSpec((N, GROUP), lambda j, *_: (0, jnp.maximum(j - 1, 0))),
        ],
        [
            jax.ShapeDtypeStruct((ext, half), bf16),
            jax.ShapeDtypeStruct((ext, half), bf16),
            jax.ShapeDtypeStruct((ext, CONV), bf16),
            jax.ShapeDtypeStruct((tok_count, CONV), bf16),
            jax.ShapeDtypeStruct((tok_count, CONV), bf16),
            jax.ShapeDtypeStruct((tok_count, LANE), f32),
            jax.ShapeDtypeStruct((tok_count, LANE), f32),
            jax.ShapeDtypeStruct((tok_count, LANE), f32),
            jax.ShapeDtypeStruct((LANE, tok_count), f32),
            jax.ShapeDtypeStruct((N, DIN), f32),
            jax.ShapeDtypeStruct((N, DIN), bf16),
        ],
        [
            pltpu.VMEM((ext, GROUP), f32),
            pltpu.VMEM((N, tok_count), bf16),
            pltpu.VMEM((tok_count, LANE), f32),
        ],
        2 * ext * d * (CONV + LANE),
        2 * (ext * d + d * CONV + 3 * ext * CONV),
        "front",
    )(scal, tok, halo, gain, wu_own, wu_oth, wu_own, wu_oth, taps, heads)


def intra_kernel(scal, x, bc, dt, cum, cumt, y_out, s0_out, scores, bt):
    group = pl.program_id(0)
    blocks = x.shape[0] // QB

    @pl.when(group == 0)
    def _():
        lower = iota((QB, QB), 0) >= iota((QB, QB), 1)
        bt[...] = bc[:, :N].astype(f32).T.astype(bf16)
        for q in range(blocks):
            rows = slice(q * QB, (q + 1) * QB)
            scores[q] = jnp.where(lower, nt(bc[rows, N:], bc[rows, :N]), 0.0)

    dtr = head_columns(dt[...], group)
    cumr = head_columns(cum[...], group)
    carry = jnp.zeros((N, GROUP), f32)
    for q in range(blocks):
        rows = slice(q * QB, (q + 1) * QB)
        cq = cumr[rows]
        end = cq[QB - 1 : QB]
        start = cumr[q * QB - 1 : q * QB] if q else jnp.zeros((1, LANE), f32)
        xt = (x[rows, :].astype(f32) * spread_group(dtr[rows])).astype(bf16)
        low_carry = carry.astype(bf16)
        s0_out[q] = low_carry
        ys = []
        for pair in range(2):
            mats = []
            for e in range(2):
                h = 2 * pair + e
                row = cumt[0, h : h + 1, rows]
                decay = jnp.exp(jnp.minimum(cq[:, h : h + 1] - row, 0.0))
                mats.append((decay * scores[q]).astype(bf16))
            ys.append(
                nn(
                    jnp.concatenate(mats, axis=1),
                    block_diag(xt[:, pair * LANE : (pair + 1) * LANE]),
                )
            )
        y = jnp.concatenate(ys, axis=1)
        if q:
            y = y + jnp.exp(spread_group(cq - start)) * nn(bc[rows, N:], low_carry)
        y_out[rows, :] = y
        if q < blocks - 1:
            xw = (xt.astype(f32) * jnp.exp(spread_group(end - cq))).astype(bf16)
            fresh = nn(bt[:, rows], xw)
            carry = fresh if q == 0 else fresh + carry * jnp.exp(spread_group(end - start))


def intra(scal, act, dt, cum, cumt):
    tok_count = act.shape[0]
    blocks = tok_count // QB
    groups = DIN // GROUP
    return call(
        intra_kernel,
        (groups,),
        [
            pl.BlockSpec((tok_count, GROUP), lambda j, *_: (0, j)),
            pl.BlockSpec((tok_count, GROUP), lambda j, *_: (0, groups)),
            const_spec((tok_count, LANE)),
            const_spec((tok_count, LANE)),
            pl.BlockSpec((1, 4, tok_count), lambda j, *_: (j, 0, 0)),
        ],
        [
            pl.BlockSpec((tok_count, GROUP), lambda j, *_: (0, j)),
            pl.BlockSpec((blocks, N, GROUP), lambda j, *_: (0, 0, j)),
        ],
        [
            jax.ShapeDtypeStruct((tok_count, DIN), f32),
            jax.ShapeDtypeStruct((blocks, N, DIN), bf16),
        ],
        [pltpu.VMEM((blocks, QB, QB), f32), pltpu.VMEM((N, tok_count), bf16)],
        2 * tok_count * DIN * 3 * N,
        8 * tok_count * DIN,
        "intra",
    )(scal, act, act, dt, cum, cumt)


def gate_kernel(
    scal, yloc, act, z, eg, cum, s_in, vecs,
    own_out, oth_out, ey_out, ez_out, r_loc, r_dev, dc_out, g_out, gs_out, g_low,
    pick, vbuf, ytbuf, ydbuf,
):
    step = pl.program_id(0)
    rows = yloc.shape[0]
    groups = DIN // GROUP
    per = groups // 2

    @pl.when(step == 0)
    def _():
        pick[...] = head_picker(DIN, 0)
        g_out[...] = jnp.zeros_like(g_out)
        gs_out[...] = jnp.zeros_like(gs_out)

    pos = iota((rows, 1), 0) + step * rows
    valid = ((pos >= scal[1]) & (pos < scal[2])).astype(f32)
    cq = cum[...]
    ecq = jnp.exp(cq)
    cmat = act[:, DIN + N :]
    ssq = jnp.zeros((rows, GROUP), f32)
    for g in range(groups):
        cols = slice(g * GROUP, (g + 1) * GROUP)
        eg_cum = jnp.concatenate([spread(ecq, 2 * g), spread(ecq, 2 * g + 1)], axis=1)
        yd = eg_cum * nn(cmat, s_in[:, cols])
        ydbuf[:, cols] = yd
        yt = yloc[:, cols] + yd + vecs[1:2, cols] * act[:, cols].astype(f32)
        ytbuf[:, cols] = yt
        zz = z[:, cols].astype(f32)
        v = yt * (zz * sigmoid(zz))
        vbuf[:, cols] = v
        ssq = ssq + v * v
    rs = lax.rsqrt(jnp.sum(ssq, axis=-1, keepdims=True) / DIN + EPS)
    mixed = jnp.zeros((rows, GROUP), f32)
    low_half = scal[0] == 0
    for i in range(per):
        local = slice(i * GROUP, (i + 1) * GROUP)
        outs = []
        for half in range(2):
            g = half * per + i
            cols = slice(g * GROUP, (g + 1) * GROUP)
            n = vbuf[:, cols] * rs
            vbuf[:, cols] = n
            gain = vecs[0:1, cols]
            outs.append((n * gain * valid).astype(bf16))
            e = eg[half ^ scal[0], :, local].astype(f32) * valid
            gs_out[0:1, cols] += jnp.sum(e * n, axis=0, keepdims=True)
            mixed = mixed + e * gain * n
        own_out[:, local] = jnp.where(low_half, outs[0], outs[1])
        oth_out[:, local] = jnp.where(low_half, outs[1], outs[0])
    m2 = jnp.sum(mixed, axis=-1, keepdims=True) / DIN
    rl = jnp.zeros((rows, LANE), f32)
    rd = jnp.zeros((rows, LANE), f32)
    dc = jnp.zeros((rows, N), f32)
    ct = cmat.astype(f32).T.astype(bf16)
    for g in range(groups):
        cols = slice(g * GROUP, (g + 1) * GROUP)
        n = vbuf[:, cols]
        side = (g // per) ^ scal[0]
        local = slice((g % per) * GROUP, (g % per + 1) * GROUP)
        e = eg[side, :, local].astype(f32) * valid
        ev = rs * (e * vecs[0:1, cols] - n * m2)
        zz = z[:, cols].astype(f32)
        sz = sigmoid(zz)
        ey = ev * (zz * sz)
        ez_out[:, cols] = (ev * ytbuf[:, cols] * (sz * (1.0 + zz * (1.0 - sz)))).astype(bf16)
        gs_out[1:2, cols] += jnp.sum(ey * act[:, cols].astype(f32), axis=0, keepdims=True)
        low = ey.astype(bf16)
        ey_out[:, cols] = low
        eyf = low.astype(f32)
        ph, pl_ = split_two(eyf * yloc[:, cols])
        rl = rl + nn(ph, pick[cols, :]) + nn(pl_, pick[cols, :])
        rd = rd + nn((eyf * ydbuf[:, cols]).astype(bf16), pick[cols, :])
        eg_cum = jnp.concatenate([spread(ecq, 2 * g), spread(ecq, 2 * g + 1)], axis=1)
        eye = (eyf * eg_cum).astype(bf16)
        g_out[:, cols] += nn(ct, eye)
        dc = dc + nt(eye, s_in[:, cols])
    r_loc[...] = rl
    r_dev[...] = rd
    dc_out[...] = dc

    @pl.when(step == pl.num_programs(0) - 1)
    def _():
        g_low[...] = g_out[...].astype(bf16)


def gate(scal, yloc, act, z, eg, cum, s_in, vecs):
    tok_count = act.shape[0]
    rows = QB

    def rowspec(width):
        return pl.BlockSpec((rows, width), lambda j, *_: (j, 0))

    def out(width, kind):
        return jax.ShapeDtypeStruct((tok_count, width), kind)

    sides = pl.BlockSpec((2, rows, DIN // 2), lambda j, *_: (0, j, 0))

    return call(
        gate_kernel,
        (tok_count // rows,),
        [
            rowspec(DIN),
            rowspec(CONV),
            rowspec(DIN),
            sides,
            rowspec(LANE),
            const_spec((N, DIN)),
            const_spec((8, DIN)),
        ],
        [
            rowspec(DIN // 2),
            rowspec(DIN // 2),
            rowspec(DIN),
            rowspec(DIN),
            rowspec(LANE),
            rowspec(LANE),
            rowspec(LANE),
            const_spec((N, DIN)),
            const_spec((8, DIN)),
            const_spec((N, DIN)),
        ],
        [
            out(DIN // 2, bf16),
            out(DIN // 2, bf16),
            out(DIN, bf16),
            out(DIN, bf16),
            out(LANE, f32),
            out(LANE, f32),
            out(LANE, f32),
            jax.ShapeDtypeStruct((N, DIN), f32),
            jax.ShapeDtypeStruct((8, DIN), f32),
            jax.ShapeDtypeStruct((N, DIN), bf16),
        ],
        [
            pltpu.VMEM((DIN, LANE), bf16),
            pltpu.VMEM((rows, DIN), f32),
            pltpu.VMEM((rows, DIN), f32),
            pltpu.VMEM((rows, DIN), f32),
        ],
        2 * tok_count * DIN * 6 * N,
        20 * tok_count * DIN,
        "gate",
    )(scal, yloc, act, z, eg, cum, s_in, vecs)


def back_kernel(
    scal, x, bc, dt, cum, cumt, ey, s0,
    dxt_out, db_out, dc_out, r2_out, cq_out,
    scores, dscores, ct,
):
    group = pl.program_id(0)
    last = pl.num_programs(0) - 1
    blocks = x.shape[0] // QB
    upper = iota((QB, QB), 0) <= iota((QB, QB), 1)

    @pl.when(group == 0)
    def _():
        ct[...] = bc[:, N:].astype(f32).T.astype(bf16)
        for q in range(blocks):
            rows = slice(q * QB, (q + 1) * QB)
            scores[q] = jnp.where(upper, nt(bc[rows, :N], bc[rows, N:]), 0.0)
        dscores[...] = jnp.zeros_like(dscores)
        db_out[...] = jnp.zeros_like(db_out)
        dc_out[...] = jnp.zeros_like(dc_out)
        r2_out[...] = jnp.zeros_like(r2_out)
        cq_out[...] = jnp.zeros_like(cq_out)

    dtr = head_columns(dt[...], group)
    cumr = head_columns(cum[...], group)
    picks = [head_picker(LANE, 4 * group + 2 * pair) for pair in range(2)]
    picks2 = [jnp.concatenate([p, p], axis=0) for p in picks]
    pick_all = head_picker(GROUP, 4 * group).astype(f32)
    carry = None
    for q in reversed(range(blocks)):
        rows = slice(q * QB, (q + 1) * QB)
        cq = cumr[rows]
        end = cq[QB - 1 : QB]
        start = cumr[q * QB - 1 : q * QB] if q else jnp.zeros((1, LANE), f32)
        xt = (x[rows, :].astype(f32) * spread_group(dtr[rows])).astype(bf16)
        eyq = ey[rows, :]
        dxs = []
        ds = jnp.zeros((QB, QB), f32)
        for pair in range(2):
            lanes = slice(pair * LANE, (pair + 1) * LANE)
            eybd = block_diag(eyq[:, lanes])
            dm = nt(xt[:, lanes], eybd)
            mats = []
            for e in range(2):
                h = 2 * pair + e
                row = cumt[0, h : h + 1, rows]
                decay = jnp.exp(jnp.minimum(row - cq[:, h : h + 1], 0.0))
                mats.append((decay * scores[q]).astype(bf16))
                ds = ds + decay * dm[:, e * QB : (e + 1) * QB]
            dxs.append(nn(jnp.concatenate(mats, axis=1), eybd))
        dscores[q] += ds
        dx = jnp.concatenate(dxs, axis=1)
        xtf = xt.astype(f32)
        eye = None
        if q:
            eye = (eyq.astype(f32) * jnp.exp(spread_group(cq - start))).astype(bf16)
            dc_out[rows, :] += nt(eye, s0[q])
        if carry is not None:
            low = carry.astype(bf16)
            ecl = jnp.exp(spread_group(end - cq))
            dst = ecl * nn(bc[rows, :N], low)
            db_out[rows, :] += nt((xtf * ecl).astype(bf16), low)
            total = jnp.exp(spread_group(end - start))
            vec = jnp.sum(xtf * dst, axis=0, keepdims=True)
            if q:
                vec = vec + total * jnp.sum(carry * s0[q].astype(f32), axis=0, keepdims=True)
            cq_out[q : q + 1, :] += exact_nn(jnp.broadcast_to(vec, (8, GROUP)), pick_all)[0:1]
            dx = dx + dst
        if q:
            fresh = nn(ct[:, rows], eye)
            carry = fresh if carry is None else fresh + total * carry
        dxt_out[rows, :] = dx.astype(bf16)
        prod = xtf * dx
        acc = jnp.zeros((QB, LANE), f32)
        for pair in range(2):
            ph, pl_ = split_two(prod[:, pair * LANE : (pair + 1) * LANE])
            acc = acc + nn(jnp.concatenate([ph, pl_], axis=1), picks2[pair])
        r2_out[rows, :] += acc

    @pl.when(group == last)
    def _():
        for q in range(blocks):
            rows = slice(q * QB, (q + 1) * QB)
            ds = jnp.where(upper, dscores[q], 0.0)
            db_out[rows, :] += nn(ds.astype(bf16), bc[rows, N:])
            dc_out[rows, :] += nn(ds.T.astype(bf16), bc[rows, :N])


def back(scal, act, dt, cum, cumt, ey, s0):
    tok_count = act.shape[0]
    blocks = tok_count // QB
    groups = DIN // GROUP
    wide = pl.BlockSpec((tok_count, GROUP), lambda j, *_: (0, j))
    small = const_spec((tok_count, LANE))
    return call(
        back_kernel,
        (groups,),
        [
            wide,
            pl.BlockSpec((tok_count, GROUP), lambda j, *_: (0, groups)),
            small,
            small,
            pl.BlockSpec((1, 4, tok_count), lambda j, *_: (j, 0, 0)),
            wide,
            pl.BlockSpec((blocks, N, GROUP), lambda j, *_: (0, 0, j)),
        ],
        [wide, small, small, small, const_spec((8, LANE))],
        [
            jax.ShapeDtypeStruct((tok_count, DIN), bf16),
            jax.ShapeDtypeStruct((tok_count, LANE), f32),
            jax.ShapeDtypeStruct((tok_count, LANE), f32),
            jax.ShapeDtypeStruct((tok_count, LANE), f32),
            jax.ShapeDtypeStruct((8, LANE), f32),
        ],
        [
            pltpu.VMEM((blocks, QB, QB), f32),
            pltpu.VMEM((blocks, QB, QB), f32),
            pltpu.VMEM((N, tok_count), bf16),
        ],
        2 * tok_count * DIN * 8 * N,
        8 * tok_count * DIN,
        "back",
    )(scal, act, act, dt, cum, cumt, ey, s0)


def tail_kernel(
    scal, act, bc, dact, u, ey, dxt, taps, dt, sg, cum, g_in, s_in, skip, heads,
    db_loc, dc_loc, dc_dev, r_loc, r_dev, r2, cq,
    *rest,
):
    chunks = rest[: CHUNKS + 1]
    gconv, ghead, ebuf, ubuf, p_acc, d_acc, db_acc, gs_acc = rest[CHUNKS + 1 :]
    eu_out = chunks[-1]
    step = pl.program_id(0)
    last = pl.num_programs(0) - 2
    tok_count = act.shape[0]
    ext = tok_count + HALO
    lo = scal[1]
    hi = scal[2]

    @pl.when(step == 0)
    def _():
        p_acc[...] = jnp.zeros_like(p_acc)
        d_acc[...] = jnp.zeros_like(d_acc)
        db_acc[...] = jnp.zeros_like(db_acc)
        gs_acc[...] = jnp.zeros_like(gs_acc)
        ebuf[...] = jnp.zeros_like(ebuf)

    bmat = bc[:, :N]

    @pl.when(step < last)
    def _():
        cumr = head_columns(cum[...], step)
        dtr = spread_group(head_columns(dt[...], step))
        xf = act[...].astype(f32)
        xtf = (xf * dtr).astype(bf16).astype(f32)
        low = g_in[...]
        end = cumr[tok_count - 1 : tok_count]
        ecl = jnp.exp(spread_group(end - cumr))
        dxd = ecl * nn(bmat, low)
        dx = dxt[...].astype(f32) + dxd
        pick = head_picker(GROUP, 4 * step)
        p_acc[...] += nn((xtf * dxd).astype(bf16), pick)
        d_acc[...] += nn((xf * dx).astype(bf16), pick)
        db_acc[...] += nt((xtf * ecl).astype(bf16), low)
        vec = jnp.sum(low.astype(f32) * s_in[...].astype(f32), axis=0, keepdims=True)
        vec = vec * jnp.exp(spread_group(end))
        gs_acc[...] += exact_nn(jnp.broadcast_to(vec, (8, GROUP)), pick.astype(f32))
        ebuf[HALO : HALO + tok_count, :] = (
            dtr * dx + skip[1:2, :] * ey[...].astype(f32)
        ) * dact[...].astype(f32)

    @pl.when(step == last)
    def _():
        ebuf[HALO : HALO + tok_count, :N] = (db_loc[...] + db_acc[...]) * dact[:, :N].astype(f32)
        ebuf[HALO : HALO + tok_count, N:] = (dc_loc[...] + dc_dev[...]) * dact[:, N:].astype(f32)

    @pl.when(step > last)
    def _():
        rate = heads[1:2, :]
        upper = (iota((QB, QB), 0) <= iota((QB, QB), 1)).astype(f32)
        strict = (iota((QB, QB), 0) > iota((QB, QB), 1)).astype(f32)
        blocks = tok_count // QB
        devs = jnp.zeros((1, LANE), f32)
        suffix = [None] * blocks
        for q in reversed(range(blocks)):
            rows = slice(q * QB, (q + 1) * QB)
            within = exact_nn(upper, r_loc[rows, :] - r2[rows, :]) + cq[q : q + 1, :]
            dev = exact_nn(upper, r_dev[rows, :]) + devs
            devs = dev[0:1]
            suffix[q] = within + dev
        before = gs_acc[0:1, :]
        glog = jnp.zeros((1, LANE), f32)
        gdt = jnp.zeros((1, LANE), f32)
        eu_out[...] = jnp.zeros_like(eu_out)
        for q in range(blocks):
            rows = slice(q * QB, (q + 1) * QB)
            pq = p_acc[rows, :]
            eda = suffix[q] + exact_nn(strict, pq) + before
            before = before + jnp.sum(pq, axis=0, keepdims=True)
            er = (d_acc[rows, :] + rate * eda) * sg[rows, :]
            gdt = gdt + jnp.sum(er, axis=0, keepdims=True)
            glog = glog + rate * jnp.sum(dt[rows, :] * eda, axis=0, keepdims=True)
            eu_out[HALO + q * QB : HALO + (q + 1) * QB, :LANE] = er.astype(bf16)
        ghead[...] = jnp.concatenate([gdt, glog, jnp.zeros((6, LANE), f32)], axis=0)

    @pl.when(step <= last)
    def _():
        ubuf[...] = u[...].astype(f32)
        ec = ebuf[HALO : HALO + tok_count, :]
        gs = [
            jnp.sum(ec * ubuf[HALO - 3 + k : HALO - 3 + k + tok_count, :], axis=0, keepdims=True)
            for k in range(K)
        ]
        gs.append(jnp.sum(ec, axis=0, keepdims=True))
        gs.append(jnp.zeros((3, ec.shape[1]), f32))
        gconv[...] = jnp.concatenate(gs, axis=0)
        eu = sum(taps[k : k + 1, :] * ebuf[3 - k : 3 - k + ext, :] for k in range(K))
        pos = iota(eu.shape, 0) - HALO
        eu = jnp.where((pos >= lo) & (pos < hi), eu, 0.0).astype(bf16)
        for c, chunk in enumerate(chunks):
            @pl.when(step // 2 == c)
            def _():
                chunk[...] = eu


def tail(scal, act, dact, u, ey, dxt, taps, dt, sg, cum, g_in, s_in, skip, heads, smalls):
    tok_count = act.shape[0]
    ext = tok_count + HALO
    groups = DIN // GROUP

    def col(j, *_):
        return (0, jnp.minimum(j, groups))

    def colx(j, *_):
        return (0, jnp.minimum(j, groups - 1))

    def chunk(c):
        return pl.BlockSpec((ext, GROUP), lambda j, *_: (0, jnp.clip(j - 2 * c, 0, 1)))

    wide = pl.BlockSpec((tok_count, GROUP), col)
    widex = pl.BlockSpec((tok_count, GROUP), colx)
    small = const_spec((tok_count, LANE))
    return call(
        tail_kernel,
        (groups + 2,),
        [
            wide,
            pl.BlockSpec((tok_count, GROUP), lambda j, *_: (0, groups)),
            wide,
            pl.BlockSpec((ext, GROUP), col),
            widex,
            widex,
            pl.BlockSpec((8, GROUP), col),
            small,
            small,
            small,
            pl.BlockSpec((N, GROUP), colx),
            pl.BlockSpec((N, GROUP), colx),
            pl.BlockSpec((8, GROUP), lambda j, *_: (0, jnp.minimum(j, groups - 1))),
            const_spec((8, LANE)),
            small,
            small,
            small,
            small,
            small,
            small,
            const_spec((8, LANE)),
        ],
        [
            *[chunk(c) for c in range(CHUNKS + 1)],
            pl.BlockSpec((8, GROUP), col),
            const_spec((8, LANE)),
        ],
        [
            *[jax.ShapeDtypeStruct((ext, 2 * GROUP), bf16)] * (CHUNKS + 1),
            jax.ShapeDtypeStruct((8, CONV), f32),
            jax.ShapeDtypeStruct((8, LANE), f32),
        ],
        [
            pltpu.VMEM((ext + HALO, GROUP), f32),
            pltpu.VMEM((ext, GROUP), f32),
            pltpu.VMEM((tok_count, LANE), f32),
            pltpu.VMEM((tok_count, LANE), f32),
            pltpu.VMEM((tok_count, LANE), f32),
            pltpu.VMEM((8, LANE), f32),
        ],
        2 * tok_count * DIN * 4 * N,
        12 * tok_count * DIN,
        "tail",
    )(
        scal, act, act, dact, u, ey, dxt, taps, dt, sg, cum, g_in, s_in, skip, heads, *smalls
    )


def gate_proj_kernel(scal, a_own, a_oth, w_own, w_oth, out):
    out[...] = (
        nt(a_own[HALO:, :], w_own[...]) + nt(a_oth[HALO:, :], w_oth[...])
    ).astype(bf16)


def gate_proj(scal, n_own, n_oth, wz_own, wz_oth):
    ext, half = n_own.shape
    rows = ext - HALO
    wide = 2 * GROUP
    weight = pl.BlockSpec((wide, half), lambda j, *_: (j, 0))
    return call(
        gate_proj_kernel,
        (DIN // wide,),
        [const_spec((ext, half)), const_spec((ext, half)), weight, weight],
        pl.BlockSpec((rows, wide), lambda j, *_: (0, j)),
        jax.ShapeDtypeStruct((rows, DIN), bf16),
        [],
        4 * rows * half * DIN,
        4 * DIN * half,
        "gate_proj",
    )(scal, n_own, n_oth, wz_own, wz_oth)


def grad_gated_kernel(scal, e, w_own, w_oth, out):
    out[0] = nt(e[...], w_own[...]).astype(bf16)
    out[1] = nt(e[...], w_oth[...]).astype(bf16)


def grad_gated(scal, e, wo_own, wo_oth):
    rows, d = e.shape
    half = wo_own.shape[0]
    weight = pl.BlockSpec((GROUP, d), lambda j, *_: (j, 0))
    return call(
        grad_gated_kernel,
        (half // GROUP,),
        [const_spec((rows, d)), weight, weight],
        pl.BlockSpec((2, rows, GROUP), lambda j, *_: (0, 0, j)),
        jax.ShapeDtypeStruct((2, rows, half), bf16),
        [],
        4 * rows * half * d,
        4 * d * half,
        "grad_gated",
    )(scal, e, wo_own, wo_oth)


def out_proj_kernel(scal, a_own, a_oth, w_own, w_oth, tok, out):
    total = tok[...].astype(f32) + nn(a_own[...], w_own[...]) + nn(a_oth[...], w_oth[...])
    out[...] = total.astype(bf16)


def out_proj(scal, g_own, g_oth, wo_own, wo_oth, tok):
    rows, d = tok.shape
    half = wo_own.shape[0]
    wide = 2 * GROUP
    weight = pl.BlockSpec((half, wide), lambda j, *_: (0, j))
    cols = pl.BlockSpec((rows, wide), lambda j, *_: (0, j))
    return call(
        out_proj_kernel,
        (d // wide,),
        [const_spec(g_own.shape), const_spec(g_oth.shape), weight, weight, cols],
        cols,
        jax.ShapeDtypeStruct((rows, d), bf16),
        [],
        4 * rows * half * d,
        4 * d * half,
        "out_proj",
    )(scal, g_own, g_oth, wo_own, wo_oth, tok)


def input_back_kernel(
    scal, ez, wz_own, wz_oth, wu_own, wu_oth, tok, halo, up, gain, *rest
):
    chunks = rest[: CHUNKS + 1]
    grad_out, edge_out, gain_out, acc = rest[CHUNKS + 1 :]
    step = pl.program_id(0)
    per = pl.num_programs(0) // 2
    half = acc.shape[1] // 2
    side = jnp.where(step < per, scal[0], 1 - scal[0])
    place = pl.ds(pl.multiple_of(side * half + lax.rem(step, per) * GROUP, GROUP), GROUP)

    def fill(wz, wu):
        deep = chunks[0].shape[1]
        part = sum(nn(e[...], wu[c * deep : (c + 1) * deep]) for c, e in enumerate(chunks))
        acc[0:HALO, place] = part[0:HALO]
        acc[HALO:, place] = part[HALO:] + nn(ez[...], wz[...])

    @pl.when(step < per)
    def _():
        fill(wz_own, wu_own)

    @pl.when(step >= per)
    def _():
        fill(wz_oth, wu_oth)

    def norm_back(x, rows):
        rs = lax.rsqrt(jnp.mean(x * x, axis=-1, keepdims=True) + EPS)
        unit = x * rs
        en = acc[rows, :]
        scaled = en * gain[...]
        gain_out[0:1, :] += jnp.sum(en * unit, axis=0, keepdims=True)
        return rs * (scaled - unit * jnp.mean(scaled * unit, axis=-1, keepdims=True))

    @pl.when(step == 2 * per - 1)
    def _():
        gain_out[...] = jnp.zeros_like(gain_out)
        edge_out[...] = norm_back(halo[...].astype(f32), pl.ds(0, HALO))

        def body(i, carry):
            rows = pl.ds(pl.multiple_of(i * 64, 64), 64)
            ext_rows = pl.ds(pl.multiple_of(i * 64 + HALO, 16), 64)
            grad_out[rows, :] = up[rows, :].astype(f32) + norm_back(
                tok[rows, :].astype(f32), ext_rows
            )
            return carry

        lax.fori_loop(0, tok.shape[0] // 64, body, 0)


def input_back(scal, ez, eu, wz_own, wz_oth, wu_own, wu_oth, tok, halo, up, gain):
    rows, d = tok.shape
    ext = rows + HALO
    half = wz_own.shape[1]
    per = half // GROUP

    def own(depth):
        return pl.BlockSpec((depth, GROUP), lambda j, *_: (0, jnp.minimum(j, per - 1)))

    def oth(depth):
        return pl.BlockSpec((depth, GROUP), lambda j, *_: (0, jnp.maximum(j - per, 0)))

    zd = wz_own.shape[0]
    ud = wu_own.shape[0]
    return call(
        input_back_kernel,
        (2 * per,),
        [
            const_spec(ez.shape),
            own(zd),
            oth(zd),
            own(ud),
            oth(ud),
            const_spec((rows, d)),
            const_spec((HALO, d)),
            const_spec((rows, d)),
            const_spec((1, d)),
            *[const_spec(e.shape) for e in eu],
        ],
        [const_spec((rows, d)), const_spec((HALO, d)), const_spec((8, d))],
        [
            pltpu.HBM((rows, d), f32),
            jax.ShapeDtypeStruct((HALO, d), f32),
            jax.ShapeDtypeStruct((8, d), f32),
        ],
        [pltpu.VMEM((ext, d), f32)],
        2 * ext * d * (zd + ud),
        2 * d * (zd + ud) + 8 * rows * d,
        "input_back",
    )(scal, ez, wz_own, wz_oth, wu_own, wu_oth, tok, halo, up, gain, *eu)


SIDE = 4


def place_blocks(groups, base, group, parts, rows):
    where = group ^ (base // SIDE)
    within = lax.rem(base, SIDE)
    for k in range(SIDE):
        @pl.when(where == k)
        def _():
            for i, part in enumerate(parts):
                for span, value in zip(rows, part):
                    groups[k][i ^ within, span, :] = value


def outer_ab_kernel(scal, a1, a2, ra1, ra2, b1, b2, rb1, rb2, *groups):
    step = pl.program_id(0)
    base = scal[3]
    width = groups[0].shape[2]
    high = a1.shape[1] // SIDE
    deep = b1.shape[1] // SIDE

    @pl.when(step < SIDE)
    def _():
        low = (tn(a1[...], ra1[...]) + tn(a2[...], ra2[...])).astype(bf16)
        parts = [
            (low[i * high : (i + 1) * high, :width], low[i * high : (i + 1) * high, width:])
            for i in range(SIDE)
        ]
        place_blocks(groups, base, step, parts, [slice(0, high), slice(high, 2 * high)])

    @pl.when(step >= SIDE)
    def _():
        low = (tn(b1[...], rb1[HALO:, :]) + tn(b2[...], rb2[HALO:, :])).astype(bf16)
        parts = [(low[i * deep : (i + 1) * deep],) for i in range(SIDE)]
        place_blocks(groups, base, step - SIDE, parts, [slice(2 * high, 2 * high + deep)])


def outer_ab(scal, a1, a2, ra1, ra2, b1, b2, rb1, rb2):
    toks = a1.shape[0]
    width = rb1.shape[1]
    a_cols = a1.shape[1] // SIDE
    b_cols = b1.shape[1] // SIDE
    shape = (SIDE, 2 * a_cols // SIDE + b_cols // SIDE, width)
    a_spec = pl.BlockSpec((toks, a_cols), lambda j, *_: (0, jnp.minimum(j, SIDE - 1)))
    b_spec = pl.BlockSpec((toks, b_cols), lambda j, *_: (0, jnp.maximum(j - SIDE, 0)))
    return call(
        outer_ab_kernel,
        (2 * SIDE,),
        [
            a_spec,
            a_spec,
            const_spec(ra1.shape),
            const_spec(ra2.shape),
            b_spec,
            b_spec,
            const_spec(rb1.shape),
            const_spec(rb2.shape),
        ],
        [const_spec(shape)] * SIDE,
        [jax.ShapeDtypeStruct(shape, bf16)] * SIDE,
        [],
        8 * toks * a1.shape[1] * ra1.shape[1],
        10**7,
        "outer_ab",
    )(scal, a1, a2, ra1, ra2, b1, b2, rb1, rb2)


def outer_c_kernel(scal, *rest):
    mine = rest[: CHUNKS + 1]
    other = rest[CHUNKS + 1 : 2 * CHUNKS + 2]
    r1, r2 = rest[2 * CHUNKS + 2 : 2 * CHUNKS + 4]
    groups = rest[2 * CHUNKS + 4 : 2 * CHUNKS + 4 + SIDE]
    base = scal[3]
    within = lax.rem(base, SIDE)
    offset = 0
    for c in range(CHUNKS + 1):
        acc = tn(mine[c][...], r1[...]) + tn(other[c][...], r2[...])
        low = acc.astype(bf16)
        height = (low.shape[0] if c < CHUNKS else 2 * N) // BLOCKS
        span = slice(offset, offset + height)
        offset += height
        for k in range(SIDE):
            @pl.when(base // SIDE == k)
            def _():
                for t in range(BLOCKS):
                    groups[(t // SIDE) ^ k][(t % SIDE) ^ within, span, :] = low[
                        t * height : (t + 1) * height
                    ]
    rest[-1][...] = acc[2 * N : 2 * N + H]


def outer_c(scal, mine, other, r1, r2):
    toks, width = r1.shape
    shape = (SIDE, CONV // BLOCKS, width)
    args = [*mine, *other, r1, r2]
    return call(
        outer_c_kernel,
        (1,),
        [const_spec(a.shape) for a in args],
        [const_spec(shape)] * SIDE + [const_spec((H, width))],
        [jax.ShapeDtypeStruct(shape, bf16)] * SIDE + [jax.ShapeDtypeStruct((H, width), f32)],
        [],
        4 * toks * CONV * width,
        10**7,
        "outer_c",
    )(scal, *args)


def own_copies(kernel, args, outs, scratch, aliases, name):
    return pl.pallas_call(
        kernel,
        grid_spec=pltpu.PrefetchScalarGridSpec(
            num_scalar_prefetch=1,
            grid=(1,),
            in_specs=[pl.BlockSpec(memory_space=pl.ANY)] * (len(args) - 1),
            out_specs=[pl.BlockSpec(memory_space=pl.ANY)] * len(outs),
            scratch_shapes=scratch,
        ),
        out_shape=outs,
        input_output_aliases=aliases,
        compiler_params=params(1),
        cost_estimate=pl.CostEstimate(flops=0, bytes_accessed=10**4, transcendentals=0),
        name=name,
    )(*args)


def unload(scal, ab, c, first, targets, shapes, rates, name):
    _, rows_ab, width = ab[0].shape
    rows_c = c[0].shape[1]
    half_in, d = shapes[0]
    high = half_in // BLOCKS
    deep = DIN // BLOCKS
    tall = DIN // (CHUNKS * BLOCKS)
    pieces = [(DIN + i * tall * BLOCKS, tall, i * tall) for i in range(CHUNKS)]
    pieces.append((DIN + CONV - 2 * N, 2 * N // BLOCKS, CHUNKS * tall))
    count = len(ab)
    blocks = sum(p.shape[0] for p in ab)
    extra = [rates] if rates is not None else []
    skip = 2 * count + len(extra) + len(targets)

    def kernel(scal, *refs):
        out_a, out_b, ab_buf, c_buf, wide_a, wide_b, wide_c, in_sems, sems = refs[skip:]
        stores = []

        def send(src, dst, sem):
            store = pltpu.make_async_copy(src, dst, sem)
            store.start()
            stores.append(store)

        def rows_at(ref, start, t, size):
            return ref.at[pl.ds(pl.multiple_of(start + t * size, size), size), :]

        loads = []
        row = 0
        for i in range(count):
            n = ab[i].shape[0]
            for j, (src, buf) in enumerate(((refs[i], ab_buf), (refs[count + i], c_buf))):
                load = pltpu.make_async_copy(src, buf.at[pl.ds(row, n)], in_sems.at[j, i])
                load.start()
                loads.append((load, j, row, n))
            row += n
        if extra:
            send(refs[2 * count], out_b.at[pl.ds(DIN + CONV, H), :], sems.at[blocks, 0])
        for load, kind, row, n in loads:
            load.wait()
            for p in range(row, row + n):
                t = (first + p) ^ scal[3]
                if kind == 0:
                    wide_a[p, :, 0:width] = ab_buf[p, 0:high].astype(f32)
                    wide_a[p, :, width:] = ab_buf[p, high : 2 * high].astype(f32)
                    wide_b[p] = ab_buf[p, 2 * high :].astype(f32)
                    send(wide_a.at[p], rows_at(out_a, 0, t, high), sems.at[p, 0])
                    send(wide_b.at[p], rows_at(out_b, 0, t, deep), sems.at[p, 1])
                    continue
                wide_c[p] = c_buf[p].astype(f32)
                for i, (start, height, inner) in enumerate(pieces):
                    send(
                        wide_c.at[p, pl.ds(inner, height)],
                        rows_at(out_b, start, t, height),
                        sems.at[p, 2 + i],
                    )
        for store in stores:
            store.wait()

    args = [scal, *ab, *c, *extra, *targets]
    return own_copies(
        kernel,
        args,
        [jax.ShapeDtypeStruct(shape, f32) for shape in shapes],
        [
            pltpu.VMEM((blocks, rows_ab, width), bf16),
            pltpu.VMEM((blocks, rows_c, width), bf16),
            pltpu.VMEM((blocks, high, d), f32),
            pltpu.VMEM((blocks, deep, width), f32),
            pltpu.VMEM((blocks, rows_c, width), f32),
            pltpu.SemaphoreType.DMA((2, count)),
            pltpu.SemaphoreType.DMA((blocks + 1, 2 + len(pieces))),
        ],
        {len(args) - 2 + i: i for i in range(len(targets))},
        name,
    )


def swap(x):
    return lax.ppermute(x, "fsdp", [(0, 1), (1, 0)])


def shifted(x, by):
    length = lax.axis_size("tm")
    return lax.ppermute(x, "tm", [(i, (i + by) % length) for i in range(length)])


def across(x, axis, mask):
    return lax.ppermute(x, axis, [(i, i ^ mask) for i in range(lax.axis_size(axis))])


def after(value, *deps):
    return lax.optimization_barrier((value, *deps))[0]


def sum_low(values):
    return sum(v.astype(f32) for v in values).astype(bf16)


def exchange_corner(groups):
    half = SIDE // 2
    return across(groups[3][:half], "rep", 2), across(groups[3][half:], "rep", 1)


def exchange_sides(groups, corner, *cover):
    half = SIDE // 2
    lo, hi = corner
    first = after(groups[1], *cover)
    by_x = jnp.concatenate([sum_low([first[:half], lo]), first[half:]])
    by_y = jnp.concatenate([groups[2][:half], sum_low([groups[2][half:], hi])])
    return across(by_x, "rep", 1), across(by_y, "rep", 2)


def sum_parts(own, got, *cover):
    every = [after(own, *cover), *got]
    return [sum_low([g[m] for g in every]) for m in range(SIDE)]


def reduce_times(parts, *cover):
    got = [across(parts[m], "tm", m) for m in range(1, SIDE)]
    piece = sum_low([after(parts[0], *cover), *got])
    for axis in ("rep", "tm"):
        bit = SIDE
        while bit < lax.axis_size(axis):
            piece = sum_low([piece, across(piece, axis, bit)])
            bit *= 2
    return piece


def gather_times(piece, *cover):
    got = [across(piece, "tm", m) for m in range(1, SIDE)]
    return jnp.stack([after(piece, *cover), *got])


def gather_replicas(near):
    by_x = across(near, "rep", 1)
    by_y = across(near, "rep", 2)
    return by_x, by_y


def gather_corner(by_x, by_y):
    return across(by_x[: SIDE // 2], "rep", 2), across(by_y[SIDE // 2 :], "rep", 1)


def chain(local, low, total, logs, by, *cover):
    size = lax.axis_size("tm")
    tm = lax.axis_index("tm")

    def widen(row):
        return jnp.exp(jnp.repeat(row[0, :H], P_SIZE))[None]

    def moved(v, hops):
        return shifted(v, by * hops)

    def inside(v, hops):
        outside = tm < hops if by > 0 else tm >= size - hops
        return jnp.where(outside, 0.0, v.astype(f32))

    def inclusive(held):
        return (local + total * held).astype(bf16)

    first = moved(low, 1)
    reach = moved(logs, 1)
    total = after(total, *cover)
    held = inside(first, 1)
    sent = inclusive(held)
    got = moved(sent, 2)

    def finish(*cover):
        nonlocal held, got, reach
        span = 1
        reach = after(reach, *cover)
        while True:
            held = held + widen(reach) * inside(got, span + 1)
            if 2 * span + 1 >= size - 1:
                return held.astype(bf16)
            reach = reach + moved(logs + reach, span + 1)
            span = 2 * span + 1
            got = moved(inclusive(held), span + 1)

    return sent, finish


def body(
    tokens, in_weight, out_weight, norm_gain, conv_weight, conv_bias, dt_bias, a_log,
    d_skip, gate_gain, lengths, starts, cotangent,
):
    core = lax.axis_index("fsdp")
    tm = lax.axis_index("tm")
    tm_size = lax.axis_size("tm")
    tok = tokens[0]
    upstream = cotangent[0]
    tok_count, d = tok.shape
    half_d = in_weight.shape[0]
    half_in = out_weight.shape[0]
    half_conv = conv_bias.shape[0]
    half_heads = dt_bias.shape[0]

    lo = starts[0] - tm * tok_count
    scal = jnp.stack(
        [
            core,
            lo,
            lo + lengths[0],
            SIDE * (lax.axis_index("rep") % SIDE) + tm % SIDE,
        ]
    ).astype(jnp.int32)

    def fill(v):
        return [v, jnp.zeros((half_conv - v.shape[0],), f32)]

    pack = jnp.concatenate(
        [conv_weight.reshape(-1), conv_bias]
        + fill(gate_gain)
        + fill(norm_gain)
        + [dt_bias, a_log, d_skip, jnp.zeros((half_conv - 3 * half_heads,), f32)]
    )
    pack = pack.reshape(8, half_conv)
    pack_oth = swap(pack)
    edge_tok = tok[tok_count - HALO :]
    halo = shifted(edge_tok, 1)
    w_t = after(in_weight.T, edge_tok)
    wu_own = jnp.pad(w_t[DIN:], ((0, GROUP - H), (0, 0))).astype(bf16)
    wu_oth = swap(wu_own)
    taps, vecs, heads, gain = pack_vectors(scal, pack, pack_oth, d)
    wz_own = w_t[:DIN].astype(bf16)
    wz_oth = swap(wz_own)
    wo_own = after(out_weight, wu_own).astype(bf16)
    wo_oth = swap(wo_own)
    up_oth = swap(upstream)

    n_own, n_oth, u, act, dact, dt, sg, cum, cumt, st, st_low = front(
        scal, tok, halo, gain, after(wu_own, wz_own, wo_own), wu_oth, taps, heads
    )
    n_got = swap(n_oth)
    cumt = cumt[:H].reshape(H // 4, 4, tok_count)
    total = jnp.exp(jnp.repeat(cum[tok_count - 1, :H], P_SIZE))[None]

    logs = cum[tok_count - 1 :]
    eg = grad_gated(scal, upstream, wo_own, wo_oth)
    sent, finish = chain(st, st_low, total, logs, 1, eg)
    z = gate_proj(scal, after(n_own, sent), n_oth, wz_own, wz_oth)
    yloc, s0 = intra(scal, after(act, z), dt, cum, cumt)
    s_in = finish(yloc)
    g_own, g_oth, ey, ez, r_loc, r_dev, dc_dev, g_loc, gs, g_low = gate(
        scal, yloc, act, z, eg, cum, s_in, vecs
    )

    gated_got = swap(g_oth)
    ez_got = swap(ez)
    ab = outer_ab(scal, g_own, gated_got, upstream, up_oth, ez, ez_got, n_own, n_got)
    sent, finish = chain(g_loc, g_low, total, logs, -1, ab[0])
    dxt, db_loc, dc_loc, r2, cq = back(scal, after(act, sent), dt, cum, cumt, ey, s0)
    g_in = finish(dxt)
    ab_corner = exchange_corner(ab)
    ab_got = exchange_sides(ab, ab_corner, dxt)
    *eu, gconv, ghead = tail(
        scal, after(act, *ab_corner), dact, u, ey, dxt, taps, dt, sg, cum, g_in, s_in, vecs, heads,
        (db_loc, dc_loc, dc_dev, r_loc, r_dev, r2, cq),
    )
    eu_got = [swap(e) for e in eu]
    ab_parts = sum_parts(ab[0], ab_got, gconv)
    *c, g_rates = outer_c(scal, eu, eu_got, after(n_own, *ab_parts), n_got)
    c_corner = exchange_corner(c)
    grad_in, edge, ggain = input_back(
        scal, ez, eu, wz_own, wz_oth, wu_own, wu_oth, after(tok, c[0]), halo, upstream, gain
    )
    grad_skip = jnp.sum(gs[1].reshape(H, P_SIZE), axis=1)

    def side(v, half):
        return jnp.stack([v[:half], v[half : 2 * half]])

    def slot(v, half):
        return jnp.pad(side(v, half), ((0, 0), (0, half_conv - half)))[:, None]

    head_grads = jnp.stack([ghead[0, :H], ghead[1, :H], grad_skip])
    head_sides = jnp.stack(
        [head_grads[:, :half_heads].reshape(-1), head_grads[:, half_heads:].reshape(-1)]
    )
    packed = jnp.concatenate(
        [
            gconv[:5].reshape(5, 2, half_conv).transpose(1, 0, 2),
            slot(gs[0], half_in),
            slot(ggain[0], half_d),
            jnp.pad(head_sides, ((0, 0), (0, half_conv - 3 * half_heads)))[:, None],
        ],
        axis=1,
    )
    c_got = exchange_sides(c, c_corner, packed)
    ab_piece = reduce_times(ab_parts, packed)
    output = out_proj(scal, g_own, g_oth, wo_own, wo_oth, after(tok, ab_piece))
    c_parts = sum_parts(c[0], c_got, output)
    ab_near = gather_times(ab_piece, *c_parts)
    packed = after(packed, *c_corner)
    own = lax.dynamic_index_in_dim(packed, core, 0, keepdims=False)
    small = own + swap(lax.dynamic_index_in_dim(packed, 1 - core, 0, keepdims=False))
    small = jnp.concatenate([small, g_rates.reshape(8, -1)], axis=1)

    def total_over(v, axis):
        v = v + sum(across(v, axis, mask) for mask in range(1, SIDE))
        bit = SIDE
        while bit < lax.axis_size(axis):
            v = v + across(v, axis, bit)
            bit *= 2
        return v

    small = total_over(small, "rep")
    ab_x, ab_y = gather_replicas(ab_near)
    c_piece = reduce_times(c_parts)
    c_near = gather_times(c_piece)
    small = total_over(after(small, c_piece), "tm")
    edge = shifted(after(edge.astype(bf16), *c_parts), -1).astype(f32)
    edge = jnp.where(tm == tm_size - 1, jnp.zeros_like(edge), edge)
    input_grad = grad_in.at[tok_count - HALO :].add(edge)
    c_x, c_y = gather_replicas(c_near)
    ab_lo, ab_hi = gather_corner(ab_x, ab_y)
    c_lo, c_hi = gather_corner(c_x, c_y)
    rates = small[:, half_conv:].reshape(H, half_d)

    shapes = [(half_in, d), (DIN + CONV + H, half_d)]
    near = unload(
        scal, [ab_near, ab_x, ab_y], [c_near, c_x, c_y], 0, [], shapes, rates, "finish_near"
    )
    grad_out_w, grad_in_t = unload(
        scal, [ab_lo, ab_hi], [c_lo, c_hi], 3 * SIDE, near, shapes, None, "finish_far"
    )
    hs = half_heads
    return (
        output[None],
        input_grad[None],
        grad_in_t.T,
        grad_out_w,
        small[6, :half_d],
        small[:4, :half_conv],
        small[4, :half_conv],
        small[7, :hs],
        small[7, hs : 2 * hs],
        small[7, 2 * hs : 3 * hs],
        small[5, :half_in],
    )


def solution(mesh):
    return jax.shard_map(
        body,
        mesh=mesh,
        in_specs=(
            P(("rep", "fsdp"), "tm", None),
            P("fsdp", None),
            P("fsdp", None),
            P("fsdp"),
            P(None, "fsdp"),
            P("fsdp"),
            P("fsdp"),
            P("fsdp"),
            P("fsdp"),
            P("fsdp"),
            P(("rep", "fsdp")),
            P(("rep", "fsdp")),
            P(("rep", "fsdp"), "tm", None),
        ),
        out_specs=(
            P(("rep", "fsdp"), "tm", None),
            P(("rep", "fsdp"), "tm", None),
            P("fsdp", None),
            P("fsdp", None),
            P("fsdp"),
            P(None, "fsdp"),
            P("fsdp"),
            P("fsdp"),
            P("fsdp"),
            P("fsdp"),
            P("fsdp"),
        ),
        check_vma=False,
    )
```
